512 devices in a mesh: band: 16 (over y, x_lo, core), fft: 32 (over z, x_hi).
Axes of the slice: x: 4 (x_hi: 2, x_lo: 2; x = x_hi * 2 + x_lo), y: 4, z: 16, core: 2. Of those that a mesh axis runs over, the one named last changes fastest.
Arguments:
- wave_coeffs: bfloat16 [16, 2, 192, 192, 256], P('band', None, None, 'fft'), may hold values from -4 to 4
- occupation: float32 [16, 2], P('band'), may hold values from 0.05 to 0.2
- potential: bfloat16 [192, 192, 256], P('fft'), may hold values from -1.5 to 1.5
- projectors: bfloat16 [128, 8, 64, 128], P('fft'), may hold values from -0.0625 to 0.0625
- coupling: float32 [8, 8], replicated, may hold values from -4 to 4
- sphere_blocks: int32 [128, 64], replicated, may hold values from 0 to 73727, as said below
Outputs:
- applied: bfloat16 [16, 2, 192, 192, 256], P('band', None, None, 'fft')
- rho: bfloat16 [192, 192, 256], P('fft')
- projections: float32 [16, 128, 2, 8], P('band', 'fft')
The draws below stay inside these ranges and needn't reach their ends.
Inputs may be any that keep to these rules, and one draw needn't show every extreme that they name: `sphere_blocks`: row a holds 64 distinct block numbers. The first-dimension planes of all of them lie among the planes b * 6 - 6 to b * 6 + 11, counted around the periodic grid, with b = a // 4; every row has 16 blocks in the lowest of these planes and 16 in the highest.
All inputs are finite; a program needn't handle non-finite values.
Results may differ from the reference program's by a relative error of at most 0.025.
Values may be sent and summed in bfloat16 or wider, within the bound.
A program may use at most 64 MiB of HBM per device.

```python
import math
import jax
import jax.numpy as jnp
from jax import lax

NX = 192
NY = 192
NZ = 256
BLOCK = 128
NPROJ = 8
SB = 64
HALO = 6
ATOM_DEV = 4
SLAB = 6
ATOMS = 128
PAIRS = 16


def draw_sphere_blocks(key, part):
    zblocks = NZ // BLOCK
    plane_blocks = NY * zblocks
    ext_planes = SLAB + 2 * HALO
    inner_count = (ext_planes - 2) * plane_blocks
    edge_count = SB // 4

    def one_atom(atom_key, atom_number):
        key_low, key_high, key_rest, key_order = jax.random.split(atom_key, 4)
        lowest = jax.random.permutation(key_low, plane_blocks)[:edge_count]
        highest = (ext_planes - 1) * plane_blocks + jax.random.permutation(key_high, plane_blocks)[:edge_count]
        others = plane_blocks + jax.random.permutation(key_rest, inner_count)[:SB - 2 * edge_count]
        chosen = jnp.concatenate([lowest, highest, others]).astype(jnp.int32)
        chosen = chosen[jax.random.permutation(key_order, SB)]
        ext_plane = chosen // plane_blocks
        within = chosen % plane_blocks
        owner = atom_number // ATOM_DEV
        plane_index = (owner * SLAB - HALO + ext_plane + NX) % NX
        return (plane_index * plane_blocks + within).astype(jnp.int32)
    atom_keys = jax.random.split(key, ATOMS)
    return jax.vmap(one_atom)(atom_keys, jnp.arange(ATOMS, dtype=jnp.int32))


def block_levels(key, dims, shards, smallest, top_value):
    loudness = 1.0
    for position, shards_of in shards:
        steps = jax.random.uniform(jax.random.fold_in(jax.random.fold_in(key, 6), position), (shards_of,), jnp.float32, smallest / len(shards), top_value / len(shards))
        loudness = loudness * jnp.repeat(jnp.exp(steps), dims[position] // shards_of).reshape((-1,) + (1,) * (len(dims) - 1 - position))
    return loudness


def noise(own_key, extent, width, bound, cuts=(), kind=jnp.bfloat16):
    drawn = width * jax.random.normal(own_key, extent, jnp.float32)
    if cuts:
        drawn = drawn * block_levels(own_key, extent, cuts, -0.22, 0.18)
    return jnp.clip(drawn, -bound, bound).astype(kind)


def setup_inputs(seed: int = 0) -> dict:
    keys = jax.random.split(jax.random.key(seed), 7)
    return {
        "wave_coeffs": noise(keys[0], (PAIRS, 2, NX, NY, NZ), 1.0, 4.0, ((0, 16), (3, 32))),
        "occupation": jnp.clip(0.05 + 0.15 * jax.random.uniform(keys[1], (PAIRS, 2), jnp.float32) ** block_levels(keys[1], (PAIRS, 2), ((0, 16),), -0.2, 0.2), 0.05, 0.2),
        "potential": jnp.clip(jax.random.uniform(keys[2], (NX, NY, NZ), jnp.float32, -1.5, 1.5) * block_levels(keys[2], (NX, NY, NZ), ((0, 32),), -0.4, 0.0), -1.5, 1.5).astype(jnp.bfloat16),
        "projectors": noise(keys[3], (ATOMS, NPROJ, SB, BLOCK), (SB * BLOCK) ** -0.5, 0.0625, ((0, 32),)),
        "coupling": noise(keys[4], (NPROJ, NPROJ), 1.0, 4.0, (), jnp.float32),
        "sphere_blocks": draw_sphere_blocks(jax.random.fold_in(keys[6], 71), 0),
    }


def to_complex(pair_values):
    return pair_values[0].astype(jnp.float32) + 1j * pair_values[1].astype(jnp.float32)

def to_pair(values):
    return jnp.stack([jnp.real(values), jnp.imag(values)]).astype(jnp.bfloat16)

def wave_squares(length):
    indices = jnp.arange(length, dtype=jnp.int32)
    frequency = jnp.where(2 * indices < length, indices, indices - length).astype(jnp.float32) / length
    return frequency * frequency

def reference(wave_coeffs, occupation, potential, projectors, coupling, sphere_blocks):
    plane_blocks = NY * (NZ // BLOCK)
    strength = 3.0 * math.sqrt(BLOCK * SB) / NPROJ
    coupled = (coupling + coupling.T) * (0.5 * strength)
    kinetic = wave_squares(NX)[:, None, None] + wave_squares(NY)[None, :, None] + wave_squares(NZ)[None, None, :]
    beta_values = projectors.astype(jnp.float32)
    local_potential = potential.astype(jnp.float32)

    def one_pair(density, inputs):
        coeffs, weights = inputs
        section = to_pair(jnp.fft.ifft(to_complex(coeffs), axis=0, norm='ortho'))
        section = to_pair(jnp.fft.ifft(to_complex(section), axis=1, norm='ortho'))
        wave_field = to_pair(jnp.fft.ifft(to_complex(section), axis=2, norm='ortho'))
        real_part = wave_field[0].astype(jnp.float32)
        imag_part = wave_field[1].astype(jnp.float32)
        density = density + weights[0] * real_part * real_part + weights[1] * imag_part * imag_part
        blocks = wave_field.astype(jnp.float32).reshape(2, NX * plane_blocks, BLOCK)[:, sphere_blocks]
        projected = jnp.einsum('ajsk,bask->abj', beta_values, blocks, precision=lax.Precision.HIGHEST)
        energy = jnp.einsum('ij,abj->abi', coupled, projected, precision=lax.Precision.HIGHEST)
        spread = jnp.einsum('ajsk,abj->bask', beta_values, energy, precision=lax.Precision.HIGHEST)
        nonlocal_term = jnp.zeros((2, NX * plane_blocks, BLOCK), jnp.float32).at[:, sphere_blocks].add(spread)
        nonlocal_term = nonlocal_term.reshape(2, NX, NY, NZ)
        total_field = (local_potential[None] * wave_field.astype(jnp.float32) + nonlocal_term).astype(jnp.bfloat16)
        section = to_pair(jnp.fft.fft(to_complex(total_field), axis=2, norm='ortho'))
        section = to_pair(jnp.fft.fft(to_complex(section), axis=1, norm='ortho'))
        last = jnp.fft.fft(to_complex(section), axis=0, norm='ortho')
        transformed = jnp.stack([jnp.real(last), jnp.imag(last)]).astype(jnp.float32)
        applied = (transformed + kinetic[None] * coeffs.astype(jnp.float32)).astype(jnp.bfloat16)
        return (density, (applied, projected))
    start = jnp.zeros((NX, NY, NZ), jnp.float32)
    density, (applied, projections) = lax.scan(one_pair, start, (wave_coeffs, occupation))
    return (applied, density.astype(jnp.bfloat16), projections)
```

```python
import math

import jax
import jax.numpy as jnp
from jax import lax
from jax.sharding import PartitionSpec as P

HALO = 6


def extended_2(shard, sides, width):
    for axis, dim in sides:
        count, length = (lax.axis_size(axis), shard.shape[dim])
        up = [(i, (i + 1) % count) for i in range(count)]
        down = [(j, i) for i, j in up]
        last = lax.slice_in_dim(shard, length - width, length, axis=dim)
        first = lax.slice_in_dim(shard, 0, width, axis=dim)
        before = lax.ppermute(last, axis, up)
        after = lax.ppermute(first, axis, down)
        shard = jnp.concatenate([before, shard, after], axis=dim)
    return shard


def passed_along(block, axis, distance):
    devices = range(lax.axis_size(axis))
    route = [((i - distance) % len(devices), i) for i in devices]
    return lax.ppermute(block, axis, route)


def dft_table(length, sign_value):
    indices = jnp.arange(length, dtype=jnp.int32)
    phases = indices[:, None] * indices[None, :] % length
    angles = 2.0 * math.pi / length * phases.astype(jnp.float32)
    factor = 1.0 / math.sqrt(length)
    cosine = jnp.cos(angles) * factor
    sine_part = jnp.sin(angles) * (sign_value * factor)
    upper_rows = jnp.stack([cosine, -sine_part])
    bottom = jnp.stack([sine_part, cosine])
    return jnp.stack([upper_rows, bottom]).astype(jnp.bfloat16)


def wave_squares(indices, length):
    frequency = (
        jnp.where(2 * indices < length, indices, indices - length).astype(jnp.float32) / length
    )
    return frequency * frequency


def per_device(wave_coeffs, occupation, potential, projectors, coupling, sphere_blocks):
    pieces = lax.axis_size("fft")
    slab_index = lax.axis_index("fft")
    coeffs = wave_coeffs[0]
    size_x = coeffs.shape[1]
    columns = coeffs.shape[2]
    size_z = coeffs.shape[3]
    slab_planes = potential.shape[0]
    size_y = potential.shape[1]
    atom_dev = projectors.shape[0]
    nproj_count = projectors.shape[1]
    block_cells = projectors.shape[3]
    zblocks = size_z // block_cells
    plane_blocks = size_y * zblocks
    table_x = dft_table(size_x, 1.0).transpose(0, 2, 1, 3).reshape(2 * size_x, 2 * size_x)
    inverse_y = dft_table(size_y, 1.0)
    inverse_z = dft_table(size_z, 1.0)
    flattened = coeffs.reshape(2 * size_x, columns * size_z)
    along_x = jnp.dot(table_x, flattened, preferred_element_type=jnp.float32)
    along_x = along_x.reshape(2, size_x, columns, size_z).astype(jnp.bfloat16)
    along_y = jnp.einsum(
        "abyk,bxkz->axyz",
        inverse_y,
        lax.all_to_all(along_x, "fft", split_axis=1, concat_axis=2, tiled=True),
        preferred_element_type=jnp.float32,
    ).astype(jnp.bfloat16)
    wave_field = jnp.einsum(
        "abzk,bxyk->axyz", inverse_z, along_y, preferred_element_type=jnp.float32
    ).astype(jnp.bfloat16)
    weights = occupation[0]
    real_part = wave_field[0].astype(jnp.float32)
    imag_part = wave_field[1].astype(jnp.float32)
    partial_density = weights[0] * real_part * real_part + weights[1] * imag_part * imag_part
    density = lax.psum(partial_density.astype(jnp.bfloat16), "band")
    strength = 3.0 * math.sqrt(block_cells * projectors.shape[2]) / nproj_count
    coupled = (coupling + coupling.T) * (0.5 * strength)
    own_blocks = wave_field.reshape(2, slab_planes * plane_blocks, block_cells)
    slab_blocks = slab_planes * plane_blocks
    around = [(slab_index + shift) % pieces for shift in (-1, 0, 1)]
    atom_rows = jnp.stack(
        [lax.dynamic_slice_in_dim(sphere_blocks, d * atom_dev, atom_dev, 0) for d in around]
    )
    local_index = atom_rows - slab_index * slab_blocks
    is_mine = (atom_rows // slab_blocks) == slab_index
    safe_index = jnp.where(is_mine, local_index, 0)
    picked = jnp.where(is_mine[None, ..., None], own_blocks[:, safe_index], 0).astype(jnp.bfloat16)
    from_right = passed_along(picked[:, 0], "fft", -1)
    from_left = passed_along(picked[:, 2], "fft", 1)
    gathered = picked[:, 1] + from_right + from_left
    projections_own = jnp.einsum(
        "ajsk,bask->abj", projectors, gathered, preferred_element_type=jnp.float32
    )
    energy = jnp.einsum("ij,abj->abi", coupled, projections_own, precision=lax.Precision.HIGHEST)
    spread = jnp.einsum(
        "ajsk,abj->bask", projectors.astype(jnp.float32), energy, precision=lax.Precision.HIGHEST
    )
    spread_sent = spread.astype(jnp.bfloat16)
    spread_left = passed_along(spread_sent, "fft", 1).astype(jnp.float32)
    spread_right = passed_along(spread_sent, "fft", -1).astype(jnp.float32)
    spread_all = jnp.stack([spread_left, spread, spread_right], axis=1)
    drop_index = jnp.where(is_mine, local_index, slab_blocks)
    nonlocal_term = (
        jnp.zeros((2, slab_blocks, block_cells), jnp.float32)
        .at[:, drop_index]
        .add(spread_all, mode="drop")
    ).reshape(2, slab_planes, size_y, size_z)
    total_field = (
        potential.astype(jnp.float32)[None] * wave_field.astype(jnp.float32) + nonlocal_term
    ).astype(jnp.bfloat16)
    forward_z = dft_table(size_z, -1.0)
    forward_y = dft_table(size_y, -1.0)
    forward_x = dft_table(size_x, -1.0)
    back_z = jnp.einsum(
        "abzk,bxyk->axyz", forward_z, total_field, preferred_element_type=jnp.float32
    ).astype(jnp.bfloat16)
    back_y = jnp.einsum(
        "abyk,bxkz->axyz", forward_y, back_z, preferred_element_type=jnp.float32
    ).astype(jnp.bfloat16)
    transformed = jnp.einsum(
        "abxk,bkyz->axyz",
        forward_x,
        lax.all_to_all(back_y, "fft", split_axis=2, concat_axis=1, tiled=True),
        preferred_element_type=jnp.float32,
    )
    index_x = jnp.arange(size_x, dtype=jnp.int32)
    index_y = slab_index * columns + jnp.arange(columns, dtype=jnp.int32)
    index_z = jnp.arange(size_z, dtype=jnp.int32)
    kinetic = (
        wave_squares(index_x, size_x)[:, None, None]
        + wave_squares(index_y, size_y)[None, :, None]
        + wave_squares(index_z, size_z)[None, None, :]
    )
    applied = (transformed + kinetic[None] * coeffs.astype(jnp.float32)).astype(jnp.bfloat16)
    return (applied[None], density, projections_own[None])


def solution(mesh):
    placed = (
        P("band", None, None, "fft", None),
        P("band", None),
        P("fft", None, None),
        P("fft", None, None, None),
        P(),
        P(),
    )
    return jax.shard_map(
        per_device,
        mesh=mesh,
        in_specs=placed,
        out_specs=(
            P("band", None, None, "fft", None),
            P("fft", None, None),
            P("band", "fft", None, None),
        ),
        check_vma=False,
    )
```

```python
import math

import jax
import jax.numpy as jnp
from jax import lax
from jax.sharding import PartitionSpec as P

HALO = 6


def extended_2(shard, sides, width):
    for axis, dim in sides:
        count, length = (lax.axis_size(axis), shard.shape[dim])
        up = [(i, (i + 1) % count) for i in range(count)]
        down = [(j, i) for i, j in up]
        last = lax.slice_in_dim(shard, length - width, length, axis=dim)
        first = lax.slice_in_dim(shard, 0, width, axis=dim)
        before = lax.ppermute(last, axis, up)
        after = lax.ppermute(first, axis, down)
        shard = jnp.concatenate([before, shard, after], axis=dim)
    return shard


def passed_along(block, axis, distance):
    devices = range(lax.axis_size(axis))
    route = [((i - distance) % len(devices), i) for i in devices]
    return lax.ppermute(block, axis, route)


def dft_table(length, sign_value):
    indices = jnp.arange(length, dtype=jnp.int32)
    phases = indices[:, None] * indices[None, :] % length
    angles = 2.0 * math.pi / length * phases.astype(jnp.float32)
    factor = 1.0 / math.sqrt(length)
    cosine = jnp.cos(angles) * factor
    sine_part = jnp.sin(angles) * (sign_value * factor)
    upper_rows = jnp.stack([cosine, -sine_part])
    bottom = jnp.stack([sine_part, cosine])
    return jnp.stack([upper_rows, bottom]).astype(jnp.bfloat16)


def wave_squares(indices, length):
    frequency = (
        jnp.where(2 * indices < length, indices, indices - length).astype(jnp.float32) / length
    )
    return frequency * frequency


def per_device(wave_coeffs, occupation, potential, projectors, coupling, sphere_blocks):
    pieces = lax.axis_size("fft")
    slab_index = lax.axis_index("fft")
    coeffs = wave_coeffs[0]
    size_x = coeffs.shape[1]
    columns = coeffs.shape[2]
    size_z = coeffs.shape[3]
    slab_planes = potential.shape[0]
    size_y = potential.shape[1]
    atom_dev = projectors.shape[0]
    nproj_count = projectors.shape[1]
    block_cells = projectors.shape[3]
    zblocks = size_z // block_cells
    plane_blocks = size_y * zblocks
    table_x = dft_table(size_x, 1.0).transpose(0, 2, 1, 3).reshape(2 * size_x, 2 * size_x)
    inverse_y = dft_table(size_y, 1.0)
    inverse_z = dft_table(size_z, 1.0)
    flattened = coeffs.reshape(2 * size_x, columns * size_z)
    along_x = jnp.dot(table_x, flattened, preferred_element_type=jnp.float32)
    along_x = along_x.reshape(2, size_x, columns, size_z).astype(jnp.bfloat16)
    along_y = jnp.einsum(
        "abyk,bxkz->axyz",
        inverse_y,
        lax.all_to_all(along_x, "fft", split_axis=1, concat_axis=2, tiled=True),
        preferred_element_type=jnp.float32,
    ).astype(jnp.bfloat16)
    wave_field = jnp.einsum(
        "abzk,bxyk->axyz", inverse_z, along_y, preferred_element_type=jnp.float32
    ).astype(jnp.bfloat16)
    weights = occupation[0]
    real_part = wave_field[0].astype(jnp.float32)
    imag_part = wave_field[1].astype(jnp.float32)
    partial_density = weights[0] * real_part * real_part + weights[1] * imag_part * imag_part
    density = lax.psum(partial_density.astype(jnp.bfloat16), "band")
    strength = 3.0 * math.sqrt(block_cells * projectors.shape[2]) / nproj_count
    coupled = (coupling + coupling.T) * (0.5 * strength)
    slab_blocks = slab_planes * plane_blocks
    slab_rows = slab_planes * size_y
    around = [(slab_index + shift) % pieces for shift in (-1, 0, 1)]
    atom_rows = jnp.stack(
        [lax.dynamic_slice_in_dim(sphere_blocks, d * atom_dev, atom_dev, 0) for d in around]
    ).reshape(-1)
    local_index = atom_rows - slab_index * slab_blocks
    is_mine = (atom_rows // slab_blocks) == slab_index
    row_of = local_index // zblocks
    half_of = (local_index % zblocks)[None, :, None]
    selector = (
        (row_of[:, None] == jnp.arange(slab_rows, dtype=jnp.int32)[None, :]) & is_mine[:, None]
    ).astype(jnp.bfloat16)
    field_rows = wave_field.reshape(2, slab_rows, size_z)
    picked_rows = jnp.einsum(
        "er,crz->cez", selector, field_rows, preferred_element_type=jnp.float32
    ).reshape(2, -1, zblocks, block_cells)
    picked = jnp.zeros_like(picked_rows[:, :, 0])
    for q in range(zblocks):
        picked = jnp.where(half_of == q, picked_rows[:, :, q], picked)
    picked = picked.astype(jnp.bfloat16).reshape(2, 3, atom_dev, -1, block_cells)
    from_right = passed_along(picked[:, 0], "fft", -1)
    from_left = passed_along(picked[:, 2], "fft", 1)
    gathered = picked[:, 1] + from_right + from_left
    projections_own = jnp.einsum(
        "ajsk,bask->abj", projectors, gathered, preferred_element_type=jnp.float32
    )
    energy = jnp.einsum("ij,abj->abi", coupled, projections_own, precision=lax.Precision.HIGHEST)
    spread = jnp.einsum(
        "ajsk,abj->bask", projectors.astype(jnp.float32), energy, precision=lax.Precision.HIGHEST
    )
    spread_sent = spread.astype(jnp.bfloat16)
    spread_left = passed_along(spread_sent, "fft", 1).astype(jnp.float32)
    spread_right = passed_along(spread_sent, "fft", -1).astype(jnp.float32)
    spread_all = jnp.stack([spread_left, spread, spread_right], axis=1).reshape(
        2, -1, 1, block_cells
    )
    placed_halves = jnp.concatenate(
        [jnp.where(half_of[..., None] == q, spread_all, 0.0) for q in range(zblocks)], axis=2
    ).reshape(2, -1, size_z)
    upper = placed_halves.astype(jnp.bfloat16)
    lower = (placed_halves - upper.astype(jnp.float32)).astype(jnp.bfloat16)
    nonlocal_parts = jnp.einsum(
        "er,cez->crz",
        selector,
        jnp.concatenate([upper, lower]),
        preferred_element_type=jnp.float32,
    )
    nonlocal_term = (nonlocal_parts[:2] + nonlocal_parts[2:]).reshape(
        2, slab_planes, size_y, size_z
    )
    total_field = (
        potential.astype(jnp.float32)[None] * wave_field.astype(jnp.float32) + nonlocal_term
    ).astype(jnp.bfloat16)
    forward_z = dft_table(size_z, -1.0)
    forward_y = dft_table(size_y, -1.0)
    forward_x = dft_table(size_x, -1.0)
    back_z = jnp.einsum(
        "abzk,bxyk->axyz", forward_z, total_field, preferred_element_type=jnp.float32
    ).astype(jnp.bfloat16)
    back_y = jnp.einsum(
        "abyk,bxkz->axyz", forward_y, back_z, preferred_element_type=jnp.float32
    ).astype(jnp.bfloat16)
    transformed = jnp.einsum(
        "abxk,bkyz->axyz",
        forward_x,
        lax.all_to_all(back_y, "fft", split_axis=2, concat_axis=1, tiled=True),
        preferred_element_type=jnp.float32,
    )
    index_x = jnp.arange(size_x, dtype=jnp.int32)
    index_y = slab_index * columns + jnp.arange(columns, dtype=jnp.int32)
    index_z = jnp.arange(size_z, dtype=jnp.int32)
    kinetic = (
        wave_squares(index_x, size_x)[:, None, None]
        + wave_squares(index_y, size_y)[None, :, None]
        + wave_squares(index_z, size_z)[None, None, :]
    )
    applied = (transformed + kinetic[None] * coeffs.astype(jnp.float32)).astype(jnp.bfloat16)
    return (applied[None], density, projections_own[None])


def solution(mesh):
    placed = (
        P("band", None, None, "fft", None),
        P("band", None),
        P("fft", None, None),
        P("fft", None, None, None),
        P(),
        P(),
    )
    return jax.shard_map(
        per_device,
        mesh=mesh,
        in_specs=placed,
        out_specs=(
            P("band", None, None, "fft", None),
            P("fft", None, None),
            P("band", "fft", None, None),
        ),
        check_vma=False,
    )
```

```python
import math

import jax
import jax.numpy as jnp
from jax import lax
from jax.experimental import pallas as pl
from jax.experimental.pallas import tpu as pltpu
from jax.sharding import PartitionSpec as P

HALO = 6


MESH = pl.DeviceIdType.MESH


def band_sum_kernel(part_ref, out_ref, received, reduced, sems):
    count = part_ref.shape[0]
    me = lax.axis_index("band")
    column = lax.axis_index("fft")
    barrier = pltpu.get_barrier_semaphore()
    for k in range(1, count):
        pl.semaphore_signal(
            barrier, inc=1, device_id=((me + k) % count, column), device_id_type=MESH
        )
    pl.semaphore_wait(barrier, count - 1)
    scatter = []
    for k in range(1, count):
        target = (me + k) % count
        scatter.append(
            pltpu.make_async_remote_copy(
                src_ref=part_ref.at[target],
                dst_ref=received.at[me],
                send_sem=sems.at[0, k],
                recv_sem=sems.at[1, k],
                device_id=(target, column),
                device_id_type=MESH,
            )
        )
    for copy in scatter:
        copy.start()
    for copy in scatter:
        copy.wait()
    total = part_ref[me].astype(jnp.float32)
    for k in range(1, count):
        total = total + received[(me + count - k) % count].astype(jnp.float32)
    reduced[me] = total.astype(reduced.dtype)
    spread_out = []
    for k in range(1, count):
        target = (me + k) % count
        spread_out.append(
            pltpu.make_async_remote_copy(
                src_ref=reduced.at[me],
                dst_ref=reduced.at[me],
                send_sem=sems.at[2, k],
                recv_sem=sems.at[3, k],
                device_id=(target, column),
                device_id_type=MESH,
            )
        )
    for copy in spread_out:
        copy.start()
    for copy in spread_out:
        copy.wait()
    out_ref[...] = reduced[...]


def band_sum(values):
    count = lax.axis_size("band")
    shape = values.shape
    rows = values.size // (count * 128)
    chunks = values.reshape(count, rows, 128)
    summed = pl.pallas_call(
        band_sum_kernel,
        out_shape=jax.ShapeDtypeStruct(chunks.shape, chunks.dtype),
        in_specs=[pl.BlockSpec(memory_space=pltpu.VMEM)],
        out_specs=pl.BlockSpec(memory_space=pltpu.VMEM),
        scratch_shapes=[
            pltpu.VMEM(chunks.shape, chunks.dtype),
            pltpu.VMEM(chunks.shape, chunks.dtype),
            pltpu.SemaphoreType.DMA((4, count)),
        ],
        compiler_params=pltpu.CompilerParams(collective_id=0, has_side_effects=True),
        cost_estimate=pl.CostEstimate(
            flops=values.size, bytes_accessed=6 * values.size, transcendentals=0
        ),
    )(chunks)
    return summed.reshape(shape)


def extended_2(shard, sides, width):
    for axis, dim in sides:
        count, length = (lax.axis_size(axis), shard.shape[dim])
        up = [(i, (i + 1) % count) for i in range(count)]
        down = [(j, i) for i, j in up]
        last = lax.slice_in_dim(shard, length - width, length, axis=dim)
        first = lax.slice_in_dim(shard, 0, width, axis=dim)
        before = lax.ppermute(last, axis, up)
        after = lax.ppermute(first, axis, down)
        shard = jnp.concatenate([before, shard, after], axis=dim)
    return shard


def passed_along(block, axis, distance):
    devices = range(lax.axis_size(axis))
    route = [((i - distance) % len(devices), i) for i in devices]
    return lax.ppermute(block, axis, route)


def dft_table(length, sign_value):
    indices = jnp.arange(length, dtype=jnp.int32)
    phases = indices[:, None] * indices[None, :] % length
    angles = 2.0 * math.pi / length * phases.astype(jnp.float32)
    factor = 1.0 / math.sqrt(length)
    cosine = jnp.cos(angles) * factor
    sine_part = jnp.sin(angles) * (sign_value * factor)
    upper_rows = jnp.stack([cosine, -sine_part])
    bottom = jnp.stack([sine_part, cosine])
    return jnp.stack([upper_rows, bottom]).astype(jnp.bfloat16)


def wave_squares(indices, length):
    frequency = (
        jnp.where(2 * indices < length, indices, indices - length).astype(jnp.float32) / length
    )
    return frequency * frequency


def per_device(wave_coeffs, occupation, potential, projectors, coupling, sphere_blocks):
    pieces = lax.axis_size("fft")
    slab_index = lax.axis_index("fft")
    coeffs = wave_coeffs[0]
    size_x = coeffs.shape[1]
    columns = coeffs.shape[2]
    size_z = coeffs.shape[3]
    slab_planes = potential.shape[0]
    size_y = potential.shape[1]
    atom_dev = projectors.shape[0]
    nproj_count = projectors.shape[1]
    block_cells = projectors.shape[3]
    zblocks = size_z // block_cells
    plane_blocks = size_y * zblocks
    table_x = dft_table(size_x, 1.0).transpose(0, 2, 1, 3).reshape(2 * size_x, 2 * size_x)
    inverse_y = dft_table(size_y, 1.0)
    inverse_z = dft_table(size_z, 1.0)
    flattened = coeffs.reshape(2 * size_x, columns * size_z)
    along_x = jnp.dot(table_x, flattened, preferred_element_type=jnp.float32)
    along_x = along_x.reshape(2, size_x, columns, size_z).astype(jnp.bfloat16)
    along_y = jnp.einsum(
        "abyk,bxkz->axyz",
        inverse_y,
        lax.all_to_all(along_x, "fft", split_axis=1, concat_axis=2, tiled=True),
        preferred_element_type=jnp.float32,
    ).astype(jnp.bfloat16)
    wave_field = jnp.einsum(
        "abzk,bxyk->axyz", inverse_z, along_y, preferred_element_type=jnp.float32
    ).astype(jnp.bfloat16)
    weights = occupation[0]
    real_part = wave_field[0].astype(jnp.float32)
    imag_part = wave_field[1].astype(jnp.float32)
    partial_density = weights[0] * real_part * real_part + weights[1] * imag_part * imag_part
    density = band_sum(partial_density.astype(jnp.bfloat16))
    strength = 3.0 * math.sqrt(block_cells * projectors.shape[2]) / nproj_count
    coupled = (coupling + coupling.T) * (0.5 * strength)
    slab_blocks = slab_planes * plane_blocks
    slab_rows = slab_planes * size_y
    around = [(slab_index + shift) % pieces for shift in (-1, 0, 1)]
    atom_rows = jnp.stack(
        [lax.dynamic_slice_in_dim(sphere_blocks, d * atom_dev, atom_dev, 0) for d in around]
    ).reshape(-1)
    local_index = atom_rows - slab_index * slab_blocks
    is_mine = (atom_rows // slab_blocks) == slab_index
    row_of = local_index // zblocks
    half_of = (local_index % zblocks)[None, :, None]
    selector = (
        (row_of[:, None] == jnp.arange(slab_rows, dtype=jnp.int32)[None, :]) & is_mine[:, None]
    ).astype(jnp.bfloat16)
    field_rows = wave_field.reshape(2, slab_rows, size_z)
    picked_rows = jnp.einsum(
        "er,crz->cez", selector, field_rows, preferred_element_type=jnp.float32
    ).reshape(2, -1, zblocks, block_cells)
    picked = jnp.zeros_like(picked_rows[:, :, 0])
    for q in range(zblocks):
        picked = jnp.where(half_of == q, picked_rows[:, :, q], picked)
    picked = picked.astype(jnp.bfloat16).reshape(2, 3, atom_dev, -1, block_cells)
    from_right = passed_along(picked[:, 0], "fft", -1)
    from_left = passed_along(picked[:, 2], "fft", 1)
    gathered = picked[:, 1] + from_right + from_left
    projections_own = jnp.einsum(
        "ajsk,bask->abj", projectors, gathered, preferred_element_type=jnp.float32
    )
    energy = jnp.einsum("ij,abj->abi", coupled, projections_own, precision=lax.Precision.HIGHEST)
    spread = jnp.einsum(
        "ajsk,abj->bask", projectors.astype(jnp.float32), energy, precision=lax.Precision.HIGHEST
    )
    spread_sent = spread.astype(jnp.bfloat16)
    spread_left = passed_along(spread_sent, "fft", 1).astype(jnp.float32)
    spread_right = passed_along(spread_sent, "fft", -1).astype(jnp.float32)
    spread_all = jnp.stack([spread_left, spread, spread_right], axis=1).reshape(
        2, -1, 1, block_cells
    )
    placed_halves = jnp.concatenate(
        [jnp.where(half_of[..., None] == q, spread_all, 0.0) for q in range(zblocks)], axis=2
    ).reshape(2, -1, size_z)
    upper = placed_halves.astype(jnp.bfloat16)
    lower = (placed_halves - upper.astype(jnp.float32)).astype(jnp.bfloat16)
    nonlocal_parts = jnp.einsum(
        "er,cez->crz",
        selector,
        jnp.concatenate([upper, lower]),
        preferred_element_type=jnp.float32,
    )
    nonlocal_term = (nonlocal_parts[:2] + nonlocal_parts[2:]).reshape(
        2, slab_planes, size_y, size_z
    )
    total_field = (
        potential.astype(jnp.float32)[None] * wave_field.astype(jnp.float32) + nonlocal_term
    ).astype(jnp.bfloat16)
    forward_z = dft_table(size_z, -1.0)
    forward_y = dft_table(size_y, -1.0)
    forward_x = dft_table(size_x, -1.0)
    back_z = jnp.einsum(
        "abzk,bxyk->axyz", forward_z, total_field, preferred_element_type=jnp.float32
    ).astype(jnp.bfloat16)
    back_y = jnp.einsum(
        "abyk,bxkz->axyz", forward_y, back_z, preferred_element_type=jnp.float32
    ).astype(jnp.bfloat16)
    transformed = jnp.einsum(
        "abxk,bkyz->axyz",
        forward_x,
        lax.all_to_all(back_y, "fft", split_axis=2, concat_axis=1, tiled=True),
        preferred_element_type=jnp.float32,
    )
    index_x = jnp.arange(size_x, dtype=jnp.int32)
    index_y = slab_index * columns + jnp.arange(columns, dtype=jnp.int32)
    index_z = jnp.arange(size_z, dtype=jnp.int32)
    kinetic = (
        wave_squares(index_x, size_x)[:, None, None]
        + wave_squares(index_y, size_y)[None, :, None]
        + wave_squares(index_z, size_z)[None, None, :]
    )
    applied = (transformed + kinetic[None] * coeffs.astype(jnp.float32)).astype(jnp.bfloat16)
    return (applied[None], density, projections_own[None])


def solution(mesh):
    placed = (
        P("band", None, None, "fft", None),
        P("band", None),
        P("fft", None, None),
        P("fft", None, None, None),
        P(),
        P(),
    )
    return jax.shard_map(
        per_device,
        mesh=mesh,
        in_specs=placed,
        out_specs=(
            P("band", None, None, "fft", None),
            P("fft", None, None),
            P("band", "fft", None, None),
        ),
        check_vma=False,
    )
```

```python
import functools
import math

import jax
import jax.numpy as jnp
from jax import lax
from jax.experimental import pallas as pl
from jax.experimental.pallas import tpu as pltpu
from jax.sharding import PartitionSpec as P

HALO = 6


MESH = pl.DeviceIdType.MESH


def band_sum_kernel(part_ref, out_ref, received, reduced, sems):
    count = part_ref.shape[0]
    me = lax.axis_index("band")
    column = lax.axis_index("fft")
    barrier = pltpu.get_barrier_semaphore()
    for k in range(1, count):
        pl.semaphore_signal(
            barrier, inc=1, device_id=((me + k) % count, column), device_id_type=MESH
        )
    pl.semaphore_wait(barrier, count - 1)
    scatter = []
    for k in range(1, count):
        target = (me + k) % count
        scatter.append(
            pltpu.make_async_remote_copy(
                src_ref=part_ref.at[target],
                dst_ref=received.at[me],
                send_sem=sems.at[0, k],
                recv_sem=sems.at[1, k],
                device_id=(target, column),
                device_id_type=MESH,
            )
        )
    for copy in scatter:
        copy.start()
    for copy in scatter:
        copy.wait()
    total = part_ref[me].astype(jnp.float32)
    for k in range(1, count):
        total = total + received[(me + count - k) % count].astype(jnp.float32)
    reduced[me] = total.astype(reduced.dtype)
    spread_out = []
    for k in range(1, count):
        target = (me + k) % count
        spread_out.append(
            pltpu.make_async_remote_copy(
                src_ref=reduced.at[me],
                dst_ref=reduced.at[me],
                send_sem=sems.at[2, k],
                recv_sem=sems.at[3, k],
                device_id=(target, column),
                device_id_type=MESH,
            )
        )
    for copy in spread_out:
        copy.start()
    for copy in spread_out:
        copy.wait()
    out_ref[...] = reduced[...]


def band_sum(values):
    count = lax.axis_size("band")
    shape = values.shape
    rows = values.size // (count * 128)
    chunks = values.reshape(count, rows, 128)
    summed = pl.pallas_call(
        band_sum_kernel,
        out_shape=jax.ShapeDtypeStruct(chunks.shape, chunks.dtype),
        in_specs=[pl.BlockSpec(memory_space=pltpu.VMEM)],
        out_specs=pl.BlockSpec(memory_space=pltpu.VMEM),
        scratch_shapes=[
            pltpu.VMEM(chunks.shape, chunks.dtype),
            pltpu.VMEM(chunks.shape, chunks.dtype),
            pltpu.SemaphoreType.DMA((4, count)),
        ],
        compiler_params=pltpu.CompilerParams(collective_id=0, has_side_effects=True),
        cost_estimate=pl.CostEstimate(
            flops=values.size, bytes_accessed=6 * values.size, transcendentals=0
        ),
    )(chunks)
    return summed.reshape(shape)


def exchange_kernel(axis, chunks_ref, out_ref, received, sems):
    count = chunks_ref.shape[0]
    me = lax.axis_index(axis)
    if axis == "fft":
        place = lambda t: (lax.axis_index("band"), t)
    else:
        place = lambda t: (t, lax.axis_index("fft"))
    barrier = pltpu.get_barrier_semaphore()
    for k in range(1, count):
        pl.semaphore_signal(
            barrier, inc=1, device_id=place((me + k) % count), device_id_type=MESH
        )
    pl.semaphore_wait(barrier, count - 1)
    copies = []
    for k in range(1, count):
        target = (me + k) % count
        copies.append(
            pltpu.make_async_remote_copy(
                src_ref=chunks_ref.at[target],
                dst_ref=received.at[me],
                send_sem=sems.at[0, k],
                recv_sem=sems.at[1, k],
                device_id=place(target),
                device_id_type=MESH,
            )
        )
    for copy in copies:
        copy.start()
    received[me] = chunks_ref[me]
    for copy in copies:
        copy.wait()
    out_ref[...] = received[...]


def exchange(chunks, axis, tag):
    return pl.pallas_call(
        functools.partial(exchange_kernel, axis),
        out_shape=jax.ShapeDtypeStruct(chunks.shape, chunks.dtype),
        in_specs=[pl.BlockSpec(memory_space=pltpu.VMEM)],
        out_specs=pl.BlockSpec(memory_space=pltpu.VMEM),
        scratch_shapes=[
            pltpu.VMEM(chunks.shape, chunks.dtype),
            pltpu.SemaphoreType.DMA((2, chunks.shape[0])),
        ],
        compiler_params=pltpu.CompilerParams(collective_id=tag, has_side_effects=True),
        cost_estimate=pl.CostEstimate(
            flops=0, bytes_accessed=4 * chunks.size, transcendentals=0
        ),
    )(chunks)


def extended_2(shard, sides, width):
    for axis, dim in sides:
        count, length = (lax.axis_size(axis), shard.shape[dim])
        up = [(i, (i + 1) % count) for i in range(count)]
        down = [(j, i) for i, j in up]
        last = lax.slice_in_dim(shard, length - width, length, axis=dim)
        first = lax.slice_in_dim(shard, 0, width, axis=dim)
        before = lax.ppermute(last, axis, up)
        after = lax.ppermute(first, axis, down)
        shard = jnp.concatenate([before, shard, after], axis=dim)
    return shard


def passed_along(block, axis, distance):
    devices = range(lax.axis_size(axis))
    route = [((i - distance) % len(devices), i) for i in devices]
    return lax.ppermute(block, axis, route)


def dft_table(length, sign_value):
    indices = jnp.arange(length, dtype=jnp.int32)
    phases = indices[:, None] * indices[None, :] % length
    angles = 2.0 * math.pi / length * phases.astype(jnp.float32)
    factor = 1.0 / math.sqrt(length)
    cosine = jnp.cos(angles) * factor
    sine_part = jnp.sin(angles) * (sign_value * factor)
    upper_rows = jnp.stack([cosine, -sine_part])
    bottom = jnp.stack([sine_part, cosine])
    return jnp.stack([upper_rows, bottom]).astype(jnp.bfloat16)


def wave_squares(indices, length):
    frequency = (
        jnp.where(2 * indices < length, indices, indices - length).astype(jnp.float32) / length
    )
    return frequency * frequency


def per_device(wave_coeffs, occupation, potential, projectors, coupling, sphere_blocks):
    pieces = lax.axis_size("fft")
    slab_index = lax.axis_index("fft")
    coeffs = wave_coeffs[0]
    size_x = coeffs.shape[1]
    columns = coeffs.shape[2]
    size_z = coeffs.shape[3]
    slab_planes = potential.shape[0]
    size_y = potential.shape[1]
    atom_dev = projectors.shape[0]
    nproj_count = projectors.shape[1]
    block_cells = projectors.shape[3]
    zblocks = size_z // block_cells
    plane_blocks = size_y * zblocks
    table_x = dft_table(size_x, 1.0).transpose(0, 2, 1, 3).reshape(2 * size_x, 2 * size_x)
    inverse_y = dft_table(size_y, 1.0)
    inverse_z = dft_table(size_z, 1.0)
    flattened = coeffs.reshape(2 * size_x, columns * size_z)
    along_x = jnp.dot(table_x, flattened, preferred_element_type=jnp.float32)
    along_x = along_x.reshape(2, size_x, columns, size_z).astype(jnp.bfloat16)
    outgoing = along_x.reshape(2, pieces, slab_planes, columns, size_z).transpose(1, 0, 2, 3, 4)
    arrived = exchange(outgoing.reshape(pieces, -1, 128), "fft", 1)
    arrived = (
        arrived.reshape(pieces, 2, slab_planes, columns, size_z)
        .transpose(1, 2, 0, 3, 4)
        .reshape(2, slab_planes, pieces * columns, size_z)
    )
    along_y = jnp.einsum(
        "abyk,bxkz->axyz",
        inverse_y,
        arrived,
        preferred_element_type=jnp.float32,
    ).astype(jnp.bfloat16)
    wave_field = jnp.einsum(
        "abzk,bxyk->axyz", inverse_z, along_y, preferred_element_type=jnp.float32
    ).astype(jnp.bfloat16)
    weights = occupation[0]
    real_part = wave_field[0].astype(jnp.float32)
    imag_part = wave_field[1].astype(jnp.float32)
    partial_density = weights[0] * real_part * real_part + weights[1] * imag_part * imag_part
    density = band_sum(partial_density.astype(jnp.bfloat16))
    strength = 3.0 * math.sqrt(block_cells * projectors.shape[2]) / nproj_count
    coupled = (coupling + coupling.T) * (0.5 * strength)
    slab_blocks = slab_planes * plane_blocks
    slab_rows = slab_planes * size_y
    around = [(slab_index + shift) % pieces for shift in (-1, 0, 1)]
    atom_rows = jnp.stack(
        [lax.dynamic_slice_in_dim(sphere_blocks, d * atom_dev, atom_dev, 0) for d in around]
    ).reshape(-1)
    local_index = atom_rows - slab_index * slab_blocks
    is_mine = (atom_rows // slab_blocks) == slab_index
    row_of = local_index // zblocks
    half_of = (local_index % zblocks)[None, :, None]
    selector = (
        (row_of[:, None] == jnp.arange(slab_rows, dtype=jnp.int32)[None, :]) & is_mine[:, None]
    ).astype(jnp.bfloat16)
    field_rows = wave_field.reshape(2, slab_rows, size_z)
    picked_rows = jnp.einsum(
        "er,crz->cez", selector, field_rows, preferred_element_type=jnp.float32
    ).reshape(2, -1, zblocks, block_cells)
    picked = jnp.zeros_like(picked_rows[:, :, 0])
    for q in range(zblocks):
        picked = jnp.where(half_of == q, picked_rows[:, :, q], picked)
    picked = picked.astype(jnp.bfloat16).reshape(2, 3, atom_dev, -1, block_cells)
    from_right = passed_along(picked[:, 0], "fft", -1)
    from_left = passed_along(picked[:, 2], "fft", 1)
    gathered = picked[:, 1] + from_right + from_left
    projections_own = jnp.einsum(
        "ajsk,bask->abj", projectors, gathered, preferred_element_type=jnp.float32
    )
    energy = jnp.einsum("ij,abj->abi", coupled, projections_own, precision=lax.Precision.HIGHEST)
    spread = jnp.einsum(
        "ajsk,abj->bask", projectors.astype(jnp.float32), energy, precision=lax.Precision.HIGHEST
    )
    spread_sent = spread.astype(jnp.bfloat16)
    spread_left = passed_along(spread_sent, "fft", 1).astype(jnp.float32)
    spread_right = passed_along(spread_sent, "fft", -1).astype(jnp.float32)
    spread_all = jnp.stack([spread_left, spread, spread_right], axis=1).reshape(
        2, -1, 1, block_cells
    )
    placed_halves = jnp.concatenate(
        [jnp.where(half_of[..., None] == q, spread_all, 0.0) for q in range(zblocks)], axis=2
    ).reshape(2, -1, size_z)
    upper = placed_halves.astype(jnp.bfloat16)
    lower = (placed_halves - upper.astype(jnp.float32)).astype(jnp.bfloat16)
    nonlocal_parts = jnp.einsum(
        "er,cez->crz",
        selector,
        jnp.concatenate([upper, lower]),
        preferred_element_type=jnp.float32,
    )
    nonlocal_term = (nonlocal_parts[:2] + nonlocal_parts[2:]).reshape(
        2, slab_planes, size_y, size_z
    )
    total_field = (
        potential.astype(jnp.float32)[None] * wave_field.astype(jnp.float32) + nonlocal_term
    ).astype(jnp.bfloat16)
    forward_z = dft_table(size_z, -1.0)
    forward_y = dft_table(size_y, -1.0)
    forward_x = dft_table(size_x, -1.0)
    back_z = jnp.einsum(
        "abzk,bxyk->axyz", forward_z, total_field, preferred_element_type=jnp.float32
    ).astype(jnp.bfloat16)
    back_y = jnp.einsum(
        "abyk,bxkz->axyz", forward_y, back_z, preferred_element_type=jnp.float32
    ).astype(jnp.bfloat16)
    transformed = jnp.einsum(
        "abxk,bkyz->axyz",
        forward_x,
        lax.all_to_all(back_y, "fft", split_axis=2, concat_axis=1, tiled=True),
        preferred_element_type=jnp.float32,
    )
    index_x = jnp.arange(size_x, dtype=jnp.int32)
    index_y = slab_index * columns + jnp.arange(columns, dtype=jnp.int32)
    index_z = jnp.arange(size_z, dtype=jnp.int32)
    kinetic = (
        wave_squares(index_x, size_x)[:, None, None]
        + wave_squares(index_y, size_y)[None, :, None]
        + wave_squares(index_z, size_z)[None, None, :]
    )
    applied = (transformed + kinetic[None] * coeffs.astype(jnp.float32)).astype(jnp.bfloat16)
    return (applied[None], density, projections_own[None])


def solution(mesh):
    placed = (
        P("band", None, None, "fft", None),
        P("band", None),
        P("fft", None, None),
        P("fft", None, None, None),
        P(),
        P(),
    )
    return jax.shard_map(
        per_device,
        mesh=mesh,
        in_specs=placed,
        out_specs=(
            P("band", None, None, "fft", None),
            P("fft", None, None),
            P("band", "fft", None, None),
        ),
        check_vma=False,
    )
```

```python
import math

import jax
import jax.numpy as jnp
from jax import lax
from jax.experimental import pallas as pl
from jax.experimental.pallas import tpu as pltpu
from jax.sharding import PartitionSpec as P

HALO = 6


MESH = pl.DeviceIdType.MESH


def band_sum_kernel(part_ref, out_ref, received, reduced, sems):
    count = part_ref.shape[0]
    me = lax.axis_index("band")
    column = lax.axis_index("fft")
    barrier = pltpu.get_barrier_semaphore()
    for k in range(1, count):
        pl.semaphore_signal(
            barrier, inc=1, device_id=((me + k) % count, column), device_id_type=MESH
        )
    pl.semaphore_wait(barrier, count - 1)
    scatter = []
    for k in range(1, count):
        target = (me + k) % count
        scatter.append(
            pltpu.make_async_remote_copy(
                src_ref=part_ref.at[target],
                dst_ref=received.at[me],
                send_sem=sems.at[0, k],
                recv_sem=sems.at[1, k],
                device_id=(target, column),
                device_id_type=MESH,
            )
        )
    for copy in scatter:
        copy.start()
    for copy in scatter:
        copy.wait()
    total = part_ref[me].astype(jnp.float32)
    for k in range(1, count):
        total = total + received[(me + count - k) % count].astype(jnp.float32)
    reduced[me] = total.astype(reduced.dtype)
    spread_out = []
    for k in range(1, count):
        target = (me + k) % count
        spread_out.append(
            pltpu.make_async_remote_copy(
                src_ref=reduced.at[me],
                dst_ref=reduced.at[me],
                send_sem=sems.at[2, k],
                recv_sem=sems.at[3, k],
                device_id=(target, column),
                device_id_type=MESH,
            )
        )
    for copy in spread_out:
        copy.start()
    for copy in spread_out:
        copy.wait()
    out_ref[...] = reduced[...]


def band_sum(values):
    count = lax.axis_size("band")
    shape = values.shape
    rows = values.size // (count * 128)
    chunks = values.reshape(count, rows, 128)
    summed = pl.pallas_call(
        band_sum_kernel,
        out_shape=jax.ShapeDtypeStruct(chunks.shape, chunks.dtype),
        in_specs=[pl.BlockSpec(memory_space=pltpu.VMEM)],
        out_specs=pl.BlockSpec(memory_space=pltpu.VMEM),
        scratch_shapes=[
            pltpu.VMEM(chunks.shape, chunks.dtype),
            pltpu.VMEM(chunks.shape, chunks.dtype),
            pltpu.SemaphoreType.DMA((4, count)),
        ],
        compiler_params=pltpu.CompilerParams(collective_id=0, has_side_effects=True),
        cost_estimate=pl.CostEstimate(
            flops=values.size, bytes_accessed=6 * values.size, transcendentals=0
        ),
    )(chunks)
    return summed.reshape(shape)


def swap_kernel(to_left_ref, to_right_ref, from_right_ref, from_left_ref, landed, sems):
    count = lax.axis_size("fft")
    me = lax.axis_index("fft")
    band = lax.axis_index("band")
    left = (me + count - 1) % count
    right = (me + 1) % count
    barrier = pltpu.get_barrier_semaphore()
    for neighbour in (left, right):
        pl.semaphore_signal(barrier, inc=1, device_id=(band, neighbour), device_id_type=MESH)
    pl.semaphore_wait(barrier, 2)
    copies = [
        pltpu.make_async_remote_copy(
            src_ref=to_left_ref,
            dst_ref=landed.at[0],
            send_sem=sems.at[0],
            recv_sem=sems.at[1],
            device_id=(band, left),
            device_id_type=MESH,
        ),
        pltpu.make_async_remote_copy(
            src_ref=to_right_ref,
            dst_ref=landed.at[1],
            send_sem=sems.at[2],
            recv_sem=sems.at[3],
            device_id=(band, right),
            device_id_type=MESH,
        ),
    ]
    for copy in copies:
        copy.start()
    for copy in copies:
        copy.wait()
    from_right_ref[...] = landed[0]
    from_left_ref[...] = landed[1]


def neighbour_swap(to_left, to_right, tag):
    shape = jax.ShapeDtypeStruct(to_left.shape, to_left.dtype)
    return pl.pallas_call(
        swap_kernel,
        out_shape=(shape, shape),
        in_specs=[pl.BlockSpec(memory_space=pltpu.VMEM)] * 2,
        out_specs=(pl.BlockSpec(memory_space=pltpu.VMEM),) * 2,
        scratch_shapes=[
            pltpu.VMEM((2,) + to_left.shape, to_left.dtype),
            pltpu.SemaphoreType.DMA((4,)),
        ],
        compiler_params=pltpu.CompilerParams(collective_id=tag, has_side_effects=True),
        cost_estimate=pl.CostEstimate(
            flops=0, bytes_accessed=4 * to_left.size, transcendentals=0
        ),
    )(to_left, to_right)


def extended_2(shard, sides, width):
    for axis, dim in sides:
        count, length = (lax.axis_size(axis), shard.shape[dim])
        up = [(i, (i + 1) % count) for i in range(count)]
        down = [(j, i) for i, j in up]
        last = lax.slice_in_dim(shard, length - width, length, axis=dim)
        first = lax.slice_in_dim(shard, 0, width, axis=dim)
        before = lax.ppermute(last, axis, up)
        after = lax.ppermute(first, axis, down)
        shard = jnp.concatenate([before, shard, after], axis=dim)
    return shard


def passed_along(block, axis, distance):
    devices = range(lax.axis_size(axis))
    route = [((i - distance) % len(devices), i) for i in devices]
    return lax.ppermute(block, axis, route)


def dft_table(length, sign_value):
    indices = jnp.arange(length, dtype=jnp.int32)
    phases = indices[:, None] * indices[None, :] % length
    angles = 2.0 * math.pi / length * phases.astype(jnp.float32)
    factor = 1.0 / math.sqrt(length)
    cosine = jnp.cos(angles) * factor
    sine_part = jnp.sin(angles) * (sign_value * factor)
    upper_rows = jnp.stack([cosine, -sine_part])
    bottom = jnp.stack([sine_part, cosine])
    return jnp.stack([upper_rows, bottom]).astype(jnp.bfloat16)


def wave_squares(indices, length):
    frequency = (
        jnp.where(2 * indices < length, indices, indices - length).astype(jnp.float32) / length
    )
    return frequency * frequency


def per_device(wave_coeffs, occupation, potential, projectors, coupling, sphere_blocks):
    pieces = lax.axis_size("fft")
    slab_index = lax.axis_index("fft")
    coeffs = wave_coeffs[0]
    size_x = coeffs.shape[1]
    columns = coeffs.shape[2]
    size_z = coeffs.shape[3]
    slab_planes = potential.shape[0]
    size_y = potential.shape[1]
    atom_dev = projectors.shape[0]
    nproj_count = projectors.shape[1]
    block_cells = projectors.shape[3]
    zblocks = size_z // block_cells
    plane_blocks = size_y * zblocks
    table_x = dft_table(size_x, 1.0).transpose(0, 2, 1, 3).reshape(2 * size_x, 2 * size_x)
    inverse_y = dft_table(size_y, 1.0)
    inverse_z = dft_table(size_z, 1.0)
    flattened = coeffs.reshape(2 * size_x, columns * size_z)
    along_x = jnp.dot(table_x, flattened, preferred_element_type=jnp.float32)
    along_x = along_x.reshape(2, size_x, columns, size_z).astype(jnp.bfloat16)
    along_y = jnp.einsum(
        "abyk,bxkz->axyz",
        inverse_y,
        lax.all_to_all(along_x, "fft", split_axis=1, concat_axis=2, tiled=True),
        preferred_element_type=jnp.float32,
    ).astype(jnp.bfloat16)
    wave_field = jnp.einsum(
        "abzk,bxyk->axyz", inverse_z, along_y, preferred_element_type=jnp.float32
    ).astype(jnp.bfloat16)
    weights = occupation[0]
    real_part = wave_field[0].astype(jnp.float32)
    imag_part = wave_field[1].astype(jnp.float32)
    partial_density = weights[0] * real_part * real_part + weights[1] * imag_part * imag_part
    density = band_sum(partial_density.astype(jnp.bfloat16))
    strength = 3.0 * math.sqrt(block_cells * projectors.shape[2]) / nproj_count
    coupled = (coupling + coupling.T) * (0.5 * strength)
    slab_blocks = slab_planes * plane_blocks
    slab_rows = slab_planes * size_y
    around = [(slab_index + shift) % pieces for shift in (-1, 0, 1)]
    atom_rows = jnp.stack(
        [lax.dynamic_slice_in_dim(sphere_blocks, d * atom_dev, atom_dev, 0) for d in around]
    ).reshape(-1)
    local_index = atom_rows - slab_index * slab_blocks
    is_mine = (atom_rows // slab_blocks) == slab_index
    row_of = local_index // zblocks
    half_of = (local_index % zblocks)[None, :, None]
    selector = (
        (row_of[:, None] == jnp.arange(slab_rows, dtype=jnp.int32)[None, :]) & is_mine[:, None]
    ).astype(jnp.bfloat16)
    field_rows = wave_field.reshape(2, slab_rows, size_z)
    picked_rows = jnp.einsum(
        "er,crz->cez", selector, field_rows, preferred_element_type=jnp.float32
    ).reshape(2, -1, zblocks, block_cells)
    picked = jnp.zeros_like(picked_rows[:, :, 0])
    for q in range(zblocks):
        picked = jnp.where(half_of == q, picked_rows[:, :, q], picked)
    picked = picked.astype(jnp.bfloat16).reshape(2, 3, atom_dev, -1, block_cells)
    from_right, from_left = neighbour_swap(picked[:, 0], picked[:, 2], 2)
    gathered = picked[:, 1] + from_right + from_left
    projections_own = jnp.einsum(
        "ajsk,bask->abj", projectors, gathered, preferred_element_type=jnp.float32
    )
    energy = jnp.einsum("ij,abj->abi", coupled, projections_own, precision=lax.Precision.HIGHEST)
    spread = jnp.einsum(
        "ajsk,abj->bask", projectors.astype(jnp.float32), energy, precision=lax.Precision.HIGHEST
    )
    spread_sent = spread.astype(jnp.bfloat16)
    spread_right, spread_left = neighbour_swap(spread_sent, spread_sent, 3)
    spread_right = spread_right.astype(jnp.float32)
    spread_left = spread_left.astype(jnp.float32)
    spread_all = jnp.stack([spread_left, spread, spread_right], axis=1).reshape(
        2, -1, 1, block_cells
    )
    placed_halves = jnp.concatenate(
        [jnp.where(half_of[..., None] == q, spread_all, 0.0) for q in range(zblocks)], axis=2
    ).reshape(2, -1, size_z)
    upper = placed_halves.astype(jnp.bfloat16)
    lower = (placed_halves - upper.astype(jnp.float32)).astype(jnp.bfloat16)
    nonlocal_parts = jnp.einsum(
        "er,cez->crz",
        selector,
        jnp.concatenate([upper, lower]),
        preferred_element_type=jnp.float32,
    )
    nonlocal_term = (nonlocal_parts[:2] + nonlocal_parts[2:]).reshape(
        2, slab_planes, size_y, size_z
    )
    total_field = (
        potential.astype(jnp.float32)[None] * wave_field.astype(jnp.float32) + nonlocal_term
    ).astype(jnp.bfloat16)
    forward_z = dft_table(size_z, -1.0)
    forward_y = dft_table(size_y, -1.0)
    forward_x = dft_table(size_x, -1.0)
    back_z = jnp.einsum(
        "abzk,bxyk->axyz", forward_z, total_field, preferred_element_type=jnp.float32
    ).astype(jnp.bfloat16)
    back_y = jnp.einsum(
        "abyk,bxkz->axyz", forward_y, back_z, preferred_element_type=jnp.float32
    ).astype(jnp.bfloat16)
    transformed = jnp.einsum(
        "abxk,bkyz->axyz",
        forward_x,
        lax.all_to_all(back_y, "fft", split_axis=2, concat_axis=1, tiled=True),
        preferred_element_type=jnp.float32,
    )
    index_x = jnp.arange(size_x, dtype=jnp.int32)
    index_y = slab_index * columns + jnp.arange(columns, dtype=jnp.int32)
    index_z = jnp.arange(size_z, dtype=jnp.int32)
    kinetic = (
        wave_squares(index_x, size_x)[:, None, None]
        + wave_squares(index_y, size_y)[None, :, None]
        + wave_squares(index_z, size_z)[None, None, :]
    )
    applied = (transformed + kinetic[None] * coeffs.astype(jnp.float32)).astype(jnp.bfloat16)
    return (applied[None], density, projections_own[None])


def solution(mesh):
    placed = (
        P("band", None, None, "fft", None),
        P("band", None),
        P("fft", None, None),
        P("fft", None, None, None),
        P(),
        P(),
    )
    return jax.shard_map(
        per_device,
        mesh=mesh,
        in_specs=placed,
        out_specs=(
            P("band", None, None, "fft", None),
            P("fft", None, None),
            P("band", "fft", None, None),
        ),
        check_vma=False,
    )
```

```python
import math

import jax
import jax.numpy as jnp
from jax import lax
from jax.experimental import pallas as pl
from jax.experimental.pallas import tpu as pltpu
from jax.sharding import PartitionSpec as P

HALO = 6


MESH = pl.DeviceIdType.MESH


def band_sum_kernel(part_ref, out_ref, received, reduced, sems):
    count = part_ref.shape[0]
    me = lax.axis_index("band")
    column = lax.axis_index("fft")
    barrier = pltpu.get_barrier_semaphore()
    for k in range(1, count):
        pl.semaphore_signal(
            barrier, inc=1, device_id=((me + k) % count, column), device_id_type=MESH
        )
    pl.semaphore_wait(barrier, count - 1)
    scatter = []
    for k in range(1, count):
        target = (me + k) % count
        scatter.append(
            pltpu.make_async_remote_copy(
                src_ref=part_ref.at[target],
                dst_ref=received.at[me],
                send_sem=sems.at[0, k],
                recv_sem=sems.at[1, k],
                device_id=(target, column),
                device_id_type=MESH,
            )
        )
    for copy in scatter:
        copy.start()
    for copy in scatter:
        copy.wait()
    total = part_ref[me].astype(jnp.float32)
    for k in range(1, count):
        total = total + received[(me + count - k) % count].astype(jnp.float32)
    reduced[me] = total.astype(reduced.dtype)
    spread_out = []
    for k in range(1, count):
        target = (me + k) % count
        spread_out.append(
            pltpu.make_async_remote_copy(
                src_ref=reduced.at[me],
                dst_ref=reduced.at[me],
                send_sem=sems.at[2, k],
                recv_sem=sems.at[3, k],
                device_id=(target, column),
                device_id_type=MESH,
            )
        )
    for copy in spread_out:
        copy.start()
    for copy in spread_out:
        copy.wait()
    out_ref[...] = reduced[...]


def band_sum(values):
    count = lax.axis_size("band")
    shape = values.shape
    rows = values.size // (count * 128)
    chunks = values.reshape(count, rows, 128)
    summed = pl.pallas_call(
        band_sum_kernel,
        out_shape=jax.ShapeDtypeStruct(chunks.shape, chunks.dtype),
        in_specs=[pl.BlockSpec(memory_space=pltpu.VMEM)],
        out_specs=pl.BlockSpec(memory_space=pltpu.VMEM),
        scratch_shapes=[
            pltpu.VMEM(chunks.shape, chunks.dtype),
            pltpu.VMEM(chunks.shape, chunks.dtype),
            pltpu.SemaphoreType.DMA((4, count)),
        ],
        compiler_params=pltpu.CompilerParams(collective_id=0, has_side_effects=True),
        cost_estimate=pl.CostEstimate(
            flops=values.size, bytes_accessed=6 * values.size, transcendentals=0
        ),
    )(chunks)
    return summed.reshape(shape)


def swap_kernel(to_left_ref, to_right_ref, from_right_ref, from_left_ref, landed, sems):
    count = lax.axis_size("fft")
    me = lax.axis_index("fft")
    band = lax.axis_index("band")
    left = (me + count - 1) % count
    right = (me + 1) % count
    barrier = pltpu.get_barrier_semaphore()
    for neighbour in (left, right):
        pl.semaphore_signal(barrier, inc=1, device_id=(band, neighbour), device_id_type=MESH)
    pl.semaphore_wait(barrier, 2)
    copies = [
        pltpu.make_async_remote_copy(
            src_ref=to_left_ref,
            dst_ref=landed.at[0],
            send_sem=sems.at[0],
            recv_sem=sems.at[1],
            device_id=(band, left),
            device_id_type=MESH,
        ),
        pltpu.make_async_remote_copy(
            src_ref=to_right_ref,
            dst_ref=landed.at[1],
            send_sem=sems.at[2],
            recv_sem=sems.at[3],
            device_id=(band, right),
            device_id_type=MESH,
        ),
    ]
    for copy in copies:
        copy.start()
    for copy in copies:
        copy.wait()
    from_right_ref[...] = landed[0]
    from_left_ref[...] = landed[1]


def neighbour_swap(to_left, to_right, tag):
    shape = jax.ShapeDtypeStruct(to_left.shape, to_left.dtype)
    return pl.pallas_call(
        swap_kernel,
        out_shape=(shape, shape),
        in_specs=[pl.BlockSpec(memory_space=pltpu.VMEM)] * 2,
        out_specs=(pl.BlockSpec(memory_space=pltpu.VMEM),) * 2,
        scratch_shapes=[
            pltpu.VMEM((2,) + to_left.shape, to_left.dtype),
            pltpu.SemaphoreType.DMA((4,)),
        ],
        compiler_params=pltpu.CompilerParams(collective_id=tag, has_side_effects=True),
        cost_estimate=pl.CostEstimate(
            flops=0, bytes_accessed=4 * to_left.size, transcendentals=0
        ),
    )(to_left, to_right)


def halo_kernel(
    to_left_ref, own_ref, to_right_ref, beta_ref, coupled_ref,
    proj_ref, spread_ref, spread_right_ref, spread_left_ref,
    landed, outgoing, landed_spread, sems,
):
    count = lax.axis_size("fft")
    me = lax.axis_index("fft")
    band = lax.axis_index("band")
    left = (me + count - 1) % count
    right = (me + 1) % count
    barrier = pltpu.get_barrier_semaphore()
    for neighbour in (left, right):
        pl.semaphore_signal(barrier, inc=1, device_id=(band, neighbour), device_id_type=MESH)
    pl.semaphore_wait(barrier, 2)

    def swap(first, second, into, base):
        copies = [
            pltpu.make_async_remote_copy(
                src_ref=first,
                dst_ref=into.at[0],
                send_sem=sems.at[base],
                recv_sem=sems.at[base + 1],
                device_id=(band, left),
                device_id_type=MESH,
            ),
            pltpu.make_async_remote_copy(
                src_ref=second,
                dst_ref=into.at[1],
                send_sem=sems.at[base + 2],
                recv_sem=sems.at[base + 3],
                device_id=(band, right),
                device_id_type=MESH,
            ),
        ]
        for copy in copies:
            copy.start()
        for copy in copies:
            copy.wait()

    swap(to_left_ref, to_right_ref, landed, 0)
    atoms, nproj = beta_ref.shape[0], beta_ref.shape[1]
    lane = lax.broadcasted_iota(jnp.int32, (1, 128), 1)
    for c in range(2):
        for a in range(atoms):
            block = (
                own_ref[c, a].astype(jnp.float32)
                + landed[0, c, a].astype(jnp.float32)
                + landed[1, c, a].astype(jnp.float32)
            )
            sums = []
            row = jnp.zeros((1, 128), jnp.float32)
            for j in range(nproj):
                value = jnp.sum(beta_ref[a, j].astype(jnp.float32) * block, keepdims=True)
                sums.append(value)
                row = row + jnp.where(lane == j, value, 0.0)
            proj_ref[pl.ds(a * 2 + c, 1), :] = row
            spread = jnp.zeros(block.shape, jnp.float32)
            for i in range(nproj):
                energy = sums[0] * coupled_ref[i, 0]
                for j in range(1, nproj):
                    energy = energy + sums[j] * coupled_ref[i, j]
                spread = spread + beta_ref[a, i].astype(jnp.float32) * energy
            spread_ref[c, a] = spread
            outgoing[c, a] = spread.astype(outgoing.dtype)
    swap(outgoing, outgoing, landed_spread, 4)
    spread_right_ref[...] = landed_spread[0]
    spread_left_ref[...] = landed_spread[1]


def halo_exchange(to_left, own, to_right, projectors, coupled):
    atoms = projectors.shape[0]
    half = jax.ShapeDtypeStruct(own.shape, jnp.bfloat16)
    vmem = pl.BlockSpec(memory_space=pltpu.VMEM)
    return pl.pallas_call(
        halo_kernel,
        out_shape=(
            jax.ShapeDtypeStruct((2 * atoms, 128), jnp.float32),
            jax.ShapeDtypeStruct(own.shape, jnp.float32),
            half,
            half,
        ),
        in_specs=[vmem, vmem, vmem, vmem, pl.BlockSpec(memory_space=pltpu.SMEM)],
        out_specs=(vmem, vmem, vmem, vmem),
        scratch_shapes=[
            pltpu.VMEM((2,) + own.shape, jnp.bfloat16),
            pltpu.VMEM(own.shape, jnp.bfloat16),
            pltpu.VMEM((2,) + own.shape, jnp.bfloat16),
            pltpu.SemaphoreType.DMA((8,)),
        ],
        compiler_params=pltpu.CompilerParams(collective_id=2, has_side_effects=True),
        cost_estimate=pl.CostEstimate(
            flops=8 * projectors.size, bytes_accessed=16 * own.size, transcendentals=0
        ),
    )(to_left, own, to_right, projectors, coupled)


def extended_2(shard, sides, width):
    for axis, dim in sides:
        count, length = (lax.axis_size(axis), shard.shape[dim])
        up = [(i, (i + 1) % count) for i in range(count)]
        down = [(j, i) for i, j in up]
        last = lax.slice_in_dim(shard, length - width, length, axis=dim)
        first = lax.slice_in_dim(shard, 0, width, axis=dim)
        before = lax.ppermute(last, axis, up)
        after = lax.ppermute(first, axis, down)
        shard = jnp.concatenate([before, shard, after], axis=dim)
    return shard


def passed_along(block, axis, distance):
    devices = range(lax.axis_size(axis))
    route = [((i - distance) % len(devices), i) for i in devices]
    return lax.ppermute(block, axis, route)


def dft_table(length, sign_value):
    indices = jnp.arange(length, dtype=jnp.int32)
    phases = indices[:, None] * indices[None, :] % length
    angles = 2.0 * math.pi / length * phases.astype(jnp.float32)
    factor = 1.0 / math.sqrt(length)
    cosine = jnp.cos(angles) * factor
    sine_part = jnp.sin(angles) * (sign_value * factor)
    upper_rows = jnp.stack([cosine, -sine_part])
    bottom = jnp.stack([sine_part, cosine])
    return jnp.stack([upper_rows, bottom]).astype(jnp.bfloat16)


def wave_squares(indices, length):
    frequency = (
        jnp.where(2 * indices < length, indices, indices - length).astype(jnp.float32) / length
    )
    return frequency * frequency


def per_device(wave_coeffs, occupation, potential, projectors, coupling, sphere_blocks):
    pieces = lax.axis_size("fft")
    slab_index = lax.axis_index("fft")
    coeffs = wave_coeffs[0]
    size_x = coeffs.shape[1]
    columns = coeffs.shape[2]
    size_z = coeffs.shape[3]
    slab_planes = potential.shape[0]
    size_y = potential.shape[1]
    atom_dev = projectors.shape[0]
    nproj_count = projectors.shape[1]
    block_cells = projectors.shape[3]
    zblocks = size_z // block_cells
    plane_blocks = size_y * zblocks
    table_x = dft_table(size_x, 1.0).transpose(0, 2, 1, 3).reshape(2 * size_x, 2 * size_x)
    inverse_y = dft_table(size_y, 1.0)
    inverse_z = dft_table(size_z, 1.0)
    flattened = coeffs.reshape(2 * size_x, columns * size_z)
    along_x = jnp.dot(table_x, flattened, preferred_element_type=jnp.float32)
    along_x = along_x.reshape(2, size_x, columns, size_z).astype(jnp.bfloat16)
    along_y = jnp.einsum(
        "abyk,bxkz->axyz",
        inverse_y,
        lax.all_to_all(along_x, "fft", split_axis=1, concat_axis=2, tiled=True),
        preferred_element_type=jnp.float32,
    ).astype(jnp.bfloat16)
    wave_field = jnp.einsum(
        "abzk,bxyk->axyz", inverse_z, along_y, preferred_element_type=jnp.float32
    ).astype(jnp.bfloat16)
    weights = occupation[0]
    real_part = wave_field[0].astype(jnp.float32)
    imag_part = wave_field[1].astype(jnp.float32)
    partial_density = weights[0] * real_part * real_part + weights[1] * imag_part * imag_part
    density = band_sum(partial_density.astype(jnp.bfloat16))
    strength = 3.0 * math.sqrt(block_cells * projectors.shape[2]) / nproj_count
    coupled = (coupling + coupling.T) * (0.5 * strength)
    slab_blocks = slab_planes * plane_blocks
    slab_rows = slab_planes * size_y
    around = [(slab_index + shift) % pieces for shift in (-1, 0, 1)]
    atom_rows = jnp.stack(
        [lax.dynamic_slice_in_dim(sphere_blocks, d * atom_dev, atom_dev, 0) for d in around]
    ).reshape(-1)
    local_index = atom_rows - slab_index * slab_blocks
    is_mine = (atom_rows // slab_blocks) == slab_index
    row_of = local_index // zblocks
    half_of = (local_index % zblocks)[None, :, None]
    selector = (
        (row_of[:, None] == jnp.arange(slab_rows, dtype=jnp.int32)[None, :]) & is_mine[:, None]
    ).astype(jnp.bfloat16)
    field_rows = wave_field.reshape(2, slab_rows, size_z)
    picked_rows = jnp.einsum(
        "er,crz->cez", selector, field_rows, preferred_element_type=jnp.float32
    ).reshape(2, -1, zblocks, block_cells)
    picked = jnp.zeros_like(picked_rows[:, :, 0])
    for q in range(zblocks):
        picked = jnp.where(half_of == q, picked_rows[:, :, q], picked)
    picked = picked.astype(jnp.bfloat16).reshape(2, 3, atom_dev, -1, block_cells)
    proj_rows, spread, spread_right, spread_left = halo_exchange(
        picked[:, 0], picked[:, 1], picked[:, 2], projectors, coupled
    )
    projections_own = proj_rows[:, :nproj_count].reshape(atom_dev, 2, nproj_count)
    spread_right = spread_right.astype(jnp.float32)
    spread_left = spread_left.astype(jnp.float32)
    spread_all = jnp.stack([spread_left, spread, spread_right], axis=1).reshape(
        2, -1, 1, block_cells
    )
    placed_halves = jnp.concatenate(
        [jnp.where(half_of[..., None] == q, spread_all, 0.0) for q in range(zblocks)], axis=2
    ).reshape(2, -1, size_z)
    upper = placed_halves.astype(jnp.bfloat16)
    lower = (placed_halves - upper.astype(jnp.float32)).astype(jnp.bfloat16)
    nonlocal_parts = jnp.einsum(
        "er,cez->crz",
        selector,
        jnp.concatenate([upper, lower]),
        preferred_element_type=jnp.float32,
    )
    nonlocal_term = (nonlocal_parts[:2] + nonlocal_parts[2:]).reshape(
        2, slab_planes, size_y, size_z
    )
    total_field = (
        potential.astype(jnp.float32)[None] * wave_field.astype(jnp.float32) + nonlocal_term
    ).astype(jnp.bfloat16)
    forward_z = dft_table(size_z, -1.0)
    forward_y = dft_table(size_y, -1.0)
    forward_x = dft_table(size_x, -1.0)
    back_z = jnp.einsum(
        "abzk,bxyk->axyz", forward_z, total_field, preferred_element_type=jnp.float32
    ).astype(jnp.bfloat16)
    back_y = jnp.einsum(
        "abyk,bxkz->axyz", forward_y, back_z, preferred_element_type=jnp.float32
    ).astype(jnp.bfloat16)
    transformed = jnp.einsum(
        "abxk,bkyz->axyz",
        forward_x,
        lax.all_to_all(back_y, "fft", split_axis=2, concat_axis=1, tiled=True),
        preferred_element_type=jnp.float32,
    )
    index_x = jnp.arange(size_x, dtype=jnp.int32)
    index_y = slab_index * columns + jnp.arange(columns, dtype=jnp.int32)
    index_z = jnp.arange(size_z, dtype=jnp.int32)
    kinetic = (
        wave_squares(index_x, size_x)[:, None, None]
        + wave_squares(index_y, size_y)[None, :, None]
        + wave_squares(index_z, size_z)[None, None, :]
    )
    applied = (transformed + kinetic[None] * coeffs.astype(jnp.float32)).astype(jnp.bfloat16)
    return (applied[None], density, projections_own[None])


def solution(mesh):
    placed = (
        P("band", None, None, "fft", None),
        P("band", None),
        P("fft", None, None),
        P("fft", None, None, None),
        P(),
        P(),
    )
    return jax.shard_map(
        per_device,
        mesh=mesh,
        in_specs=placed,
        out_specs=(
            P("band", None, None, "fft", None),
            P("fft", None, None),
            P("band", "fft", None, None),
        ),
        check_vma=False,
    )
```

```python
import math

import jax
import ml_dtypes
import numpy as np
import jax.numpy as jnp
from jax import lax
from jax.experimental import pallas as pl
from jax.experimental.pallas import tpu as pltpu
from jax.sharding import PartitionSpec as P

HALO = 6


MESH = pl.DeviceIdType.MESH


def band_sum_kernel(part_ref, out_ref, received, reduced, sems):
    count = part_ref.shape[0]
    me = lax.axis_index("band")
    column = lax.axis_index("fft")
    barrier = pltpu.get_barrier_semaphore()
    for k in range(1, count):
        pl.semaphore_signal(
            barrier, inc=1, device_id=((me + k) % count, column), device_id_type=MESH
        )
    pl.semaphore_wait(barrier, count - 1)
    scatter = []
    for k in range(1, count):
        target = (me + k) % count
        scatter.append(
            pltpu.make_async_remote_copy(
                src_ref=part_ref.at[target],
                dst_ref=received.at[me],
                send_sem=sems.at[0, k],
                recv_sem=sems.at[1, k],
                device_id=(target, column),
                device_id_type=MESH,
            )
        )
    for copy in scatter:
        copy.start()
    for copy in scatter:
        copy.wait()
    total = part_ref[me].astype(jnp.float32)
    for k in range(1, count):
        total = total + received[(me + count - k) % count].astype(jnp.float32)
    reduced[me] = total.astype(reduced.dtype)
    spread_out = []
    for k in range(1, count):
        target = (me + k) % count
        spread_out.append(
            pltpu.make_async_remote_copy(
                src_ref=reduced.at[me],
                dst_ref=reduced.at[me],
                send_sem=sems.at[2, k],
                recv_sem=sems.at[3, k],
                device_id=(target, column),
                device_id_type=MESH,
            )
        )
    for copy in spread_out:
        copy.start()
    for copy in spread_out:
        copy.wait()
    out_ref[...] = reduced[...]


def band_sum(values):
    count = lax.axis_size("band")
    shape = values.shape
    rows = values.size // (count * 128)
    chunks = values.reshape(count, rows, 128)
    summed = pl.pallas_call(
        band_sum_kernel,
        out_shape=jax.ShapeDtypeStruct(chunks.shape, chunks.dtype),
        in_specs=[pl.BlockSpec(memory_space=pltpu.VMEM)],
        out_specs=pl.BlockSpec(memory_space=pltpu.VMEM),
        scratch_shapes=[
            pltpu.VMEM(chunks.shape, chunks.dtype),
            pltpu.VMEM(chunks.shape, chunks.dtype),
            pltpu.SemaphoreType.DMA((4, count)),
        ],
        compiler_params=pltpu.CompilerParams(collective_id=0, has_side_effects=True),
        cost_estimate=pl.CostEstimate(
            flops=values.size, bytes_accessed=6 * values.size, transcendentals=0
        ),
    )(chunks)
    return summed.reshape(shape)


def swap_kernel(to_left_ref, to_right_ref, from_right_ref, from_left_ref, landed, sems):
    count = lax.axis_size("fft")
    me = lax.axis_index("fft")
    band = lax.axis_index("band")
    left = (me + count - 1) % count
    right = (me + 1) % count
    barrier = pltpu.get_barrier_semaphore()
    for neighbour in (left, right):
        pl.semaphore_signal(barrier, inc=1, device_id=(band, neighbour), device_id_type=MESH)
    pl.semaphore_wait(barrier, 2)
    copies = [
        pltpu.make_async_remote_copy(
            src_ref=to_left_ref,
            dst_ref=landed.at[0],
            send_sem=sems.at[0],
            recv_sem=sems.at[1],
            device_id=(band, left),
            device_id_type=MESH,
        ),
        pltpu.make_async_remote_copy(
            src_ref=to_right_ref,
            dst_ref=landed.at[1],
            send_sem=sems.at[2],
            recv_sem=sems.at[3],
            device_id=(band, right),
            device_id_type=MESH,
        ),
    ]
    for copy in copies:
        copy.start()
    for copy in copies:
        copy.wait()
    from_right_ref[...] = landed[0]
    from_left_ref[...] = landed[1]


def neighbour_swap(to_left, to_right, tag):
    shape = jax.ShapeDtypeStruct(to_left.shape, to_left.dtype)
    return pl.pallas_call(
        swap_kernel,
        out_shape=(shape, shape),
        in_specs=[pl.BlockSpec(memory_space=pltpu.VMEM)] * 2,
        out_specs=(pl.BlockSpec(memory_space=pltpu.VMEM),) * 2,
        scratch_shapes=[
            pltpu.VMEM((2,) + to_left.shape, to_left.dtype),
            pltpu.SemaphoreType.DMA((4,)),
        ],
        compiler_params=pltpu.CompilerParams(collective_id=tag, has_side_effects=True),
        cost_estimate=pl.CostEstimate(
            flops=0, bytes_accessed=4 * to_left.size, transcendentals=0
        ),
    )(to_left, to_right)


def halo_kernel(
    to_left_ref, own_ref, to_right_ref, beta_ref, coupled_ref,
    proj_ref, spread_ref, spread_right_ref, spread_left_ref,
    landed, outgoing, landed_spread, sems,
):
    count = lax.axis_size("fft")
    me = lax.axis_index("fft")
    band = lax.axis_index("band")
    left = (me + count - 1) % count
    right = (me + 1) % count
    barrier = pltpu.get_barrier_semaphore()
    for neighbour in (left, right):
        pl.semaphore_signal(barrier, inc=1, device_id=(band, neighbour), device_id_type=MESH)
    pl.semaphore_wait(barrier, 2)

    def swap(first, second, into, base):
        copies = [
            pltpu.make_async_remote_copy(
                src_ref=first,
                dst_ref=into.at[0],
                send_sem=sems.at[base],
                recv_sem=sems.at[base + 1],
                device_id=(band, left),
                device_id_type=MESH,
            ),
            pltpu.make_async_remote_copy(
                src_ref=second,
                dst_ref=into.at[1],
                send_sem=sems.at[base + 2],
                recv_sem=sems.at[base + 3],
                device_id=(band, right),
                device_id_type=MESH,
            ),
        ]
        for copy in copies:
            copy.start()
        for copy in copies:
            copy.wait()

    swap(to_left_ref, to_right_ref, landed, 0)
    atoms, nproj = beta_ref.shape[0], beta_ref.shape[1]
    lane = lax.broadcasted_iota(jnp.int32, (1, 128), 1)
    for c in range(2):
        for a in range(atoms):
            block = (
                own_ref[c, a].astype(jnp.float32)
                + landed[0, c, a].astype(jnp.float32)
                + landed[1, c, a].astype(jnp.float32)
            )
            sums = []
            row = jnp.zeros((1, 128), jnp.float32)
            for j in range(nproj):
                value = jnp.sum(beta_ref[a, j].astype(jnp.float32) * block, keepdims=True)
                sums.append(value)
                row = row + jnp.where(lane == j, value, 0.0)
            proj_ref[pl.ds(a * 2 + c, 1), :] = row
            spread = jnp.zeros(block.shape, jnp.float32)
            for i in range(nproj):
                energy = sums[0] * coupled_ref[i, 0]
                for j in range(1, nproj):
                    energy = energy + sums[j] * coupled_ref[i, j]
                spread = spread + beta_ref[a, i].astype(jnp.float32) * energy
            spread_ref[c, a] = spread
            outgoing[c, a] = spread.astype(outgoing.dtype)
    swap(outgoing, outgoing, landed_spread, 4)
    spread_right_ref[...] = landed_spread[0]
    spread_left_ref[...] = landed_spread[1]


def halo_exchange(to_left, own, to_right, projectors, coupled):
    atoms = projectors.shape[0]
    half = jax.ShapeDtypeStruct(own.shape, jnp.bfloat16)
    vmem = pl.BlockSpec(memory_space=pltpu.VMEM)
    return pl.pallas_call(
        halo_kernel,
        out_shape=(
            jax.ShapeDtypeStruct((2 * atoms, 128), jnp.float32),
            jax.ShapeDtypeStruct(own.shape, jnp.float32),
            half,
            half,
        ),
        in_specs=[vmem, vmem, vmem, vmem, pl.BlockSpec(memory_space=pltpu.SMEM)],
        out_specs=(vmem, vmem, vmem, vmem),
        scratch_shapes=[
            pltpu.VMEM((2,) + own.shape, jnp.bfloat16),
            pltpu.VMEM(own.shape, jnp.bfloat16),
            pltpu.VMEM((2,) + own.shape, jnp.bfloat16),
            pltpu.SemaphoreType.DMA((8,)),
        ],
        compiler_params=pltpu.CompilerParams(collective_id=2, has_side_effects=True),
        cost_estimate=pl.CostEstimate(
            flops=8 * projectors.size, bytes_accessed=16 * own.size, transcendentals=0
        ),
    )(to_left, own, to_right, projectors, coupled)


def extended_2(shard, sides, width):
    for axis, dim in sides:
        count, length = (lax.axis_size(axis), shard.shape[dim])
        up = [(i, (i + 1) % count) for i in range(count)]
        down = [(j, i) for i, j in up]
        last = lax.slice_in_dim(shard, length - width, length, axis=dim)
        first = lax.slice_in_dim(shard, 0, width, axis=dim)
        before = lax.ppermute(last, axis, up)
        after = lax.ppermute(first, axis, down)
        shard = jnp.concatenate([before, shard, after], axis=dim)
    return shard


def passed_along(block, axis, distance):
    devices = range(lax.axis_size(axis))
    route = [((i - distance) % len(devices), i) for i in devices]
    return lax.ppermute(block, axis, route)


def dft_table(length, sign_value):
    indices = jnp.arange(length, dtype=jnp.int32)
    phases = indices[:, None] * indices[None, :] % length
    angles = 2.0 * math.pi / length * phases.astype(jnp.float32)
    factor = 1.0 / math.sqrt(length)
    cosine = jnp.cos(angles) * factor
    sine_part = jnp.sin(angles) * (sign_value * factor)
    upper_rows = jnp.stack([cosine, -sine_part])
    bottom = jnp.stack([sine_part, cosine])
    return jnp.stack([upper_rows, bottom]).astype(jnp.bfloat16)


def dft_table_constant(length, sign_value):
    indices = np.arange(length, dtype=np.int64)
    phases = indices[:, None] * indices[None, :] % length
    angles = np.float32(2.0 * math.pi / length) * phases.astype(np.float32)
    factor = np.float32(1.0 / math.sqrt(length))
    cosine = np.cos(angles).astype(np.float32) * factor
    sine_part = np.sin(angles).astype(np.float32) * np.float32(sign_value) * factor
    table = np.stack([np.stack([cosine, -sine_part]), np.stack([sine_part, cosine])])
    return table.astype(ml_dtypes.bfloat16)


def wave_squares(indices, length):
    frequency = (
        jnp.where(2 * indices < length, indices, indices - length).astype(jnp.float32) / length
    )
    return frequency * frequency


def per_device(wave_coeffs, occupation, potential, projectors, coupling, sphere_blocks):
    pieces = lax.axis_size("fft")
    slab_index = lax.axis_index("fft")
    coeffs = wave_coeffs[0]
    size_x = coeffs.shape[1]
    columns = coeffs.shape[2]
    size_z = coeffs.shape[3]
    slab_planes = potential.shape[0]
    size_y = potential.shape[1]
    atom_dev = projectors.shape[0]
    nproj_count = projectors.shape[1]
    block_cells = projectors.shape[3]
    zblocks = size_z // block_cells
    plane_blocks = size_y * zblocks
    table_x = (
        dft_table_constant(size_x, 1.0)
        .reshape(2, 2, pieces, slab_planes, size_x)
        .transpose(2, 0, 3, 1, 4)
        .reshape(2 * size_x, 2 * size_x)
    )
    inverse_y = dft_table(size_y, 1.0)
    inverse_z = dft_table(size_z, 1.0)
    flattened = coeffs.reshape(2 * size_x, columns * size_z)
    along_x = jnp.dot(jnp.asarray(table_x), flattened, preferred_element_type=jnp.float32)
    along_x = along_x.reshape(pieces, 2, slab_planes, columns, size_z).astype(jnp.bfloat16)
    arrived = lax.all_to_all(along_x, "fft", split_axis=0, concat_axis=0, tiled=True)
    along_y = jnp.einsum(
        "abysu,sbxuz->axyz",
        inverse_y.reshape(2, 2, size_y, pieces, columns),
        arrived,
        preferred_element_type=jnp.float32,
    ).astype(jnp.bfloat16)
    wave_field = jnp.einsum(
        "abzk,bxyk->axyz", inverse_z, along_y, preferred_element_type=jnp.float32
    ).astype(jnp.bfloat16)
    weights = occupation[0]
    real_part = wave_field[0].astype(jnp.float32)
    imag_part = wave_field[1].astype(jnp.float32)
    partial_density = weights[0] * real_part * real_part + weights[1] * imag_part * imag_part
    density = band_sum(partial_density.astype(jnp.bfloat16))
    strength = 3.0 * math.sqrt(block_cells * projectors.shape[2]) / nproj_count
    coupled = (coupling + coupling.T) * (0.5 * strength)
    slab_blocks = slab_planes * plane_blocks
    slab_rows = slab_planes * size_y
    around = [(slab_index + shift) % pieces for shift in (-1, 0, 1)]
    atom_rows = jnp.stack(
        [lax.dynamic_slice_in_dim(sphere_blocks, d * atom_dev, atom_dev, 0) for d in around]
    ).reshape(-1)
    local_index = atom_rows - slab_index * slab_blocks
    is_mine = (atom_rows // slab_blocks) == slab_index
    row_of = local_index // zblocks
    half_of = (local_index % zblocks)[None, :, None]
    selector = (
        (row_of[:, None] == jnp.arange(slab_rows, dtype=jnp.int32)[None, :]) & is_mine[:, None]
    ).astype(jnp.bfloat16)
    field_rows = wave_field.reshape(2, slab_rows, size_z)
    picked_rows = jnp.einsum(
        "er,crz->cez", selector, field_rows, preferred_element_type=jnp.float32
    ).reshape(2, -1, zblocks, block_cells)
    picked = jnp.zeros_like(picked_rows[:, :, 0])
    for q in range(zblocks):
        picked = jnp.where(half_of == q, picked_rows[:, :, q], picked)
    picked = picked.astype(jnp.bfloat16).reshape(2, 3, atom_dev, -1, block_cells)
    proj_rows, spread, spread_right, spread_left = halo_exchange(
        picked[:, 0], picked[:, 1], picked[:, 2], projectors, coupled
    )
    projections_own = proj_rows[:, :nproj_count].reshape(atom_dev, 2, nproj_count)
    spread_right = spread_right.astype(jnp.float32)
    spread_left = spread_left.astype(jnp.float32)
    spread_all = jnp.stack([spread_left, spread, spread_right], axis=1).reshape(
        2, -1, 1, block_cells
    )
    placed_halves = jnp.concatenate(
        [jnp.where(half_of[..., None] == q, spread_all, 0.0) for q in range(zblocks)], axis=2
    ).reshape(2, -1, size_z)
    upper = placed_halves.astype(jnp.bfloat16)
    lower = (placed_halves - upper.astype(jnp.float32)).astype(jnp.bfloat16)
    nonlocal_parts = jnp.einsum(
        "er,cez->crz",
        selector,
        jnp.concatenate([upper, lower]),
        preferred_element_type=jnp.float32,
    )
    nonlocal_term = (nonlocal_parts[:2] + nonlocal_parts[2:]).reshape(
        2, slab_planes, size_y, size_z
    )
    total_field = (
        potential.astype(jnp.float32)[None] * wave_field.astype(jnp.float32) + nonlocal_term
    ).astype(jnp.bfloat16)
    forward_z = dft_table(size_z, -1.0)
    forward_y = dft_table(size_y, -1.0)
    forward_x = dft_table(size_x, -1.0)
    back_z = jnp.einsum(
        "abzk,bxyk->axyz", forward_z, total_field, preferred_element_type=jnp.float32
    ).astype(jnp.bfloat16)
    back_y = jnp.einsum(
        "abyk,bxkz->axyz", forward_y, back_z, preferred_element_type=jnp.float32
    ).astype(jnp.bfloat16)
    transformed = jnp.einsum(
        "abxk,bkyz->axyz",
        forward_x,
        lax.all_to_all(back_y, "fft", split_axis=2, concat_axis=1, tiled=True),
        preferred_element_type=jnp.float32,
    )
    index_x = jnp.arange(size_x, dtype=jnp.int32)
    index_y = slab_index * columns + jnp.arange(columns, dtype=jnp.int32)
    index_z = jnp.arange(size_z, dtype=jnp.int32)
    kinetic = (
        wave_squares(index_x, size_x)[:, None, None]
        + wave_squares(index_y, size_y)[None, :, None]
        + wave_squares(index_z, size_z)[None, None, :]
    )
    applied = (transformed + kinetic[None] * coeffs.astype(jnp.float32)).astype(jnp.bfloat16)
    return (applied[None], density, projections_own[None])


def solution(mesh):
    placed = (
        P("band", None, None, "fft", None),
        P("band", None),
        P("fft", None, None),
        P("fft", None, None, None),
        P(),
        P(),
    )
    return jax.shard_map(
        per_device,
        mesh=mesh,
        in_specs=placed,
        out_specs=(
            P("band", None, None, "fft", None),
            P("fft", None, None),
            P("band", "fft", None, None),
        ),
        check_vma=False,
    )
```

```python
import math

import jax
import ml_dtypes
import numpy as np
import jax.numpy as jnp
from jax import lax
from jax.experimental import pallas as pl
from jax.experimental.pallas import tpu as pltpu
from jax.sharding import PartitionSpec as P

HALO = 6


MESH = pl.DeviceIdType.MESH


def band_sum_kernel(part_ref, out_ref, received, reduced, sems):
    count = part_ref.shape[0]
    me = lax.axis_index("band")
    column = lax.axis_index("fft")
    barrier = pltpu.get_barrier_semaphore()
    for k in range(1, count):
        pl.semaphore_signal(
            barrier, inc=1, device_id=((me + k) % count, column), device_id_type=MESH
        )
    pl.semaphore_wait(barrier, count - 1)
    scatter = []
    for k in range(1, count):
        target = (me + k) % count
        scatter.append(
            pltpu.make_async_remote_copy(
                src_ref=part_ref.at[target],
                dst_ref=received.at[me],
                send_sem=sems.at[0, k],
                recv_sem=sems.at[1, k],
                device_id=(target, column),
                device_id_type=MESH,
            )
        )
    for copy in scatter:
        copy.start()
    for copy in scatter:
        copy.wait()
    total = part_ref[me].astype(jnp.float32)
    for k in range(1, count):
        total = total + received[(me + count - k) % count].astype(jnp.float32)
    reduced[me] = total.astype(reduced.dtype)
    spread_out = []
    for k in range(1, count):
        target = (me + k) % count
        spread_out.append(
            pltpu.make_async_remote_copy(
                src_ref=reduced.at[me],
                dst_ref=reduced.at[me],
                send_sem=sems.at[2, k],
                recv_sem=sems.at[3, k],
                device_id=(target, column),
                device_id_type=MESH,
            )
        )
    for copy in spread_out:
        copy.start()
    for copy in spread_out:
        copy.wait()
    out_ref[...] = reduced[...]


def band_sum(values):
    count = lax.axis_size("band")
    shape = values.shape
    rows = values.size // (count * 128)
    chunks = values.reshape(count, rows, 128)
    summed = pl.pallas_call(
        band_sum_kernel,
        out_shape=jax.ShapeDtypeStruct(chunks.shape, chunks.dtype),
        in_specs=[pl.BlockSpec(memory_space=pltpu.VMEM)],
        out_specs=pl.BlockSpec(memory_space=pltpu.VMEM),
        scratch_shapes=[
            pltpu.VMEM(chunks.shape, chunks.dtype),
            pltpu.VMEM(chunks.shape, chunks.dtype),
            pltpu.SemaphoreType.DMA((4, count)),
        ],
        compiler_params=pltpu.CompilerParams(collective_id=0, has_side_effects=True),
        cost_estimate=pl.CostEstimate(
            flops=values.size, bytes_accessed=6 * values.size, transcendentals=0
        ),
    )(chunks)
    return summed.reshape(shape)


def swap_kernel(to_left_ref, to_right_ref, from_right_ref, from_left_ref, landed, sems):
    count = lax.axis_size("fft")
    me = lax.axis_index("fft")
    band = lax.axis_index("band")
    left = (me + count - 1) % count
    right = (me + 1) % count
    barrier = pltpu.get_barrier_semaphore()
    for neighbour in (left, right):
        pl.semaphore_signal(barrier, inc=1, device_id=(band, neighbour), device_id_type=MESH)
    pl.semaphore_wait(barrier, 2)
    copies = [
        pltpu.make_async_remote_copy(
            src_ref=to_left_ref,
            dst_ref=landed.at[0],
            send_sem=sems.at[0],
            recv_sem=sems.at[1],
            device_id=(band, left),
            device_id_type=MESH,
        ),
        pltpu.make_async_remote_copy(
            src_ref=to_right_ref,
            dst_ref=landed.at[1],
            send_sem=sems.at[2],
            recv_sem=sems.at[3],
            device_id=(band, right),
            device_id_type=MESH,
        ),
    ]
    for copy in copies:
        copy.start()
    for copy in copies:
        copy.wait()
    from_right_ref[...] = landed[0]
    from_left_ref[...] = landed[1]


def neighbour_swap(to_left, to_right, tag):
    shape = jax.ShapeDtypeStruct(to_left.shape, to_left.dtype)
    return pl.pallas_call(
        swap_kernel,
        out_shape=(shape, shape),
        in_specs=[pl.BlockSpec(memory_space=pltpu.VMEM)] * 2,
        out_specs=(pl.BlockSpec(memory_space=pltpu.VMEM),) * 2,
        scratch_shapes=[
            pltpu.VMEM((2,) + to_left.shape, to_left.dtype),
            pltpu.SemaphoreType.DMA((4,)),
        ],
        compiler_params=pltpu.CompilerParams(collective_id=tag, has_side_effects=True),
        cost_estimate=pl.CostEstimate(
            flops=0, bytes_accessed=4 * to_left.size, transcendentals=0
        ),
    )(to_left, to_right)


def halo_kernel(
    to_left_ref, own_ref, to_right_ref, beta_ref, coupled_ref,
    proj_ref, spread_ref, spread_right_ref, spread_left_ref,
    landed, outgoing, landed_spread, sems,
):
    count = lax.axis_size("fft")
    me = lax.axis_index("fft")
    band = lax.axis_index("band")
    left = (me + count - 1) % count
    right = (me + 1) % count
    barrier = pltpu.get_barrier_semaphore()
    for neighbour in (left, right):
        pl.semaphore_signal(barrier, inc=1, device_id=(band, neighbour), device_id_type=MESH)
    pl.semaphore_wait(barrier, 2)

    def swap(first, second, into, base):
        copies = [
            pltpu.make_async_remote_copy(
                src_ref=first,
                dst_ref=into.at[0],
                send_sem=sems.at[base],
                recv_sem=sems.at[base + 1],
                device_id=(band, left),
                device_id_type=MESH,
            ),
            pltpu.make_async_remote_copy(
                src_ref=second,
                dst_ref=into.at[1],
                send_sem=sems.at[base + 2],
                recv_sem=sems.at[base + 3],
                device_id=(band, right),
                device_id_type=MESH,
            ),
        ]
        for copy in copies:
            copy.start()
        for copy in copies:
            copy.wait()

    swap(to_left_ref, to_right_ref, landed, 0)
    atoms, nproj = beta_ref.shape[0], beta_ref.shape[1]
    lane = lax.broadcasted_iota(jnp.int32, (1, 128), 1)
    for c in range(2):
        for a in range(atoms):
            block = (
                own_ref[c, a].astype(jnp.float32)
                + landed[0, c, a].astype(jnp.float32)
                + landed[1, c, a].astype(jnp.float32)
            )
            sums = []
            row = jnp.zeros((1, 128), jnp.float32)
            for j in range(nproj):
                value = jnp.sum(beta_ref[a, j].astype(jnp.float32) * block, keepdims=True)
                sums.append(value)
                row = row + jnp.where(lane == j, value, 0.0)
            proj_ref[pl.ds(a * 2 + c, 1), :] = row
            spread = jnp.zeros(block.shape, jnp.float32)
            for i in range(nproj):
                energy = sums[0] * coupled_ref[i, 0]
                for j in range(1, nproj):
                    energy = energy + sums[j] * coupled_ref[i, j]
                spread = spread + beta_ref[a, i].astype(jnp.float32) * energy
            spread_ref[c, a] = spread
            outgoing[c, a] = spread.astype(outgoing.dtype)
    swap(outgoing, outgoing, landed_spread, 4)
    spread_right_ref[...] = landed_spread[0]
    spread_left_ref[...] = landed_spread[1]


def halo_exchange(to_left, own, to_right, projectors, coupled):
    atoms = projectors.shape[0]
    half = jax.ShapeDtypeStruct(own.shape, jnp.bfloat16)
    vmem = pl.BlockSpec(memory_space=pltpu.VMEM)
    return pl.pallas_call(
        halo_kernel,
        out_shape=(
            jax.ShapeDtypeStruct((2 * atoms, 128), jnp.float32),
            jax.ShapeDtypeStruct(own.shape, jnp.float32),
            half,
            half,
        ),
        in_specs=[vmem, vmem, vmem, vmem, pl.BlockSpec(memory_space=pltpu.SMEM)],
        out_specs=(vmem, vmem, vmem, vmem),
        scratch_shapes=[
            pltpu.VMEM((2,) + own.shape, jnp.bfloat16),
            pltpu.VMEM(own.shape, jnp.bfloat16),
            pltpu.VMEM((2,) + own.shape, jnp.bfloat16),
            pltpu.SemaphoreType.DMA((8,)),
        ],
        compiler_params=pltpu.CompilerParams(collective_id=2, has_side_effects=True),
        cost_estimate=pl.CostEstimate(
            flops=8 * projectors.size, bytes_accessed=16 * own.size, transcendentals=0
        ),
    )(to_left, own, to_right, projectors, coupled)


def extended_2(shard, sides, width):
    for axis, dim in sides:
        count, length = (lax.axis_size(axis), shard.shape[dim])
        up = [(i, (i + 1) % count) for i in range(count)]
        down = [(j, i) for i, j in up]
        last = lax.slice_in_dim(shard, length - width, length, axis=dim)
        first = lax.slice_in_dim(shard, 0, width, axis=dim)
        before = lax.ppermute(last, axis, up)
        after = lax.ppermute(first, axis, down)
        shard = jnp.concatenate([before, shard, after], axis=dim)
    return shard


def passed_along(block, axis, distance):
    devices = range(lax.axis_size(axis))
    route = [((i - distance) % len(devices), i) for i in devices]
    return lax.ppermute(block, axis, route)


def dft_table(length, sign_value):
    indices = jnp.arange(length, dtype=jnp.int32)
    phases = indices[:, None] * indices[None, :] % length
    angles = 2.0 * math.pi / length * phases.astype(jnp.float32)
    factor = 1.0 / math.sqrt(length)
    cosine = jnp.cos(angles) * factor
    sine_part = jnp.sin(angles) * (sign_value * factor)
    upper_rows = jnp.stack([cosine, -sine_part])
    bottom = jnp.stack([sine_part, cosine])
    return jnp.stack([upper_rows, bottom]).astype(jnp.bfloat16)


def dft_table_constant(length, sign_value):
    indices = np.arange(length, dtype=np.int64)
    phases = indices[:, None] * indices[None, :] % length
    angles = np.float32(2.0 * math.pi / length) * phases.astype(np.float32)
    factor = np.float32(1.0 / math.sqrt(length))
    cosine = np.cos(angles).astype(np.float32) * factor
    sine_part = np.sin(angles).astype(np.float32) * np.float32(sign_value) * factor
    table = np.stack([np.stack([cosine, -sine_part]), np.stack([sine_part, cosine])])
    return table.astype(ml_dtypes.bfloat16)


def wave_squares(indices, length):
    frequency = (
        jnp.where(2 * indices < length, indices, indices - length).astype(jnp.float32) / length
    )
    return frequency * frequency


def per_device(wave_coeffs, occupation, potential, projectors, coupling, sphere_blocks):
    pieces = lax.axis_size("fft")
    slab_index = lax.axis_index("fft")
    coeffs = wave_coeffs[0]
    size_x = coeffs.shape[1]
    columns = coeffs.shape[2]
    size_z = coeffs.shape[3]
    slab_planes = potential.shape[0]
    size_y = potential.shape[1]
    atom_dev = projectors.shape[0]
    nproj_count = projectors.shape[1]
    block_cells = projectors.shape[3]
    zblocks = size_z // block_cells
    plane_blocks = size_y * zblocks
    table_x = (
        dft_table_constant(size_x, 1.0)
        .reshape(2, 2, pieces, slab_planes, size_x)
        .transpose(2, 0, 3, 1, 4)
        .reshape(2 * size_x, 2 * size_x)
    )
    inverse_y = dft_table(size_y, 1.0)
    inverse_z = dft_table(size_z, 1.0)
    flattened = coeffs.reshape(2 * size_x, columns * size_z)
    along_x = jnp.dot(jnp.asarray(table_x), flattened, preferred_element_type=jnp.float32)
    along_x = along_x.reshape(pieces, 2, slab_planes, columns, size_z).astype(jnp.bfloat16)
    arrived = lax.all_to_all(along_x, "fft", split_axis=0, concat_axis=0, tiled=True)
    along_y = jnp.einsum(
        "abysu,sbxuz->axyz",
        inverse_y.reshape(2, 2, size_y, pieces, columns),
        arrived,
        preferred_element_type=jnp.float32,
    ).astype(jnp.bfloat16)
    wave_field = jnp.einsum(
        "abzk,bxyk->axyz", inverse_z, along_y, preferred_element_type=jnp.float32
    ).astype(jnp.bfloat16)
    weights = occupation[0]
    real_part = wave_field[0].astype(jnp.float32)
    imag_part = wave_field[1].astype(jnp.float32)
    partial_density = weights[0] * real_part * real_part + weights[1] * imag_part * imag_part
    density = band_sum(partial_density.astype(jnp.bfloat16))
    strength = 3.0 * math.sqrt(block_cells * projectors.shape[2]) / nproj_count
    coupled = (coupling + coupling.T) * (0.5 * strength)
    slab_blocks = slab_planes * plane_blocks
    slab_rows = slab_planes * size_y
    around = [(slab_index + shift) % pieces for shift in (-1, 0, 1)]
    atom_rows = jnp.stack(
        [lax.dynamic_slice_in_dim(sphere_blocks, d * atom_dev, atom_dev, 0) for d in around]
    ).reshape(-1)
    local_index = atom_rows - slab_index * slab_blocks
    is_mine = (atom_rows // slab_blocks) == slab_index
    row_of = local_index // zblocks
    half_of = (local_index % zblocks)[None, :, None]
    selector = (
        (row_of[:, None] == jnp.arange(slab_rows, dtype=jnp.int32)[None, :]) & is_mine[:, None]
    ).astype(jnp.bfloat16)
    field_rows = wave_field.reshape(2, slab_rows, size_z)
    picked_rows = jnp.einsum(
        "er,crz->cez", selector, field_rows, preferred_element_type=jnp.float32
    ).reshape(2, -1, zblocks, block_cells)
    picked = jnp.zeros_like(picked_rows[:, :, 0])
    for q in range(zblocks):
        picked = jnp.where(half_of == q, picked_rows[:, :, q], picked)
    picked = picked.astype(jnp.bfloat16).reshape(2, 3, atom_dev, -1, block_cells)
    proj_rows, spread, spread_right, spread_left = halo_exchange(
        picked[:, 0], picked[:, 1], picked[:, 2], projectors, coupled
    )
    projections_own = proj_rows[:, :nproj_count].reshape(atom_dev, 2, nproj_count)
    spread_right = spread_right.astype(jnp.float32)
    spread_left = spread_left.astype(jnp.float32)
    spread_all = jnp.stack([spread_left, spread, spread_right], axis=1).reshape(
        2, -1, 1, block_cells
    )
    placed_halves = jnp.concatenate(
        [jnp.where(half_of[..., None] == q, spread_all, 0.0) for q in range(zblocks)], axis=2
    ).reshape(2, -1, size_z)
    upper = placed_halves.astype(jnp.bfloat16)
    lower = (placed_halves - upper.astype(jnp.float32)).astype(jnp.bfloat16)
    nonlocal_parts = jnp.einsum(
        "er,cez->crz",
        selector,
        jnp.concatenate([upper, lower]),
        preferred_element_type=jnp.float32,
    )
    nonlocal_term = (nonlocal_parts[:2] + nonlocal_parts[2:]).reshape(
        2, slab_planes, size_y, size_z
    )
    total_field = (
        potential.astype(jnp.float32)[None] * wave_field.astype(jnp.float32) + nonlocal_term
    ).astype(jnp.bfloat16)
    forward_z = dft_table(size_z, -1.0)
    forward_y = dft_table(size_y, -1.0)
    back_z = jnp.einsum(
        "abzk,bxyk->axyz", forward_z, total_field, preferred_element_type=jnp.float32
    ).astype(jnp.bfloat16)
    back_y = jnp.einsum(
        "abtuk,bxkz->taxuz",
        forward_y.reshape(2, 2, pieces, columns, size_y),
        back_z,
        preferred_element_type=jnp.float32,
    ).astype(jnp.bfloat16)
    returned = lax.all_to_all(back_y, "fft", split_axis=0, concat_axis=0, tiled=True)
    table_back = (
        dft_table_constant(size_x, -1.0)
        .reshape(2, 2, size_x, pieces, slab_planes)
        .transpose(0, 2, 3, 1, 4)
        .reshape(2 * size_x, 2 * size_x)
    )
    transformed = jnp.dot(
        jnp.asarray(table_back),
        returned.reshape(2 * size_x, columns * size_z),
        preferred_element_type=jnp.float32,
    ).reshape(2, size_x, columns, size_z)
    index_x = jnp.arange(size_x, dtype=jnp.int32)
    index_y = slab_index * columns + jnp.arange(columns, dtype=jnp.int32)
    index_z = jnp.arange(size_z, dtype=jnp.int32)
    kinetic = (
        wave_squares(index_x, size_x)[:, None, None]
        + wave_squares(index_y, size_y)[None, :, None]
        + wave_squares(index_z, size_z)[None, None, :]
    )
    applied = (transformed + kinetic[None] * coeffs.astype(jnp.float32)).astype(jnp.bfloat16)
    return (applied[None], density, projections_own[None])


def solution(mesh):
    placed = (
        P("band", None, None, "fft", None),
        P("band", None),
        P("fft", None, None),
        P("fft", None, None, None),
        P(),
        P(),
    )
    return jax.shard_map(
        per_device,
        mesh=mesh,
        in_specs=placed,
        out_specs=(
            P("band", None, None, "fft", None),
            P("fft", None, None),
            P("band", "fft", None, None),
        ),
        check_vma=False,
    )
```

```python
import math

import jax
import ml_dtypes
import numpy as np
import jax.numpy as jnp
from jax import lax
from jax.experimental import pallas as pl
from jax.experimental.pallas import tpu as pltpu
from jax.sharding import PartitionSpec as P

HALO = 6


MESH = pl.DeviceIdType.MESH


def band_sum_kernel(part_ref, out_ref, received, reduced, sems):
    count = part_ref.shape[0]
    me = lax.axis_index("band")
    column = lax.axis_index("fft")
    barrier = pltpu.get_barrier_semaphore()
    for k in range(1, count):
        pl.semaphore_signal(
            barrier, inc=1, device_id=((me + k) % count, column), device_id_type=MESH
        )
    pl.semaphore_wait(barrier, count - 1)
    scatter = []
    for k in range(1, count):
        target = (me + k) % count
        scatter.append(
            pltpu.make_async_remote_copy(
                src_ref=part_ref.at[target],
                dst_ref=received.at[me],
                send_sem=sems.at[0, k],
                recv_sem=sems.at[1, k],
                device_id=(target, column),
                device_id_type=MESH,
            )
        )
    for copy in scatter:
        copy.start()
    for copy in scatter:
        copy.wait()
    total = part_ref[me].astype(jnp.float32)
    for k in range(1, count):
        total = total + received[(me + count - k) % count].astype(jnp.float32)
    reduced[me] = total.astype(reduced.dtype)
    spread_out = []
    for k in range(1, count):
        target = (me + k) % count
        spread_out.append(
            pltpu.make_async_remote_copy(
                src_ref=reduced.at[me],
                dst_ref=reduced.at[me],
                send_sem=sems.at[2, k],
                recv_sem=sems.at[3, k],
                device_id=(target, column),
                device_id_type=MESH,
            )
        )
    for copy in spread_out:
        copy.start()
    for copy in spread_out:
        copy.wait()
    out_ref[...] = reduced[...]


def band_sum(values):
    count = lax.axis_size("band")
    shape = values.shape
    rows = values.size // (count * 128)
    chunks = values.reshape(count, rows, 128)
    summed = pl.pallas_call(
        band_sum_kernel,
        out_shape=jax.ShapeDtypeStruct(chunks.shape, chunks.dtype),
        in_specs=[pl.BlockSpec(memory_space=pltpu.VMEM)],
        out_specs=pl.BlockSpec(memory_space=pltpu.VMEM),
        scratch_shapes=[
            pltpu.VMEM(chunks.shape, chunks.dtype),
            pltpu.VMEM(chunks.shape, chunks.dtype),
            pltpu.SemaphoreType.DMA((4, count)),
        ],
        compiler_params=pltpu.CompilerParams(collective_id=0, has_side_effects=True),
        cost_estimate=pl.CostEstimate(
            flops=values.size, bytes_accessed=6 * values.size, transcendentals=0
        ),
    )(chunks)
    return summed.reshape(shape)


def swap_kernel(to_left_ref, to_right_ref, from_right_ref, from_left_ref, landed, sems):
    count = lax.axis_size("fft")
    me = lax.axis_index("fft")
    band = lax.axis_index("band")
    left = (me + count - 1) % count
    right = (me + 1) % count
    barrier = pltpu.get_barrier_semaphore()
    for neighbour in (left, right):
        pl.semaphore_signal(barrier, inc=1, device_id=(band, neighbour), device_id_type=MESH)
    pl.semaphore_wait(barrier, 2)
    copies = [
        pltpu.make_async_remote_copy(
            src_ref=to_left_ref,
            dst_ref=landed.at[0],
            send_sem=sems.at[0],
            recv_sem=sems.at[1],
            device_id=(band, left),
            device_id_type=MESH,
        ),
        pltpu.make_async_remote_copy(
            src_ref=to_right_ref,
            dst_ref=landed.at[1],
            send_sem=sems.at[2],
            recv_sem=sems.at[3],
            device_id=(band, right),
            device_id_type=MESH,
        ),
    ]
    for copy in copies:
        copy.start()
    for copy in copies:
        copy.wait()
    from_right_ref[...] = landed[0]
    from_left_ref[...] = landed[1]


def neighbour_swap(to_left, to_right, tag):
    shape = jax.ShapeDtypeStruct(to_left.shape, to_left.dtype)
    return pl.pallas_call(
        swap_kernel,
        out_shape=(shape, shape),
        in_specs=[pl.BlockSpec(memory_space=pltpu.VMEM)] * 2,
        out_specs=(pl.BlockSpec(memory_space=pltpu.VMEM),) * 2,
        scratch_shapes=[
            pltpu.VMEM((2,) + to_left.shape, to_left.dtype),
            pltpu.SemaphoreType.DMA((4,)),
        ],
        compiler_params=pltpu.CompilerParams(collective_id=tag, has_side_effects=True),
        cost_estimate=pl.CostEstimate(
            flops=0, bytes_accessed=4 * to_left.size, transcendentals=0
        ),
    )(to_left, to_right)


def halo_kernel(
    to_left_ref, own_ref, to_right_ref, beta_ref, coupled_ref,
    proj_ref, spread_ref,
    landed, outgoing, landed_spread, sems,
):
    count = lax.axis_size("fft")
    me = lax.axis_index("fft")
    band = lax.axis_index("band")
    left = (me + count - 1) % count
    right = (me + 1) % count
    barrier = pltpu.get_barrier_semaphore()
    for neighbour in (left, right):
        pl.semaphore_signal(barrier, inc=1, device_id=(band, neighbour), device_id_type=MESH)
    pl.semaphore_wait(barrier, 2)

    def swap(first, second, into, base):
        copies = [
            pltpu.make_async_remote_copy(
                src_ref=first,
                dst_ref=into.at[0],
                send_sem=sems.at[base],
                recv_sem=sems.at[base + 1],
                device_id=(band, left),
                device_id_type=MESH,
            ),
            pltpu.make_async_remote_copy(
                src_ref=second,
                dst_ref=into.at[1],
                send_sem=sems.at[base + 2],
                recv_sem=sems.at[base + 3],
                device_id=(band, right),
                device_id_type=MESH,
            ),
        ]
        for copy in copies:
            copy.start()
        for copy in copies:
            copy.wait()

    swap(to_left_ref, to_right_ref, landed, 0)
    atoms, nproj = beta_ref.shape[0], beta_ref.shape[1]
    lane = lax.broadcasted_iota(jnp.int32, (1, 128), 1)
    for c in range(2):
        for a in range(atoms):
            block = (
                own_ref[c, a].astype(jnp.float32)
                + landed[0, c, a].astype(jnp.float32)
                + landed[1, c, a].astype(jnp.float32)
            )
            sums = []
            row = jnp.zeros((1, 128), jnp.float32)
            for j in range(nproj):
                value = jnp.sum(beta_ref[a, j].astype(jnp.float32) * block, keepdims=True)
                sums.append(value)
                row = row + jnp.where(lane == j, value, 0.0)
            proj_ref[pl.ds(a * 2 + c, 1), :] = row
            spread = jnp.zeros(block.shape, jnp.float32)
            for i in range(nproj):
                energy = sums[0] * coupled_ref[i, 0]
                for j in range(1, nproj):
                    energy = energy + sums[j] * coupled_ref[i, j]
                spread = spread + beta_ref[a, i].astype(jnp.float32) * energy
            spread_ref[c, 1, a] = spread
            outgoing[c, a] = spread.astype(outgoing.dtype)
    swap(outgoing, outgoing, landed_spread, 4)
    for c in range(2):
        spread_ref[c, 0] = landed_spread[1, c].astype(jnp.float32)
        spread_ref[c, 2] = landed_spread[0, c].astype(jnp.float32)


def halo_exchange(to_left, own, to_right, projectors, coupled):
    atoms = projectors.shape[0]
    vmem = pl.BlockSpec(memory_space=pltpu.VMEM)
    return pl.pallas_call(
        halo_kernel,
        out_shape=(
            jax.ShapeDtypeStruct((2 * atoms, 128), jnp.float32),
            jax.ShapeDtypeStruct((2, 3) + own.shape[1:], jnp.float32),
        ),
        in_specs=[vmem, vmem, vmem, vmem, pl.BlockSpec(memory_space=pltpu.SMEM)],
        out_specs=(vmem, vmem),
        scratch_shapes=[
            pltpu.VMEM((2,) + own.shape, jnp.bfloat16),
            pltpu.VMEM(own.shape, jnp.bfloat16),
            pltpu.VMEM((2,) + own.shape, jnp.bfloat16),
            pltpu.SemaphoreType.DMA((8,)),
        ],
        compiler_params=pltpu.CompilerParams(collective_id=2, has_side_effects=True),
        cost_estimate=pl.CostEstimate(
            flops=8 * projectors.size, bytes_accessed=16 * own.size, transcendentals=0
        ),
    )(to_left, own, to_right, projectors, coupled)


def extended_2(shard, sides, width):
    for axis, dim in sides:
        count, length = (lax.axis_size(axis), shard.shape[dim])
        up = [(i, (i + 1) % count) for i in range(count)]
        down = [(j, i) for i, j in up]
        last = lax.slice_in_dim(shard, length - width, length, axis=dim)
        first = lax.slice_in_dim(shard, 0, width, axis=dim)
        before = lax.ppermute(last, axis, up)
        after = lax.ppermute(first, axis, down)
        shard = jnp.concatenate([before, shard, after], axis=dim)
    return shard


def passed_along(block, axis, distance):
    devices = range(lax.axis_size(axis))
    route = [((i - distance) % len(devices), i) for i in devices]
    return lax.ppermute(block, axis, route)


def dft_table(length, sign_value):
    indices = jnp.arange(length, dtype=jnp.int32)
    phases = indices[:, None] * indices[None, :] % length
    angles = 2.0 * math.pi / length * phases.astype(jnp.float32)
    factor = 1.0 / math.sqrt(length)
    cosine = jnp.cos(angles) * factor
    sine_part = jnp.sin(angles) * (sign_value * factor)
    upper_rows = jnp.stack([cosine, -sine_part])
    bottom = jnp.stack([sine_part, cosine])
    return jnp.stack([upper_rows, bottom]).astype(jnp.bfloat16)


def dft_table_constant(length, sign_value):
    indices = np.arange(length, dtype=np.int64)
    phases = indices[:, None] * indices[None, :] % length
    angles = np.float32(2.0 * math.pi / length) * phases.astype(np.float32)
    factor = np.float32(1.0 / math.sqrt(length))
    cosine = np.cos(angles).astype(np.float32) * factor
    sine_part = np.sin(angles).astype(np.float32) * np.float32(sign_value) * factor
    table = np.stack([np.stack([cosine, -sine_part]), np.stack([sine_part, cosine])])
    return table.astype(ml_dtypes.bfloat16)


def wave_squares(indices, length):
    frequency = (
        jnp.where(2 * indices < length, indices, indices - length).astype(jnp.float32) / length
    )
    return frequency * frequency


def per_device(wave_coeffs, occupation, potential, projectors, coupling, sphere_blocks):
    pieces = lax.axis_size("fft")
    slab_index = lax.axis_index("fft")
    coeffs = wave_coeffs[0]
    size_x = coeffs.shape[1]
    columns = coeffs.shape[2]
    size_z = coeffs.shape[3]
    slab_planes = potential.shape[0]
    size_y = potential.shape[1]
    atom_dev = projectors.shape[0]
    nproj_count = projectors.shape[1]
    block_cells = projectors.shape[3]
    zblocks = size_z // block_cells
    plane_blocks = size_y * zblocks
    table_x = (
        dft_table_constant(size_x, 1.0)
        .reshape(2, 2, pieces, slab_planes, size_x)
        .transpose(2, 0, 3, 1, 4)
        .reshape(2 * size_x, 2 * size_x)
    )
    inverse_y = dft_table(size_y, 1.0)
    inverse_z = dft_table(size_z, 1.0)
    flattened = coeffs.reshape(2 * size_x, columns * size_z)
    along_x = jnp.dot(jnp.asarray(table_x), flattened, preferred_element_type=jnp.float32)
    along_x = along_x.reshape(pieces, 2, slab_planes, columns, size_z).astype(jnp.bfloat16)
    arrived = lax.all_to_all(along_x, "fft", split_axis=0, concat_axis=0, tiled=True)
    along_y = jnp.einsum(
        "abysu,sbxuz->axyz",
        inverse_y.reshape(2, 2, size_y, pieces, columns),
        arrived,
        preferred_element_type=jnp.float32,
    ).astype(jnp.bfloat16)
    wave_field = jnp.einsum(
        "abzk,bxyk->axyz", inverse_z, along_y, preferred_element_type=jnp.float32
    ).astype(jnp.bfloat16)
    weights = occupation[0]
    real_part = wave_field[0].astype(jnp.float32)
    imag_part = wave_field[1].astype(jnp.float32)
    partial_density = weights[0] * real_part * real_part + weights[1] * imag_part * imag_part
    density = band_sum(partial_density.astype(jnp.bfloat16))
    strength = 3.0 * math.sqrt(block_cells * projectors.shape[2]) / nproj_count
    coupled = (coupling + coupling.T) * (0.5 * strength)
    slab_blocks = slab_planes * plane_blocks
    slab_rows = slab_planes * size_y
    around = [(slab_index + shift) % pieces for shift in (-1, 0, 1)]
    atom_rows = jnp.stack(
        [lax.dynamic_slice_in_dim(sphere_blocks, d * atom_dev, atom_dev, 0) for d in around]
    ).reshape(-1)
    local_index = atom_rows - slab_index * slab_blocks
    is_mine = (atom_rows // slab_blocks) == slab_index
    row_of = local_index // zblocks
    half_of = (local_index % zblocks)[None, :, None]
    selector = (
        (row_of[:, None] == jnp.arange(slab_rows, dtype=jnp.int32)[None, :]) & is_mine[:, None]
    ).astype(jnp.bfloat16)
    field_rows = wave_field.reshape(2, slab_rows, size_z)
    picked_rows = jnp.einsum(
        "er,crz->cez", selector, field_rows, preferred_element_type=jnp.float32
    ).reshape(2, -1, zblocks, block_cells)
    picked = jnp.zeros_like(picked_rows[:, :, 0])
    for q in range(zblocks):
        picked = jnp.where(half_of == q, picked_rows[:, :, q], picked)
    picked = picked.astype(jnp.bfloat16).reshape(2, 3, atom_dev, -1, block_cells)
    proj_rows, spread_all = halo_exchange(
        picked[:, 0], picked[:, 1], picked[:, 2], projectors, coupled
    )
    projections_own = proj_rows[:, :nproj_count].reshape(atom_dev, 2, nproj_count)
    spread_all = spread_all.reshape(2, -1, 1, block_cells)
    placed_halves = jnp.concatenate(
        [jnp.where(half_of[..., None] == q, spread_all, 0.0) for q in range(zblocks)], axis=2
    ).reshape(2, -1, size_z)
    upper = placed_halves.astype(jnp.bfloat16)
    lower = (placed_halves - upper.astype(jnp.float32)).astype(jnp.bfloat16)
    nonlocal_parts = jnp.einsum(
        "er,cez->crz",
        selector,
        jnp.concatenate([upper, lower]),
        preferred_element_type=jnp.float32,
    )
    nonlocal_term = (nonlocal_parts[:2] + nonlocal_parts[2:]).reshape(
        2, slab_planes, size_y, size_z
    )
    total_field = (
        potential.astype(jnp.float32)[None] * wave_field.astype(jnp.float32) + nonlocal_term
    ).astype(jnp.bfloat16)
    forward_z = dft_table(size_z, -1.0)
    forward_y = dft_table(size_y, -1.0)
    forward_x = dft_table(size_x, -1.0)
    back_z = jnp.einsum(
        "abzk,bxyk->axyz", forward_z, total_field, preferred_element_type=jnp.float32
    ).astype(jnp.bfloat16)
    back_y = jnp.einsum(
        "abyk,bxkz->axyz", forward_y, back_z, preferred_element_type=jnp.float32
    ).astype(jnp.bfloat16)
    transformed = jnp.einsum(
        "abxk,bkyz->axyz",
        forward_x,
        lax.all_to_all(back_y, "fft", split_axis=2, concat_axis=1, tiled=True),
        preferred_element_type=jnp.float32,
    )
    index_x = jnp.arange(size_x, dtype=jnp.int32)
    index_y = slab_index * columns + jnp.arange(columns, dtype=jnp.int32)
    index_z = jnp.arange(size_z, dtype=jnp.int32)
    kinetic = (
        wave_squares(index_x, size_x)[:, None, None]
        + wave_squares(index_y, size_y)[None, :, None]
        + wave_squares(index_z, size_z)[None, None, :]
    )
    applied = (transformed + kinetic[None] * coeffs.astype(jnp.float32)).astype(jnp.bfloat16)
    return (applied[None], density, projections_own[None])


def solution(mesh):
    placed = (
        P("band", None, None, "fft", None),
        P("band", None),
        P("fft", None, None),
        P("fft", None, None, None),
        P(),
        P(),
    )
    return jax.shard_map(
        per_device,
        mesh=mesh,
        in_specs=placed,
        out_specs=(
            P("band", None, None, "fft", None),
            P("fft", None, None),
            P("band", "fft", None, None),
        ),
        check_vma=False,
    )
```

```python
import math

import jax
import ml_dtypes
import numpy as np
import jax.numpy as jnp
from jax import lax
from jax.experimental import pallas as pl
from jax.experimental.pallas import tpu as pltpu
from jax.sharding import PartitionSpec as P

HALO = 6


MESH = pl.DeviceIdType.MESH


def band_sum_kernel(part_ref, out_ref, received, reduced, sems):
    count = part_ref.shape[0]
    me = lax.axis_index("band")
    column = lax.axis_index("fft")
    barrier = pltpu.get_barrier_semaphore()
    for k in range(1, count):
        pl.semaphore_signal(
            barrier, inc=1, device_id=((me + k) % count, column), device_id_type=MESH
        )
    pl.semaphore_wait(barrier, count - 1)
    scatter = []
    for k in range(1, count):
        target = (me + k) % count
        scatter.append(
            pltpu.make_async_remote_copy(
                src_ref=part_ref.at[target],
                dst_ref=received.at[me],
                send_sem=sems.at[0, k],
                recv_sem=sems.at[1, k],
                device_id=(target, column),
                device_id_type=MESH,
            )
        )
    for copy in scatter:
        copy.start()
    for copy in scatter:
        copy.wait()
    total = part_ref[me].astype(jnp.float32)
    for k in range(1, count):
        total = total + received[(me + count - k) % count].astype(jnp.float32)
    reduced[me] = total.astype(reduced.dtype)
    spread_out = []
    for k in range(1, count):
        target = (me + k) % count
        spread_out.append(
            pltpu.make_async_remote_copy(
                src_ref=reduced.at[me],
                dst_ref=reduced.at[me],
                send_sem=sems.at[2, k],
                recv_sem=sems.at[3, k],
                device_id=(target, column),
                device_id_type=MESH,
            )
        )
    for copy in spread_out:
        copy.start()
    for copy in spread_out:
        copy.wait()
    out_ref[...] = reduced[...]


def band_sum(values):
    count = lax.axis_size("band")
    shape = values.shape
    rows = values.size // (count * 128)
    chunks = values.reshape(count, rows, 128)
    summed = pl.pallas_call(
        band_sum_kernel,
        out_shape=jax.ShapeDtypeStruct(chunks.shape, chunks.dtype),
        in_specs=[pl.BlockSpec(memory_space=pltpu.VMEM)],
        out_specs=pl.BlockSpec(memory_space=pltpu.VMEM),
        scratch_shapes=[
            pltpu.VMEM(chunks.shape, chunks.dtype),
            pltpu.VMEM(chunks.shape, chunks.dtype),
            pltpu.SemaphoreType.DMA((4, count)),
        ],
        compiler_params=pltpu.CompilerParams(collective_id=0, has_side_effects=True),
        cost_estimate=pl.CostEstimate(
            flops=values.size, bytes_accessed=6 * values.size, transcendentals=0
        ),
    )(chunks)
    return summed.reshape(shape)


def swap_kernel(to_left_ref, to_right_ref, from_right_ref, from_left_ref, landed, sems):
    count = lax.axis_size("fft")
    me = lax.axis_index("fft")
    band = lax.axis_index("band")
    left = (me + count - 1) % count
    right = (me + 1) % count
    barrier = pltpu.get_barrier_semaphore()
    for neighbour in (left, right):
        pl.semaphore_signal(barrier, inc=1, device_id=(band, neighbour), device_id_type=MESH)
    pl.semaphore_wait(barrier, 2)
    copies = [
        pltpu.make_async_remote_copy(
            src_ref=to_left_ref,
            dst_ref=landed.at[0],
            send_sem=sems.at[0],
            recv_sem=sems.at[1],
            device_id=(band, left),
            device_id_type=MESH,
        ),
        pltpu.make_async_remote_copy(
            src_ref=to_right_ref,
            dst_ref=landed.at[1],
            send_sem=sems.at[2],
            recv_sem=sems.at[3],
            device_id=(band, right),
            device_id_type=MESH,
        ),
    ]
    for copy in copies:
        copy.start()
    for copy in copies:
        copy.wait()
    from_right_ref[...] = landed[0]
    from_left_ref[...] = landed[1]


def neighbour_swap(to_left, to_right, tag):
    shape = jax.ShapeDtypeStruct(to_left.shape, to_left.dtype)
    return pl.pallas_call(
        swap_kernel,
        out_shape=(shape, shape),
        in_specs=[pl.BlockSpec(memory_space=pltpu.VMEM)] * 2,
        out_specs=(pl.BlockSpec(memory_space=pltpu.VMEM),) * 2,
        scratch_shapes=[
            pltpu.VMEM((2,) + to_left.shape, to_left.dtype),
            pltpu.SemaphoreType.DMA((4,)),
        ],
        compiler_params=pltpu.CompilerParams(collective_id=tag, has_side_effects=True),
        cost_estimate=pl.CostEstimate(
            flops=0, bytes_accessed=4 * to_left.size, transcendentals=0
        ),
    )(to_left, to_right)


def halo_kernel(
    to_left_ref, own_ref, to_right_ref, beta_ref, coupled_ref,
    proj_ref, spread_ref,
    landed, outgoing, landed_spread, sems,
):
    count = lax.axis_size("fft")
    me = lax.axis_index("fft")
    band = lax.axis_index("band")
    left = (me + count - 1) % count
    right = (me + 1) % count
    barrier = pltpu.get_barrier_semaphore()
    for neighbour in (left, right):
        pl.semaphore_signal(barrier, inc=1, device_id=(band, neighbour), device_id_type=MESH)
    pl.semaphore_wait(barrier, 2)

    def swap(first, second, into, base):
        copies = [
            pltpu.make_async_remote_copy(
                src_ref=first,
                dst_ref=into.at[0],
                send_sem=sems.at[base],
                recv_sem=sems.at[base + 1],
                device_id=(band, left),
                device_id_type=MESH,
            ),
            pltpu.make_async_remote_copy(
                src_ref=second,
                dst_ref=into.at[1],
                send_sem=sems.at[base + 2],
                recv_sem=sems.at[base + 3],
                device_id=(band, right),
                device_id_type=MESH,
            ),
        ]
        for copy in copies:
            copy.start()
        for copy in copies:
            copy.wait()

    swap(to_left_ref, to_right_ref, landed, 0)
    atoms, nproj = beta_ref.shape[0], beta_ref.shape[1]
    lane = lax.broadcasted_iota(jnp.int32, (1, 128), 1)
    for c in range(2):
        for a in range(atoms):
            block = (
                own_ref[c, a].astype(jnp.float32)
                + landed[0, c, a].astype(jnp.float32)
                + landed[1, c, a].astype(jnp.float32)
            )
            sums = []
            row = jnp.zeros((1, 128), jnp.float32)
            for j in range(nproj):
                value = jnp.sum(beta_ref[a, j].astype(jnp.float32) * block, keepdims=True)
                sums.append(value)
                row = row + jnp.where(lane == j, value, 0.0)
            proj_ref[pl.ds(a * 2 + c, 1), :] = row
            spread = jnp.zeros(block.shape, jnp.float32)
            for i in range(nproj):
                energy = sums[0] * coupled_ref[i, 0]
                for j in range(1, nproj):
                    energy = energy + sums[j] * coupled_ref[i, j]
                spread = spread + beta_ref[a, i].astype(jnp.float32) * energy
            spread_ref[c, 1, a] = spread
            outgoing[c, a] = spread.astype(outgoing.dtype)
    swap(outgoing, outgoing, landed_spread, 4)
    for c in range(2):
        spread_ref[c, 0] = landed_spread[1, c].astype(jnp.float32)
        spread_ref[c, 2] = landed_spread[0, c].astype(jnp.float32)


def halo_exchange(to_left, own, to_right, projectors, coupled):
    atoms = projectors.shape[0]
    vmem = pl.BlockSpec(memory_space=pltpu.VMEM)
    return pl.pallas_call(
        halo_kernel,
        out_shape=(
            jax.ShapeDtypeStruct((2 * atoms, 128), jnp.float32),
            jax.ShapeDtypeStruct((2, 3) + own.shape[1:], jnp.float32),
        ),
        in_specs=[vmem, vmem, vmem, vmem, pl.BlockSpec(memory_space=pltpu.SMEM)],
        out_specs=(vmem, vmem),
        scratch_shapes=[
            pltpu.VMEM((2,) + own.shape, jnp.bfloat16),
            pltpu.VMEM(own.shape, jnp.bfloat16),
            pltpu.VMEM((2,) + own.shape, jnp.bfloat16),
            pltpu.SemaphoreType.DMA((8,)),
        ],
        compiler_params=pltpu.CompilerParams(collective_id=2, has_side_effects=True),
        cost_estimate=pl.CostEstimate(
            flops=8 * projectors.size, bytes_accessed=16 * own.size, transcendentals=0
        ),
    )(to_left, own, to_right, projectors, coupled)


def extended_2(shard, sides, width):
    for axis, dim in sides:
        count, length = (lax.axis_size(axis), shard.shape[dim])
        up = [(i, (i + 1) % count) for i in range(count)]
        down = [(j, i) for i, j in up]
        last = lax.slice_in_dim(shard, length - width, length, axis=dim)
        first = lax.slice_in_dim(shard, 0, width, axis=dim)
        before = lax.ppermute(last, axis, up)
        after = lax.ppermute(first, axis, down)
        shard = jnp.concatenate([before, shard, after], axis=dim)
    return shard


def passed_along(block, axis, distance):
    devices = range(lax.axis_size(axis))
    route = [((i - distance) % len(devices), i) for i in devices]
    return lax.ppermute(block, axis, route)


def dft_table(length, sign_value):
    indices = jnp.arange(length, dtype=jnp.int32)
    phases = indices[:, None] * indices[None, :] % length
    angles = 2.0 * math.pi / length * phases.astype(jnp.float32)
    factor = 1.0 / math.sqrt(length)
    cosine = jnp.cos(angles) * factor
    sine_part = jnp.sin(angles) * (sign_value * factor)
    upper_rows = jnp.stack([cosine, -sine_part])
    bottom = jnp.stack([sine_part, cosine])
    return jnp.stack([upper_rows, bottom]).astype(jnp.bfloat16)


def dft_table_constant(length, sign_value):
    indices = np.arange(length, dtype=np.int64)
    phases = indices[:, None] * indices[None, :] % length
    angles = np.float32(2.0 * math.pi / length) * phases.astype(np.float32)
    factor = np.float32(1.0 / math.sqrt(length))
    cosine = np.cos(angles).astype(np.float32) * factor
    sine_part = np.sin(angles).astype(np.float32) * np.float32(sign_value) * factor
    table = np.stack([np.stack([cosine, -sine_part]), np.stack([sine_part, cosine])])
    return table.astype(ml_dtypes.bfloat16)


def wave_squares(indices, length):
    frequency = (
        jnp.where(2 * indices < length, indices, indices - length).astype(jnp.float32) / length
    )
    return frequency * frequency


def per_device(wave_coeffs, occupation, potential, projectors, coupling, sphere_blocks):
    pieces = lax.axis_size("fft")
    slab_index = lax.axis_index("fft")
    coeffs = wave_coeffs[0]
    size_x = coeffs.shape[1]
    columns = coeffs.shape[2]
    size_z = coeffs.shape[3]
    slab_planes = potential.shape[0]
    size_y = potential.shape[1]
    atom_dev = projectors.shape[0]
    nproj_count = projectors.shape[1]
    block_cells = projectors.shape[3]
    zblocks = size_z // block_cells
    plane_blocks = size_y * zblocks
    table_x = (
        dft_table_constant(size_x, 1.0)
        .reshape(2, 2, pieces, slab_planes, size_x)
        .transpose(2, 0, 3, 1, 4)
        .reshape(2 * size_x, 2 * size_x)
    )
    inverse_y = dft_table(size_y, 1.0)
    inverse_z = dft_table(size_z, 1.0)
    table_x = jnp.asarray(table_x).reshape(2 * size_x, 2, size_x)
    along_x = jnp.einsum(
        "ypcx,cxyz->ypz",
        jnp.broadcast_to(table_x[None], (columns,) + table_x.shape),
        coeffs,
        preferred_element_type=jnp.float32,
    ).astype(jnp.bfloat16)
    along_x = along_x.reshape(columns, pieces, 2, slab_planes, size_z).transpose(1, 2, 3, 0, 4)
    arrived = lax.all_to_all(along_x, "fft", split_axis=0, concat_axis=0, tiled=True)
    along_y = jnp.einsum(
        "abysu,sbxuz->axyz",
        inverse_y.reshape(2, 2, size_y, pieces, columns),
        arrived,
        preferred_element_type=jnp.float32,
    ).astype(jnp.bfloat16)
    wave_field = jnp.einsum(
        "abzk,bxyk->axyz", inverse_z, along_y, preferred_element_type=jnp.float32
    ).astype(jnp.bfloat16)
    weights = occupation[0]
    real_part = wave_field[0].astype(jnp.float32)
    imag_part = wave_field[1].astype(jnp.float32)
    partial_density = weights[0] * real_part * real_part + weights[1] * imag_part * imag_part
    density = band_sum(partial_density.astype(jnp.bfloat16))
    strength = 3.0 * math.sqrt(block_cells * projectors.shape[2]) / nproj_count
    coupled = (coupling + coupling.T) * (0.5 * strength)
    slab_blocks = slab_planes * plane_blocks
    slab_rows = slab_planes * size_y
    around = [(slab_index + shift) % pieces for shift in (-1, 0, 1)]
    atom_rows = jnp.stack(
        [lax.dynamic_slice_in_dim(sphere_blocks, d * atom_dev, atom_dev, 0) for d in around]
    ).reshape(-1)
    local_index = atom_rows - slab_index * slab_blocks
    is_mine = (atom_rows // slab_blocks) == slab_index
    row_of = local_index // zblocks
    half_of = (local_index % zblocks)[None, :, None]
    selector = (
        (row_of[:, None] == jnp.arange(slab_rows, dtype=jnp.int32)[None, :]) & is_mine[:, None]
    ).astype(jnp.bfloat16)
    field_rows = wave_field.reshape(2, slab_rows, size_z)
    picked_rows = jnp.einsum(
        "er,crz->cez", selector, field_rows, preferred_element_type=jnp.float32
    ).reshape(2, -1, zblocks, block_cells)
    picked = jnp.zeros_like(picked_rows[:, :, 0])
    for q in range(zblocks):
        picked = jnp.where(half_of == q, picked_rows[:, :, q], picked)
    picked = picked.astype(jnp.bfloat16).reshape(2, 3, atom_dev, -1, block_cells)
    proj_rows, spread_all = halo_exchange(
        picked[:, 0], picked[:, 1], picked[:, 2], projectors, coupled
    )
    projections_own = proj_rows[:, :nproj_count].reshape(atom_dev, 2, nproj_count)
    spread_all = spread_all.reshape(2, -1, 1, block_cells)
    placed_halves = jnp.concatenate(
        [jnp.where(half_of[..., None] == q, spread_all, 0.0) for q in range(zblocks)], axis=2
    ).reshape(2, -1, size_z)
    upper = placed_halves.astype(jnp.bfloat16)
    lower = (placed_halves - upper.astype(jnp.float32)).astype(jnp.bfloat16)
    nonlocal_parts = jnp.einsum(
        "er,cez->crz",
        selector,
        jnp.concatenate([upper, lower]),
        preferred_element_type=jnp.float32,
    )
    nonlocal_term = (nonlocal_parts[:2] + nonlocal_parts[2:]).reshape(
        2, slab_planes, size_y, size_z
    )
    total_field = (
        potential.astype(jnp.float32)[None] * wave_field.astype(jnp.float32) + nonlocal_term
    ).astype(jnp.bfloat16)
    forward_z = dft_table(size_z, -1.0)
    forward_y = dft_table(size_y, -1.0)
    forward_x = dft_table(size_x, -1.0)
    back_z = jnp.einsum(
        "abzk,bxyk->axyz", forward_z, total_field, preferred_element_type=jnp.float32
    ).astype(jnp.bfloat16)
    back_y = jnp.einsum(
        "abyk,bxkz->axyz", forward_y, back_z, preferred_element_type=jnp.float32
    ).astype(jnp.bfloat16)
    transformed = jnp.einsum(
        "abxk,bkyz->axyz",
        forward_x,
        lax.all_to_all(back_y, "fft", split_axis=2, concat_axis=1, tiled=True),
        preferred_element_type=jnp.float32,
    )
    index_x = jnp.arange(size_x, dtype=jnp.int32)
    index_y = slab_index * columns + jnp.arange(columns, dtype=jnp.int32)
    index_z = jnp.arange(size_z, dtype=jnp.int32)
    kinetic = (
        wave_squares(index_x, size_x)[:, None, None]
        + wave_squares(index_y, size_y)[None, :, None]
        + wave_squares(index_z, size_z)[None, None, :]
    )
    applied = (transformed + kinetic[None] * coeffs.astype(jnp.float32)).astype(jnp.bfloat16)
    return (applied[None], density, projections_own[None])


def solution(mesh):
    placed = (
        P("band", None, None, "fft", None),
        P("band", None),
        P("fft", None, None),
        P("fft", None, None, None),
        P(),
        P(),
    )
    return jax.shard_map(
        per_device,
        mesh=mesh,
        in_specs=placed,
        out_specs=(
            P("band", None, None, "fft", None),
            P("fft", None, None),
            P("band", "fft", None, None),
        ),
        check_vma=False,
    )
```

```python
import math

import jax
import ml_dtypes
import numpy as np
import jax.numpy as jnp
from jax import lax
from jax.experimental import pallas as pl
from jax.experimental.pallas import tpu as pltpu
from jax.sharding import PartitionSpec as P

HALO = 6


MESH = pl.DeviceIdType.MESH


def band_sum_kernel(part_ref, out_ref, received, reduced, sems):
    count = part_ref.shape[0]
    me = lax.axis_index("band")
    column = lax.axis_index("fft")
    barrier = pltpu.get_barrier_semaphore()
    for k in range(1, count):
        pl.semaphore_signal(
            barrier, inc=1, device_id=((me + k) % count, column), device_id_type=MESH
        )
    pl.semaphore_wait(barrier, count - 1)
    scatter = []
    for k in range(1, count):
        target = (me + k) % count
        scatter.append(
            pltpu.make_async_remote_copy(
                src_ref=part_ref.at[target],
                dst_ref=received.at[me],
                send_sem=sems.at[0, k],
                recv_sem=sems.at[1, k],
                device_id=(target, column),
                device_id_type=MESH,
            )
        )
    for copy in scatter:
        copy.start()
    for copy in scatter:
        copy.wait()
    total = part_ref[me].astype(jnp.float32)
    for k in range(1, count):
        total = total + received[(me + count - k) % count].astype(jnp.float32)
    reduced[me] = total.astype(reduced.dtype)
    spread_out = []
    for k in range(1, count):
        target = (me + k) % count
        spread_out.append(
            pltpu.make_async_remote_copy(
                src_ref=reduced.at[me],
                dst_ref=reduced.at[me],
                send_sem=sems.at[2, k],
                recv_sem=sems.at[3, k],
                device_id=(target, column),
                device_id_type=MESH,
            )
        )
    for copy in spread_out:
        copy.start()
    for copy in spread_out:
        copy.wait()
    out_ref[...] = reduced[...]


def band_sum(values):
    count = lax.axis_size("band")
    shape = values.shape
    rows = values.size // (count * 128)
    chunks = values.reshape(count, rows, 128)
    summed = pl.pallas_call(
        band_sum_kernel,
        out_shape=jax.ShapeDtypeStruct(chunks.shape, chunks.dtype),
        in_specs=[pl.BlockSpec(memory_space=pltpu.VMEM)],
        out_specs=pl.BlockSpec(memory_space=pltpu.VMEM),
        scratch_shapes=[
            pltpu.VMEM(chunks.shape, chunks.dtype),
            pltpu.VMEM(chunks.shape, chunks.dtype),
            pltpu.SemaphoreType.DMA((4, count)),
        ],
        compiler_params=pltpu.CompilerParams(collective_id=0, has_side_effects=True),
        cost_estimate=pl.CostEstimate(
            flops=values.size, bytes_accessed=6 * values.size, transcendentals=0
        ),
    )(chunks)
    return summed.reshape(shape)


def swap_kernel(to_left_ref, to_right_ref, from_right_ref, from_left_ref, landed, sems):
    count = lax.axis_size("fft")
    me = lax.axis_index("fft")
    band = lax.axis_index("band")
    left = (me + count - 1) % count
    right = (me + 1) % count
    barrier = pltpu.get_barrier_semaphore()
    for neighbour in (left, right):
        pl.semaphore_signal(barrier, inc=1, device_id=(band, neighbour), device_id_type=MESH)
    pl.semaphore_wait(barrier, 2)
    copies = [
        pltpu.make_async_remote_copy(
            src_ref=to_left_ref,
            dst_ref=landed.at[0],
            send_sem=sems.at[0],
            recv_sem=sems.at[1],
            device_id=(band, left),
            device_id_type=MESH,
        ),
        pltpu.make_async_remote_copy(
            src_ref=to_right_ref,
            dst_ref=landed.at[1],
            send_sem=sems.at[2],
            recv_sem=sems.at[3],
            device_id=(band, right),
            device_id_type=MESH,
        ),
    ]
    for copy in copies:
        copy.start()
    for copy in copies:
        copy.wait()
    from_right_ref[...] = landed[0]
    from_left_ref[...] = landed[1]


def neighbour_swap(to_left, to_right, tag):
    shape = jax.ShapeDtypeStruct(to_left.shape, to_left.dtype)
    return pl.pallas_call(
        swap_kernel,
        out_shape=(shape, shape),
        in_specs=[pl.BlockSpec(memory_space=pltpu.VMEM)] * 2,
        out_specs=(pl.BlockSpec(memory_space=pltpu.VMEM),) * 2,
        scratch_shapes=[
            pltpu.VMEM((2,) + to_left.shape, to_left.dtype),
            pltpu.SemaphoreType.DMA((4,)),
        ],
        compiler_params=pltpu.CompilerParams(collective_id=tag, has_side_effects=True),
        cost_estimate=pl.CostEstimate(
            flops=0, bytes_accessed=4 * to_left.size, transcendentals=0
        ),
    )(to_left, to_right)


def halo_kernel(
    to_left_ref, own_ref, to_right_ref, beta_ref, coupled_ref,
    proj_ref, spread_ref,
    landed, outgoing, landed_spread, sems,
):
    count = lax.axis_size("fft")
    me = lax.axis_index("fft")
    band = lax.axis_index("band")
    left = (me + count - 1) % count
    right = (me + 1) % count
    barrier = pltpu.get_barrier_semaphore()
    for neighbour in (left, right):
        pl.semaphore_signal(barrier, inc=1, device_id=(band, neighbour), device_id_type=MESH)
    pl.semaphore_wait(barrier, 2)

    def swap(first, second, into, base):
        copies = [
            pltpu.make_async_remote_copy(
                src_ref=first,
                dst_ref=into.at[0],
                send_sem=sems.at[base],
                recv_sem=sems.at[base + 1],
                device_id=(band, left),
                device_id_type=MESH,
            ),
            pltpu.make_async_remote_copy(
                src_ref=second,
                dst_ref=into.at[1],
                send_sem=sems.at[base + 2],
                recv_sem=sems.at[base + 3],
                device_id=(band, right),
                device_id_type=MESH,
            ),
        ]
        for copy in copies:
            copy.start()
        for copy in copies:
            copy.wait()

    swap(to_left_ref, to_right_ref, landed, 0)
    atoms, nproj = beta_ref.shape[0], beta_ref.shape[1]
    lane = lax.broadcasted_iota(jnp.int32, (1, 128), 1)
    for c in range(2):
        for a in range(atoms):
            block = (
                own_ref[c, a].astype(jnp.float32)
                + landed[0, c, a].astype(jnp.float32)
                + landed[1, c, a].astype(jnp.float32)
            )
            sums = []
            row = jnp.zeros((1, 128), jnp.float32)
            for j in range(nproj):
                value = jnp.sum(beta_ref[a, j].astype(jnp.float32) * block, keepdims=True)
                sums.append(value)
                row = row + jnp.where(lane == j, value, 0.0)
            proj_ref[pl.ds(a * 2 + c, 1), :] = row
            spread = jnp.zeros(block.shape, jnp.float32)
            for i in range(nproj):
                energy = sums[0] * coupled_ref[i, 0]
                for j in range(1, nproj):
                    energy = energy + sums[j] * coupled_ref[i, j]
                spread = spread + beta_ref[a, i].astype(jnp.float32) * energy
            spread_ref[c, 1, a] = spread
            outgoing[c, a] = spread.astype(outgoing.dtype)
    swap(outgoing, outgoing, landed_spread, 4)
    for c in range(2):
        spread_ref[c, 0] = landed_spread[1, c].astype(jnp.float32)
        spread_ref[c, 2] = landed_spread[0, c].astype(jnp.float32)


def halo_exchange(to_left, own, to_right, projectors, coupled):
    atoms = projectors.shape[0]
    vmem = pl.BlockSpec(memory_space=pltpu.VMEM)
    return pl.pallas_call(
        halo_kernel,
        out_shape=(
            jax.ShapeDtypeStruct((2 * atoms, 128), jnp.float32),
            jax.ShapeDtypeStruct((2, 3) + own.shape[1:], jnp.float32),
        ),
        in_specs=[vmem, vmem, vmem, vmem, pl.BlockSpec(memory_space=pltpu.SMEM)],
        out_specs=(vmem, vmem),
        scratch_shapes=[
            pltpu.VMEM((2,) + own.shape, jnp.bfloat16),
            pltpu.VMEM(own.shape, jnp.bfloat16),
            pltpu.VMEM((2,) + own.shape, jnp.bfloat16),
            pltpu.SemaphoreType.DMA((8,)),
        ],
        compiler_params=pltpu.CompilerParams(collective_id=2, has_side_effects=True),
        cost_estimate=pl.CostEstimate(
            flops=8 * projectors.size, bytes_accessed=16 * own.size, transcendentals=0
        ),
    )(to_left, own, to_right, projectors, coupled)


def extended_2(shard, sides, width):
    for axis, dim in sides:
        count, length = (lax.axis_size(axis), shard.shape[dim])
        up = [(i, (i + 1) % count) for i in range(count)]
        down = [(j, i) for i, j in up]
        last = lax.slice_in_dim(shard, length - width, length, axis=dim)
        first = lax.slice_in_dim(shard, 0, width, axis=dim)
        before = lax.ppermute(last, axis, up)
        after = lax.ppermute(first, axis, down)
        shard = jnp.concatenate([before, shard, after], axis=dim)
    return shard


def passed_along(block, axis, distance):
    devices = range(lax.axis_size(axis))
    route = [((i - distance) % len(devices), i) for i in devices]
    return lax.ppermute(block, axis, route)


def dft_table(length, sign_value):
    indices = jnp.arange(length, dtype=jnp.int32)
    phases = indices[:, None] * indices[None, :] % length
    angles = 2.0 * math.pi / length * phases.astype(jnp.float32)
    factor = 1.0 / math.sqrt(length)
    cosine = jnp.cos(angles) * factor
    sine_part = jnp.sin(angles) * (sign_value * factor)
    upper_rows = jnp.stack([cosine, -sine_part])
    bottom = jnp.stack([sine_part, cosine])
    return jnp.stack([upper_rows, bottom]).astype(jnp.bfloat16)


def dft_table_constant(length, sign_value):
    indices = np.arange(length, dtype=np.int64)
    phases = indices[:, None] * indices[None, :] % length
    angles = np.float32(2.0 * math.pi / length) * phases.astype(np.float32)
    factor = np.float32(1.0 / math.sqrt(length))
    cosine = np.cos(angles).astype(np.float32) * factor
    sine_part = np.sin(angles).astype(np.float32) * np.float32(sign_value) * factor
    table = np.stack([np.stack([cosine, -sine_part]), np.stack([sine_part, cosine])])
    return table.astype(ml_dtypes.bfloat16)


def wave_squares(indices, length):
    frequency = (
        jnp.where(2 * indices < length, indices, indices - length).astype(jnp.float32) / length
    )
    return frequency * frequency


def per_device(wave_coeffs, occupation, potential, projectors, coupling, sphere_blocks):
    pieces = lax.axis_size("fft")
    slab_index = lax.axis_index("fft")
    coeffs = wave_coeffs[0]
    size_x = coeffs.shape[1]
    columns = coeffs.shape[2]
    size_z = coeffs.shape[3]
    slab_planes = potential.shape[0]
    size_y = potential.shape[1]
    atom_dev = projectors.shape[0]
    nproj_count = projectors.shape[1]
    block_cells = projectors.shape[3]
    zblocks = size_z // block_cells
    plane_blocks = size_y * zblocks
    table_x = (
        dft_table_constant(size_x, 1.0)
        .reshape(2, 2, pieces, slab_planes, size_x)
        .transpose(2, 0, 3, 1, 4)
        .reshape(2 * size_x, 2 * size_x)
    )
    inverse_y = dft_table(size_y, 1.0)
    inverse_z = dft_table(size_z, 1.0)
    table_x = jnp.asarray(table_x).reshape(2 * size_x, 2, size_x)
    along_x = jnp.einsum(
        "ypcx,cxyz->ypz",
        jnp.broadcast_to(table_x[None], (columns,) + table_x.shape),
        coeffs,
        preferred_element_type=jnp.float32,
    ).astype(jnp.bfloat16)
    along_x = along_x.reshape(columns, pieces, 2, slab_planes, size_z).transpose(1, 2, 3, 0, 4)
    arrived = lax.all_to_all(along_x, "fft", split_axis=0, concat_axis=0, tiled=True)
    along_y = jnp.einsum(
        "abysu,sbxuz->axyz",
        inverse_y.reshape(2, 2, size_y, pieces, columns),
        arrived,
        preferred_element_type=jnp.float32,
    ).astype(jnp.bfloat16)
    wave_field = jnp.einsum(
        "abzk,bxyk->axyz", inverse_z, along_y, preferred_element_type=jnp.float32
    ).astype(jnp.bfloat16)
    weights = occupation[0]
    real_part = wave_field[0].astype(jnp.float32)
    imag_part = wave_field[1].astype(jnp.float32)
    partial_density = weights[0] * real_part * real_part + weights[1] * imag_part * imag_part
    density = band_sum(partial_density.astype(jnp.bfloat16))
    strength = 3.0 * math.sqrt(block_cells * projectors.shape[2]) / nproj_count
    coupled = (coupling + coupling.T) * (0.5 * strength)
    slab_blocks = slab_planes * plane_blocks
    slab_rows = slab_planes * size_y
    around = [(slab_index + shift) % pieces for shift in (-1, 0, 1)]
    atom_rows = jnp.stack(
        [lax.dynamic_slice_in_dim(sphere_blocks, d * atom_dev, atom_dev, 0) for d in around]
    ).reshape(-1)
    local_index = atom_rows - slab_index * slab_blocks
    is_mine = (atom_rows // slab_blocks) == slab_index
    row_of = local_index // zblocks
    half_of = (local_index % zblocks)[None, :, None]
    selector = (
        (row_of[:, None] == jnp.arange(slab_rows, dtype=jnp.int32)[None, :]) & is_mine[:, None]
    ).astype(jnp.bfloat16)
    field_rows = wave_field.reshape(2, slab_rows, size_z)
    picked_rows = jnp.einsum(
        "er,crz->cez", selector, field_rows, preferred_element_type=jnp.float32
    ).reshape(2, -1, zblocks, block_cells)
    picked = jnp.zeros_like(picked_rows[:, :, 0])
    for q in range(zblocks):
        picked = jnp.where(half_of == q, picked_rows[:, :, q], picked)
    picked = picked.astype(jnp.bfloat16).reshape(2, 3, atom_dev, -1, block_cells)
    proj_rows, spread_all = halo_exchange(
        picked[:, 0], picked[:, 1], picked[:, 2], projectors, coupled
    )
    projections_own = proj_rows[:, :nproj_count].reshape(atom_dev, 2, nproj_count)
    spread_all = spread_all.reshape(2, -1, 1, block_cells)
    placed_halves = jnp.concatenate(
        [jnp.where(half_of[..., None] == q, spread_all, 0.0) for q in range(zblocks)], axis=2
    ).reshape(2, -1, size_z)
    upper = placed_halves.astype(jnp.bfloat16)
    lower = (placed_halves - upper.astype(jnp.float32)).astype(jnp.bfloat16)
    scatter_selector = (
        (jnp.arange(slab_rows, dtype=jnp.int32)[:, None] == row_of[None, :]) & is_mine[None, :]
    ).astype(jnp.bfloat16)
    nonlocal_term = jnp.stack(
        [
            jnp.dot(scatter_selector, upper[c], preferred_element_type=jnp.float32)
            + jnp.dot(scatter_selector, lower[c], preferred_element_type=jnp.float32)
            for c in range(2)
        ]
    ).reshape(2, slab_planes, size_y, size_z)
    total_field = (
        potential.astype(jnp.float32)[None] * wave_field.astype(jnp.float32) + nonlocal_term
    ).astype(jnp.bfloat16)
    forward_z = dft_table(size_z, -1.0)
    forward_y = dft_table(size_y, -1.0)
    forward_x = dft_table(size_x, -1.0)
    back_z = jnp.einsum(
        "abzk,bxyk->axyz", forward_z, total_field, preferred_element_type=jnp.float32
    ).astype(jnp.bfloat16)
    back_y = jnp.einsum(
        "abyk,bxkz->axyz", forward_y, back_z, preferred_element_type=jnp.float32
    ).astype(jnp.bfloat16)
    transformed = jnp.einsum(
        "abxk,bkyz->axyz",
        forward_x,
        lax.all_to_all(back_y, "fft", split_axis=2, concat_axis=1, tiled=True),
        preferred_element_type=jnp.float32,
    )
    index_x = jnp.arange(size_x, dtype=jnp.int32)
    index_y = slab_index * columns + jnp.arange(columns, dtype=jnp.int32)
    index_z = jnp.arange(size_z, dtype=jnp.int32)
    kinetic = (
        wave_squares(index_x, size_x)[:, None, None]
        + wave_squares(index_y, size_y)[None, :, None]
        + wave_squares(index_z, size_z)[None, None, :]
    )
    applied = (transformed + kinetic[None] * coeffs.astype(jnp.float32)).astype(jnp.bfloat16)
    return (applied[None], density, projections_own[None])


def solution(mesh):
    placed = (
        P("band", None, None, "fft", None),
        P("band", None),
        P("fft", None, None),
        P("fft", None, None, None),
        P(),
        P(),
    )
    return jax.shard_map(
        per_device,
        mesh=mesh,
        in_specs=placed,
        out_specs=(
            P("band", None, None, "fft", None),
            P("fft", None, None),
            P("band", "fft", None, None),
        ),
        check_vma=False,
    )
```

```python
import math

import jax
import ml_dtypes
import numpy as np
import jax.numpy as jnp
from jax import lax
from jax.experimental import pallas as pl
from jax.experimental.pallas import tpu as pltpu
from jax.sharding import PartitionSpec as P

HALO = 6


MESH = pl.DeviceIdType.MESH


def band_sum_kernel(part_ref, out_ref, received, reduced, sems):
    count = part_ref.shape[0]
    me = lax.axis_index("band")
    column = lax.axis_index("fft")
    barrier = pltpu.get_barrier_semaphore()
    for k in range(1, count):
        pl.semaphore_signal(
            barrier, inc=1, device_id=((me + k) % count, column), device_id_type=MESH
        )
    pl.semaphore_wait(barrier, count - 1)
    scatter = []
    for k in range(1, count):
        target = (me + k) % count
        scatter.append(
            pltpu.make_async_remote_copy(
                src_ref=part_ref.at[target],
                dst_ref=received.at[me],
                send_sem=sems.at[0, k],
                recv_sem=sems.at[1, k],
                device_id=(target, column),
                device_id_type=MESH,
            )
        )
    for copy in scatter:
        copy.start()
    for copy in scatter:
        copy.wait()
    total = part_ref[me].astype(jnp.float32)
    for k in range(1, count):
        total = total + received[(me + count - k) % count].astype(jnp.float32)
    reduced[me] = total.astype(reduced.dtype)
    spread_out = []
    for k in range(1, count):
        target = (me + k) % count
        spread_out.append(
            pltpu.make_async_remote_copy(
                src_ref=reduced.at[me],
                dst_ref=reduced.at[me],
                send_sem=sems.at[2, k],
                recv_sem=sems.at[3, k],
                device_id=(target, column),
                device_id_type=MESH,
            )
        )
    for copy in spread_out:
        copy.start()
    for copy in spread_out:
        copy.wait()
    out_ref[...] = reduced[...]


def band_sum(values):
    count = lax.axis_size("band")
    shape = values.shape
    rows = values.size // (count * 128)
    chunks = values.reshape(count, rows, 128)
    summed = pl.pallas_call(
        band_sum_kernel,
        out_shape=jax.ShapeDtypeStruct(chunks.shape, chunks.dtype),
        in_specs=[pl.BlockSpec(memory_space=pltpu.VMEM)],
        out_specs=pl.BlockSpec(memory_space=pltpu.VMEM),
        scratch_shapes=[
            pltpu.VMEM(chunks.shape, chunks.dtype),
            pltpu.VMEM(chunks.shape, chunks.dtype),
            pltpu.SemaphoreType.DMA((4, count)),
        ],
        compiler_params=pltpu.CompilerParams(collective_id=0, has_side_effects=True),
        cost_estimate=pl.CostEstimate(
            flops=values.size, bytes_accessed=6 * values.size, transcendentals=0
        ),
    )(chunks)
    return summed.reshape(shape)


def swap_kernel(to_left_ref, to_right_ref, from_right_ref, from_left_ref, landed, sems):
    count = lax.axis_size("fft")
    me = lax.axis_index("fft")
    band = lax.axis_index("band")
    left = (me + count - 1) % count
    right = (me + 1) % count
    barrier = pltpu.get_barrier_semaphore()
    for neighbour in (left, right):
        pl.semaphore_signal(barrier, inc=1, device_id=(band, neighbour), device_id_type=MESH)
    pl.semaphore_wait(barrier, 2)
    copies = [
        pltpu.make_async_remote_copy(
            src_ref=to_left_ref,
            dst_ref=landed.at[0],
            send_sem=sems.at[0],
            recv_sem=sems.at[1],
            device_id=(band, left),
            device_id_type=MESH,
        ),
        pltpu.make_async_remote_copy(
            src_ref=to_right_ref,
            dst_ref=landed.at[1],
            send_sem=sems.at[2],
            recv_sem=sems.at[3],
            device_id=(band, right),
            device_id_type=MESH,
        ),
    ]
    for copy in copies:
        copy.start()
    for copy in copies:
        copy.wait()
    from_right_ref[...] = landed[0]
    from_left_ref[...] = landed[1]


def neighbour_swap(to_left, to_right, tag):
    shape = jax.ShapeDtypeStruct(to_left.shape, to_left.dtype)
    return pl.pallas_call(
        swap_kernel,
        out_shape=(shape, shape),
        in_specs=[pl.BlockSpec(memory_space=pltpu.VMEM)] * 2,
        out_specs=(pl.BlockSpec(memory_space=pltpu.VMEM),) * 2,
        scratch_shapes=[
            pltpu.VMEM((2,) + to_left.shape, to_left.dtype),
            pltpu.SemaphoreType.DMA((4,)),
        ],
        compiler_params=pltpu.CompilerParams(collective_id=tag, has_side_effects=True),
        cost_estimate=pl.CostEstimate(
            flops=0, bytes_accessed=4 * to_left.size, transcendentals=0
        ),
    )(to_left, to_right)


def halo_kernel(
    to_left_ref, own_ref, to_right_ref, beta_ref, coupled_ref, lower_half_ref,
    proj_ref, placed_ref,
    landed, outgoing, landed_spread, sems,
):
    count = lax.axis_size("fft")
    me = lax.axis_index("fft")
    band = lax.axis_index("band")
    left = (me + count - 1) % count
    right = (me + 1) % count
    barrier = pltpu.get_barrier_semaphore()
    for neighbour in (left, right):
        pl.semaphore_signal(barrier, inc=1, device_id=(band, neighbour), device_id_type=MESH)
    pl.semaphore_wait(barrier, 2)

    def swap(first, second, into, base):
        copies = [
            pltpu.make_async_remote_copy(
                src_ref=first,
                dst_ref=into.at[0],
                send_sem=sems.at[base],
                recv_sem=sems.at[base + 1],
                device_id=(band, left),
                device_id_type=MESH,
            ),
            pltpu.make_async_remote_copy(
                src_ref=second,
                dst_ref=into.at[1],
                send_sem=sems.at[base + 2],
                recv_sem=sems.at[base + 3],
                device_id=(band, right),
                device_id_type=MESH,
            ),
        ]
        for copy in copies:
            copy.start()
        for copy in copies:
            copy.wait()

    swap(to_left_ref, to_right_ref, landed, 0)
    atoms, nproj = beta_ref.shape[0], beta_ref.shape[1]
    lane = lax.broadcasted_iota(jnp.int32, (1, 128), 1)
    for c in range(2):
        for a in range(atoms):
            block = (
                own_ref[c, a].astype(jnp.float32)
                + landed[0, c, a].astype(jnp.float32)
                + landed[1, c, a].astype(jnp.float32)
            )
            sums = []
            row = jnp.zeros((1, 128), jnp.float32)
            for j in range(nproj):
                value = jnp.sum(beta_ref[a, j].astype(jnp.float32) * block, keepdims=True)
                sums.append(value)
                row = row + jnp.where(lane == j, value, 0.0)
            proj_ref[pl.ds(a * 2 + c, 1), :] = row
            spread = jnp.zeros(block.shape, jnp.float32)
            for i in range(nproj):
                energy = sums[0] * coupled_ref[i, 0]
                for j in range(1, nproj):
                    energy = energy + sums[j] * coupled_ref[i, j]
                spread = spread + beta_ref[a, i].astype(jnp.float32) * energy
            place(placed_ref, lower_half_ref, c, 1, a, spread)
            outgoing[c, a] = spread.astype(outgoing.dtype)
    swap(outgoing, outgoing, landed_spread, 4)
    for c in range(2):
        for a in range(atoms):
            place(placed_ref, lower_half_ref, c, 0, a, landed_spread[1, c, a].astype(jnp.float32))
            place(placed_ref, lower_half_ref, c, 2, a, landed_spread[0, c, a].astype(jnp.float32))


def place(placed_ref, lower_half_ref, c, side, a, value):
    width = value.shape[-1]
    keep = lower_half_ref[side, a]
    upper = value.astype(jnp.bfloat16)
    lower = (value - upper.astype(jnp.float32)).astype(jnp.bfloat16)
    for part, piece in ((0, upper), (1, lower)):
        piece = piece.astype(jnp.float32)
        placed_ref[2 * part + c, side, a, :, pl.ds(0, width)] = (piece * keep).astype(jnp.bfloat16)
        placed_ref[2 * part + c, side, a, :, pl.ds(width, width)] = (
            piece * (1.0 - keep)
        ).astype(jnp.bfloat16)


def halo_exchange(to_left, own, to_right, projectors, coupled, lower_half):
    atoms = projectors.shape[0]
    vmem = pl.BlockSpec(memory_space=pltpu.VMEM)
    return pl.pallas_call(
        halo_kernel,
        out_shape=(
            jax.ShapeDtypeStruct((2 * atoms, 128), jnp.float32),
            jax.ShapeDtypeStruct((4, 3) + own.shape[1:-1] + (2 * own.shape[-1],), jnp.bfloat16),
        ),
        in_specs=[vmem, vmem, vmem, vmem, pl.BlockSpec(memory_space=pltpu.SMEM), vmem],
        out_specs=(vmem, vmem),
        scratch_shapes=[
            pltpu.VMEM((2,) + own.shape, jnp.bfloat16),
            pltpu.VMEM(own.shape, jnp.bfloat16),
            pltpu.VMEM((2,) + own.shape, jnp.bfloat16),
            pltpu.SemaphoreType.DMA((8,)),
        ],
        compiler_params=pltpu.CompilerParams(collective_id=2, has_side_effects=True),
        cost_estimate=pl.CostEstimate(
            flops=8 * projectors.size, bytes_accessed=16 * own.size, transcendentals=0
        ),
    )(to_left, own, to_right, projectors, coupled, lower_half)


def extended_2(shard, sides, width):
    for axis, dim in sides:
        count, length = (lax.axis_size(axis), shard.shape[dim])
        up = [(i, (i + 1) % count) for i in range(count)]
        down = [(j, i) for i, j in up]
        last = lax.slice_in_dim(shard, length - width, length, axis=dim)
        first = lax.slice_in_dim(shard, 0, width, axis=dim)
        before = lax.ppermute(last, axis, up)
        after = lax.ppermute(first, axis, down)
        shard = jnp.concatenate([before, shard, after], axis=dim)
    return shard


def passed_along(block, axis, distance):
    devices = range(lax.axis_size(axis))
    route = [((i - distance) % len(devices), i) for i in devices]
    return lax.ppermute(block, axis, route)


def dft_table(length, sign_value):
    indices = jnp.arange(length, dtype=jnp.int32)
    phases = indices[:, None] * indices[None, :] % length
    angles = 2.0 * math.pi / length * phases.astype(jnp.float32)
    factor = 1.0 / math.sqrt(length)
    cosine = jnp.cos(angles) * factor
    sine_part = jnp.sin(angles) * (sign_value * factor)
    upper_rows = jnp.stack([cosine, -sine_part])
    bottom = jnp.stack([sine_part, cosine])
    return jnp.stack([upper_rows, bottom]).astype(jnp.bfloat16)


def dft_table_constant(length, sign_value):
    indices = np.arange(length, dtype=np.int64)
    phases = indices[:, None] * indices[None, :] % length
    angles = np.float32(2.0 * math.pi / length) * phases.astype(np.float32)
    factor = np.float32(1.0 / math.sqrt(length))
    cosine = np.cos(angles).astype(np.float32) * factor
    sine_part = np.sin(angles).astype(np.float32) * np.float32(sign_value) * factor
    table = np.stack([np.stack([cosine, -sine_part]), np.stack([sine_part, cosine])])
    return table.astype(ml_dtypes.bfloat16)


def wave_squares(indices, length):
    frequency = (
        jnp.where(2 * indices < length, indices, indices - length).astype(jnp.float32) / length
    )
    return frequency * frequency


def per_device(wave_coeffs, occupation, potential, projectors, coupling, sphere_blocks):
    pieces = lax.axis_size("fft")
    slab_index = lax.axis_index("fft")
    coeffs = wave_coeffs[0]
    size_x = coeffs.shape[1]
    columns = coeffs.shape[2]
    size_z = coeffs.shape[3]
    slab_planes = potential.shape[0]
    size_y = potential.shape[1]
    atom_dev = projectors.shape[0]
    nproj_count = projectors.shape[1]
    block_cells = projectors.shape[3]
    zblocks = size_z // block_cells
    plane_blocks = size_y * zblocks
    table_x = (
        dft_table_constant(size_x, 1.0)
        .reshape(2, 2, pieces, slab_planes, size_x)
        .transpose(2, 0, 3, 1, 4)
        .reshape(2 * size_x, 2 * size_x)
    )
    inverse_y = dft_table(size_y, 1.0)
    inverse_z = dft_table(size_z, 1.0)
    table_x = jnp.asarray(table_x).reshape(2 * size_x, 2, size_x)
    along_x = jnp.einsum(
        "ypcx,cxyz->ypz",
        jnp.broadcast_to(table_x[None], (columns,) + table_x.shape),
        coeffs,
        preferred_element_type=jnp.float32,
    ).astype(jnp.bfloat16)
    along_x = along_x.reshape(columns, pieces, 2, slab_planes, size_z).transpose(1, 2, 3, 0, 4)
    arrived = lax.all_to_all(along_x, "fft", split_axis=0, concat_axis=0, tiled=True)
    along_y = jnp.einsum(
        "abysu,sbxuz->axyz",
        inverse_y.reshape(2, 2, size_y, pieces, columns),
        arrived,
        preferred_element_type=jnp.float32,
    ).astype(jnp.bfloat16)
    wave_field = jnp.einsum(
        "abzk,bxyk->axyz", inverse_z, along_y, preferred_element_type=jnp.float32
    ).astype(jnp.bfloat16)
    weights = occupation[0]
    real_part = wave_field[0].astype(jnp.float32)
    imag_part = wave_field[1].astype(jnp.float32)
    partial_density = weights[0] * real_part * real_part + weights[1] * imag_part * imag_part
    density = band_sum(partial_density.astype(jnp.bfloat16))
    strength = 3.0 * math.sqrt(block_cells * projectors.shape[2]) / nproj_count
    coupled = (coupling + coupling.T) * (0.5 * strength)
    slab_blocks = slab_planes * plane_blocks
    slab_rows = slab_planes * size_y
    around = [(slab_index + shift) % pieces for shift in (-1, 0, 1)]
    atom_rows = jnp.stack(
        [lax.dynamic_slice_in_dim(sphere_blocks, d * atom_dev, atom_dev, 0) for d in around]
    ).reshape(-1)
    local_index = atom_rows - slab_index * slab_blocks
    is_mine = (atom_rows // slab_blocks) == slab_index
    row_of = local_index // zblocks
    half_of = (local_index % zblocks)[None, :, None]
    selector = (
        (row_of[:, None] == jnp.arange(slab_rows, dtype=jnp.int32)[None, :]) & is_mine[:, None]
    ).astype(jnp.bfloat16)
    field_rows = wave_field.reshape(2, slab_rows, size_z)
    picked_rows = jnp.einsum(
        "er,crz->cez", selector, field_rows, preferred_element_type=jnp.float32
    ).reshape(2, -1, zblocks, block_cells)
    picked = jnp.zeros_like(picked_rows[:, :, 0])
    for q in range(zblocks):
        picked = jnp.where(half_of == q, picked_rows[:, :, q], picked)
    picked = picked.astype(jnp.bfloat16).reshape(2, 3, atom_dev, -1, block_cells)
    lower_half = jnp.broadcast_to(
        (half_of == 0).astype(jnp.float32).reshape(3, atom_dev, -1, 1),
        (3, atom_dev, projectors.shape[2], block_cells),
    )
    proj_rows, placed = halo_exchange(
        picked[:, 0], picked[:, 1], picked[:, 2], projectors, coupled, lower_half
    )
    projections_own = proj_rows[:, :nproj_count].reshape(atom_dev, 2, nproj_count)
    nonlocal_parts = jnp.einsum(
        "er,cez->crz",
        selector,
        placed.reshape(4, -1, size_z),
        preferred_element_type=jnp.float32,
    )
    nonlocal_term = (nonlocal_parts[:2] + nonlocal_parts[2:]).reshape(
        2, slab_planes, size_y, size_z
    )
    total_field = (
        potential.astype(jnp.float32)[None] * wave_field.astype(jnp.float32) + nonlocal_term
    ).astype(jnp.bfloat16)
    forward_z = dft_table(size_z, -1.0)
    forward_y = dft_table(size_y, -1.0)
    forward_x = dft_table(size_x, -1.0)
    back_z = jnp.einsum(
        "abzk,bxyk->axyz", forward_z, total_field, preferred_element_type=jnp.float32
    ).astype(jnp.bfloat16)
    back_y = jnp.einsum(
        "abyk,bxkz->axyz", forward_y, back_z, preferred_element_type=jnp.float32
    ).astype(jnp.bfloat16)
    transformed = jnp.einsum(
        "abxk,bkyz->axyz",
        forward_x,
        lax.all_to_all(back_y, "fft", split_axis=2, concat_axis=1, tiled=True),
        preferred_element_type=jnp.float32,
    )
    index_x = jnp.arange(size_x, dtype=jnp.int32)
    index_y = slab_index * columns + jnp.arange(columns, dtype=jnp.int32)
    index_z = jnp.arange(size_z, dtype=jnp.int32)
    kinetic = (
        wave_squares(index_x, size_x)[:, None, None]
        + wave_squares(index_y, size_y)[None, :, None]
        + wave_squares(index_z, size_z)[None, None, :]
    )
    applied = (transformed + kinetic[None] * coeffs.astype(jnp.float32)).astype(jnp.bfloat16)
    return (applied[None], density, projections_own[None])


def solution(mesh):
    placed = (
        P("band", None, None, "fft", None),
        P("band", None),
        P("fft", None, None),
        P("fft", None, None, None),
        P(),
        P(),
    )
    return jax.shard_map(
        per_device,
        mesh=mesh,
        in_specs=placed,
        out_specs=(
            P("band", None, None, "fft", None),
            P("fft", None, None),
            P("band", "fft", None, None),
        ),
        check_vma=False,
    )
```

```python
import math

import jax
import ml_dtypes
import numpy as np
import jax.numpy as jnp
from jax import lax
from jax.experimental import pallas as pl
from jax.experimental.pallas import tpu as pltpu
from jax.sharding import PartitionSpec as P

HALO = 6


MESH = pl.DeviceIdType.MESH


def band_sum_kernel(part_ref, out_ref, received, reduced, sems):
    count = part_ref.shape[0]
    me = lax.axis_index("band")
    column = lax.axis_index("fft")
    barrier = pltpu.get_barrier_semaphore()
    for k in range(1, count):
        pl.semaphore_signal(
            barrier, inc=1, device_id=((me + k) % count, column), device_id_type=MESH
        )
    pl.semaphore_wait(barrier, count - 1)
    scatter = []
    for k in range(1, count):
        target = (me + k) % count
        scatter.append(
            pltpu.make_async_remote_copy(
                src_ref=part_ref.at[target],
                dst_ref=received.at[me],
                send_sem=sems.at[0, k],
                recv_sem=sems.at[1, k],
                device_id=(target, column),
                device_id_type=MESH,
            )
        )
    for copy in scatter:
        copy.start()
    for copy in scatter:
        copy.wait()
    total = part_ref[me].astype(jnp.float32)
    for k in range(1, count):
        total = total + received[(me + count - k) % count].astype(jnp.float32)
    reduced[me] = total.astype(reduced.dtype)
    spread_out = []
    for k in range(1, count):
        target = (me + k) % count
        spread_out.append(
            pltpu.make_async_remote_copy(
                src_ref=reduced.at[me],
                dst_ref=reduced.at[me],
                send_sem=sems.at[2, k],
                recv_sem=sems.at[3, k],
                device_id=(target, column),
                device_id_type=MESH,
            )
        )
    for copy in spread_out:
        copy.start()
    for copy in spread_out:
        copy.wait()
    out_ref[...] = reduced[...]


def band_sum(values):
    count = lax.axis_size("band")
    shape = values.shape
    rows = values.size // (count * 128)
    chunks = values.reshape(count, rows, 128)
    summed = pl.pallas_call(
        band_sum_kernel,
        out_shape=jax.ShapeDtypeStruct(chunks.shape, chunks.dtype),
        in_specs=[pl.BlockSpec(memory_space=pltpu.VMEM)],
        out_specs=pl.BlockSpec(memory_space=pltpu.VMEM),
        scratch_shapes=[
            pltpu.VMEM(chunks.shape, chunks.dtype),
            pltpu.VMEM(chunks.shape, chunks.dtype),
            pltpu.SemaphoreType.DMA((4, count)),
        ],
        compiler_params=pltpu.CompilerParams(collective_id=0, has_side_effects=True),
        cost_estimate=pl.CostEstimate(
            flops=values.size, bytes_accessed=6 * values.size, transcendentals=0
        ),
    )(chunks)
    return summed.reshape(shape)


def swap_kernel(to_left_ref, to_right_ref, from_right_ref, from_left_ref, landed, sems):
    count = lax.axis_size("fft")
    me = lax.axis_index("fft")
    band = lax.axis_index("band")
    left = (me + count - 1) % count
    right = (me + 1) % count
    barrier = pltpu.get_barrier_semaphore()
    for neighbour in (left, right):
        pl.semaphore_signal(barrier, inc=1, device_id=(band, neighbour), device_id_type=MESH)
    pl.semaphore_wait(barrier, 2)
    copies = [
        pltpu.make_async_remote_copy(
            src_ref=to_left_ref,
            dst_ref=landed.at[0],
            send_sem=sems.at[0],
            recv_sem=sems.at[1],
            device_id=(band, left),
            device_id_type=MESH,
        ),
        pltpu.make_async_remote_copy(
            src_ref=to_right_ref,
            dst_ref=landed.at[1],
            send_sem=sems.at[2],
            recv_sem=sems.at[3],
            device_id=(band, right),
            device_id_type=MESH,
        ),
    ]
    for copy in copies:
        copy.start()
    for copy in copies:
        copy.wait()
    from_right_ref[...] = landed[0]
    from_left_ref[...] = landed[1]


def neighbour_swap(to_left, to_right, tag):
    shape = jax.ShapeDtypeStruct(to_left.shape, to_left.dtype)
    return pl.pallas_call(
        swap_kernel,
        out_shape=(shape, shape),
        in_specs=[pl.BlockSpec(memory_space=pltpu.VMEM)] * 2,
        out_specs=(pl.BlockSpec(memory_space=pltpu.VMEM),) * 2,
        scratch_shapes=[
            pltpu.VMEM((2,) + to_left.shape, to_left.dtype),
            pltpu.SemaphoreType.DMA((4,)),
        ],
        compiler_params=pltpu.CompilerParams(collective_id=tag, has_side_effects=True),
        cost_estimate=pl.CostEstimate(
            flops=0, bytes_accessed=4 * to_left.size, transcendentals=0
        ),
    )(to_left, to_right)


def halo_kernel(
    to_left_ref, own_ref, to_right_ref, beta_ref, coupled_ref, lower_half_ref,
    proj_ref, placed_ref,
    landed, outgoing, landed_spread, sems,
):
    count = lax.axis_size("fft")
    me = lax.axis_index("fft")
    band = lax.axis_index("band")
    left = (me + count - 1) % count
    right = (me + 1) % count
    barrier = pltpu.get_barrier_semaphore()
    for neighbour in (left, right):
        pl.semaphore_signal(barrier, inc=1, device_id=(band, neighbour), device_id_type=MESH)
    pl.semaphore_wait(barrier, 2)

    def swap(first, second, into, base):
        copies = [
            pltpu.make_async_remote_copy(
                src_ref=first,
                dst_ref=into.at[0],
                send_sem=sems.at[base],
                recv_sem=sems.at[base + 1],
                device_id=(band, left),
                device_id_type=MESH,
            ),
            pltpu.make_async_remote_copy(
                src_ref=second,
                dst_ref=into.at[1],
                send_sem=sems.at[base + 2],
                recv_sem=sems.at[base + 3],
                device_id=(band, right),
                device_id_type=MESH,
            ),
        ]
        for copy in copies:
            copy.start()
        for copy in copies:
            copy.wait()

    swap(to_left_ref, to_right_ref, landed, 0)
    atoms, nproj = beta_ref.shape[0], beta_ref.shape[1]
    lane = lax.broadcasted_iota(jnp.int32, (1, 128), 1)
    for c in range(2):
        for a in range(atoms):
            block = (
                own_ref[c, a].astype(jnp.float32)
                + landed[0, c, a].astype(jnp.float32)
                + landed[1, c, a].astype(jnp.float32)
            )
            sums = []
            row = jnp.zeros((1, 128), jnp.float32)
            for j in range(nproj):
                value = jnp.sum(beta_ref[a, j].astype(jnp.float32) * block, keepdims=True)
                sums.append(value)
                row = row + jnp.where(lane == j, value, 0.0)
            proj_ref[pl.ds(a * 2 + c, 1), :] = row
            spread = jnp.zeros(block.shape, jnp.float32)
            for i in range(nproj):
                energy = sums[0] * coupled_ref[i, 0]
                for j in range(1, nproj):
                    energy = energy + sums[j] * coupled_ref[i, j]
                spread = spread + beta_ref[a, i].astype(jnp.float32) * energy
            place(placed_ref, lower_half_ref, c, 1, a, spread)
            outgoing[c, a] = spread.astype(outgoing.dtype)
    swap(outgoing, outgoing, landed_spread, 4)
    for c in range(2):
        for a in range(atoms):
            place(placed_ref, lower_half_ref, c, 0, a, landed_spread[1, c, a].astype(jnp.float32))
            place(placed_ref, lower_half_ref, c, 2, a, landed_spread[0, c, a].astype(jnp.float32))


def place(placed_ref, lower_half_ref, c, side, a, value):
    width = value.shape[-1]
    keep = lower_half_ref[side, a]
    upper = value.astype(jnp.bfloat16)
    lower = (value - upper.astype(jnp.float32)).astype(jnp.bfloat16)
    for part, piece in ((0, upper), (1, lower)):
        piece = piece.astype(jnp.float32)
        placed_ref[2 * part + c, side, a, :, pl.ds(0, width)] = (piece * keep).astype(jnp.bfloat16)
        placed_ref[2 * part + c, side, a, :, pl.ds(width, width)] = (
            piece * (1.0 - keep)
        ).astype(jnp.bfloat16)


def halo_exchange(to_left, own, to_right, projectors, coupled, lower_half):
    atoms = projectors.shape[0]
    vmem = pl.BlockSpec(memory_space=pltpu.VMEM)
    return pl.pallas_call(
        halo_kernel,
        out_shape=(
            jax.ShapeDtypeStruct((2 * atoms, 128), jnp.float32),
            jax.ShapeDtypeStruct((4, 3) + own.shape[1:-1] + (2 * own.shape[-1],), jnp.bfloat16),
        ),
        in_specs=[vmem, vmem, vmem, vmem, pl.BlockSpec(memory_space=pltpu.SMEM), vmem],
        out_specs=(vmem, vmem),
        scratch_shapes=[
            pltpu.VMEM((2,) + own.shape, jnp.bfloat16),
            pltpu.VMEM(own.shape, jnp.bfloat16),
            pltpu.VMEM((2,) + own.shape, jnp.bfloat16),
            pltpu.SemaphoreType.DMA((8,)),
        ],
        compiler_params=pltpu.CompilerParams(collective_id=2, has_side_effects=True),
        cost_estimate=pl.CostEstimate(
            flops=8 * projectors.size, bytes_accessed=16 * own.size, transcendentals=0
        ),
    )(to_left, own, to_right, projectors, coupled, lower_half)


def extended_2(shard, sides, width):
    for axis, dim in sides:
        count, length = (lax.axis_size(axis), shard.shape[dim])
        up = [(i, (i + 1) % count) for i in range(count)]
        down = [(j, i) for i, j in up]
        last = lax.slice_in_dim(shard, length - width, length, axis=dim)
        first = lax.slice_in_dim(shard, 0, width, axis=dim)
        before = lax.ppermute(last, axis, up)
        after = lax.ppermute(first, axis, down)
        shard = jnp.concatenate([before, shard, after], axis=dim)
    return shard


def passed_along(block, axis, distance):
    devices = range(lax.axis_size(axis))
    route = [((i - distance) % len(devices), i) for i in devices]
    return lax.ppermute(block, axis, route)


def dft_table(length, sign_value):
    indices = jnp.arange(length, dtype=jnp.int32)
    phases = indices[:, None] * indices[None, :] % length
    angles = 2.0 * math.pi / length * phases.astype(jnp.float32)
    factor = 1.0 / math.sqrt(length)
    cosine = jnp.cos(angles) * factor
    sine_part = jnp.sin(angles) * (sign_value * factor)
    upper_rows = jnp.stack([cosine, -sine_part])
    bottom = jnp.stack([sine_part, cosine])
    return jnp.stack([upper_rows, bottom]).astype(jnp.bfloat16)


def dft_table_constant(length, sign_value):
    indices = np.arange(length, dtype=np.int64)
    phases = indices[:, None] * indices[None, :] % length
    angles = np.float32(2.0 * math.pi / length) * phases.astype(np.float32)
    factor = np.float32(1.0 / math.sqrt(length))
    cosine = np.cos(angles).astype(np.float32) * factor
    sine_part = np.sin(angles).astype(np.float32) * np.float32(sign_value) * factor
    table = np.stack([np.stack([cosine, -sine_part]), np.stack([sine_part, cosine])])
    return table.astype(ml_dtypes.bfloat16)


def wave_squares(indices, length):
    frequency = (
        jnp.where(2 * indices < length, indices, indices - length).astype(jnp.float32) / length
    )
    return frequency * frequency


def per_device(wave_coeffs, occupation, potential, projectors, coupling, sphere_blocks):
    pieces = lax.axis_size("fft")
    slab_index = lax.axis_index("fft")
    coeffs = wave_coeffs[0]
    size_x = coeffs.shape[1]
    columns = coeffs.shape[2]
    size_z = coeffs.shape[3]
    slab_planes = potential.shape[0]
    size_y = potential.shape[1]
    atom_dev = projectors.shape[0]
    nproj_count = projectors.shape[1]
    block_cells = projectors.shape[3]
    zblocks = size_z // block_cells
    plane_blocks = size_y * zblocks
    table_x = (
        dft_table_constant(size_x, 1.0)
        .reshape(2, 2, pieces, slab_planes, size_x)
        .transpose(2, 0, 3, 1, 4)
        .reshape(2 * size_x, 2 * size_x)
    )
    inverse_y = dft_table(size_y, 1.0)
    inverse_z = dft_table(size_z, 1.0)
    table_x = jnp.asarray(table_x).reshape(2 * size_x, 2, size_x)
    along_x = jnp.einsum(
        "ypcx,cxyz->ypz",
        jnp.broadcast_to(table_x[None], (columns,) + table_x.shape),
        coeffs,
        preferred_element_type=jnp.float32,
    ).astype(jnp.bfloat16)
    along_x = along_x.reshape(columns, pieces, 2, slab_planes, size_z).transpose(1, 2, 3, 0, 4)
    arrived = lax.all_to_all(along_x, "fft", split_axis=0, concat_axis=0, tiled=True)
    along_y = jnp.einsum(
        "abysu,sbxuz->axyz",
        inverse_y.reshape(2, 2, size_y, pieces, columns),
        arrived,
        preferred_element_type=jnp.float32,
    ).astype(jnp.bfloat16)
    wave_field = jnp.einsum(
        "abzk,bxyk->axyz", inverse_z, along_y, preferred_element_type=jnp.float32
    ).astype(jnp.bfloat16)
    weights = occupation[0]
    real_part = wave_field[0].astype(jnp.float32)
    imag_part = wave_field[1].astype(jnp.float32)
    partial_density = weights[0] * real_part * real_part + weights[1] * imag_part * imag_part
    density = band_sum(partial_density.astype(jnp.bfloat16))
    strength = 3.0 * math.sqrt(block_cells * projectors.shape[2]) / nproj_count
    coupled = (coupling + coupling.T) * (0.5 * strength)
    slab_blocks = slab_planes * plane_blocks
    slab_rows = slab_planes * size_y
    around = [(slab_index + shift) % pieces for shift in (-1, 0, 1)]
    atom_rows = jnp.stack(
        [lax.dynamic_slice_in_dim(sphere_blocks, d * atom_dev, atom_dev, 0) for d in around]
    ).reshape(-1)
    local_index = atom_rows - slab_index * slab_blocks
    is_mine = (atom_rows // slab_blocks) == slab_index
    row_of = local_index // zblocks
    half_of = (local_index % zblocks)[None, :, None]
    selector = (
        (row_of[:, None] == jnp.arange(slab_rows, dtype=jnp.int32)[None, :]) & is_mine[:, None]
    ).astype(jnp.bfloat16)
    field_rows = wave_field.reshape(2, slab_rows, size_z)
    picked_rows = jnp.einsum(
        "er,crz->cez", selector, field_rows, preferred_element_type=jnp.float32
    ).reshape(2, -1, zblocks, block_cells)
    picked = jnp.zeros_like(picked_rows[:, :, 0])
    for q in range(zblocks):
        picked = jnp.where(half_of == q, picked_rows[:, :, q], picked)
    picked = picked.astype(jnp.bfloat16).reshape(2, 3, atom_dev, -1, block_cells)
    lower_half = (half_of == 0).astype(jnp.float32).reshape(3, atom_dev, -1, 1)
    proj_rows, placed = halo_exchange(
        picked[:, 0], picked[:, 1], picked[:, 2], projectors, coupled, lower_half
    )
    projections_own = proj_rows[:, :nproj_count].reshape(atom_dev, 2, nproj_count)
    nonlocal_parts = jnp.einsum(
        "er,cez->crz",
        selector,
        placed.reshape(4, -1, size_z),
        preferred_element_type=jnp.float32,
    )
    nonlocal_term = (nonlocal_parts[:2] + nonlocal_parts[2:]).reshape(
        2, slab_planes, size_y, size_z
    )
    total_field = (
        potential.astype(jnp.float32)[None] * wave_field.astype(jnp.float32) + nonlocal_term
    ).astype(jnp.bfloat16)
    forward_z = dft_table(size_z, -1.0)
    forward_y = dft_table(size_y, -1.0)
    forward_x = dft_table(size_x, -1.0)
    back_z = jnp.einsum(
        "abzk,bxyk->axyz", forward_z, total_field, preferred_element_type=jnp.float32
    ).astype(jnp.bfloat16)
    back_y = jnp.einsum(
        "abyk,bxkz->axyz", forward_y, back_z, preferred_element_type=jnp.float32
    ).astype(jnp.bfloat16)
    transformed = jnp.einsum(
        "abxk,bkyz->axyz",
        forward_x,
        lax.all_to_all(back_y, "fft", split_axis=2, concat_axis=1, tiled=True),
        preferred_element_type=jnp.float32,
    )
    index_x = jnp.arange(size_x, dtype=jnp.int32)
    index_y = slab_index * columns + jnp.arange(columns, dtype=jnp.int32)
    index_z = jnp.arange(size_z, dtype=jnp.int32)
    kinetic = (
        wave_squares(index_x, size_x)[:, None, None]
        + wave_squares(index_y, size_y)[None, :, None]
        + wave_squares(index_z, size_z)[None, None, :]
    )
    applied = (transformed + kinetic[None] * coeffs.astype(jnp.float32)).astype(jnp.bfloat16)
    return (applied[None], density, projections_own[None])


def solution(mesh):
    placed = (
        P("band", None, None, "fft", None),
        P("band", None),
        P("fft", None, None),
        P("fft", None, None, None),
        P(),
        P(),
    )
    return jax.shard_map(
        per_device,
        mesh=mesh,
        in_specs=placed,
        out_specs=(
            P("band", None, None, "fft", None),
            P("fft", None, None),
            P("band", "fft", None, None),
        ),
        check_vma=False,
    )
```

```python
import math

import jax
import ml_dtypes
import numpy as np
import jax.numpy as jnp
from jax import lax
from jax.experimental import pallas as pl
from jax.experimental.pallas import tpu as pltpu
from jax.sharding import PartitionSpec as P

HALO = 6


MESH = pl.DeviceIdType.MESH


def band_sum_kernel(part_ref, out_ref, received, reduced, sems):
    count = part_ref.shape[0]
    me = lax.axis_index("band")
    column = lax.axis_index("fft")
    barrier = pltpu.get_barrier_semaphore()
    for k in range(1, count):
        pl.semaphore_signal(
            barrier, inc=1, device_id=((me + k) % count, column), device_id_type=MESH
        )
    pl.semaphore_wait(barrier, count - 1)
    scatter = []
    for k in range(1, count):
        target = (me + k) % count
        scatter.append(
            pltpu.make_async_remote_copy(
                src_ref=part_ref.at[target],
                dst_ref=received.at[me],
                send_sem=sems.at[0, k],
                recv_sem=sems.at[1, k],
                device_id=(target, column),
                device_id_type=MESH,
            )
        )
    for copy in scatter:
        copy.start()
    for copy in scatter:
        copy.wait()
    total = part_ref[me].astype(jnp.float32)
    for k in range(1, count):
        total = total + received[(me + count - k) % count].astype(jnp.float32)
    reduced[me] = total.astype(reduced.dtype)
    spread_out = []
    for k in range(1, count):
        target = (me + k) % count
        spread_out.append(
            pltpu.make_async_remote_copy(
                src_ref=reduced.at[me],
                dst_ref=reduced.at[me],
                send_sem=sems.at[2, k],
                recv_sem=sems.at[3, k],
                device_id=(target, column),
                device_id_type=MESH,
            )
        )
    for copy in spread_out:
        copy.start()
    for copy in spread_out:
        copy.wait()
    out_ref[...] = reduced[...]


def band_sum(values):
    count = lax.axis_size("band")
    shape = values.shape
    rows = values.size // (count * 128)
    chunks = values.reshape(count, rows, 128)
    summed = pl.pallas_call(
        band_sum_kernel,
        out_shape=jax.ShapeDtypeStruct(chunks.shape, chunks.dtype),
        in_specs=[pl.BlockSpec(memory_space=pltpu.VMEM)],
        out_specs=pl.BlockSpec(memory_space=pltpu.VMEM),
        scratch_shapes=[
            pltpu.VMEM(chunks.shape, chunks.dtype),
            pltpu.VMEM(chunks.shape, chunks.dtype),
            pltpu.SemaphoreType.DMA((4, count)),
        ],
        compiler_params=pltpu.CompilerParams(collective_id=0, has_side_effects=True),
        cost_estimate=pl.CostEstimate(
            flops=values.size, bytes_accessed=6 * values.size, transcendentals=0
        ),
    )(chunks)
    return summed.reshape(shape)


def swap_kernel(to_left_ref, to_right_ref, from_right_ref, from_left_ref, landed, sems):
    count = lax.axis_size("fft")
    me = lax.axis_index("fft")
    band = lax.axis_index("band")
    left = (me + count - 1) % count
    right = (me + 1) % count
    barrier = pltpu.get_barrier_semaphore()
    for neighbour in (left, right):
        pl.semaphore_signal(barrier, inc=1, device_id=(band, neighbour), device_id_type=MESH)
    pl.semaphore_wait(barrier, 2)
    copies = [
        pltpu.make_async_remote_copy(
            src_ref=to_left_ref,
            dst_ref=landed.at[0],
            send_sem=sems.at[0],
            recv_sem=sems.at[1],
            device_id=(band, left),
            device_id_type=MESH,
        ),
        pltpu.make_async_remote_copy(
            src_ref=to_right_ref,
            dst_ref=landed.at[1],
            send_sem=sems.at[2],
            recv_sem=sems.at[3],
            device_id=(band, right),
            device_id_type=MESH,
        ),
    ]
    for copy in copies:
        copy.start()
    for copy in copies:
        copy.wait()
    from_right_ref[...] = landed[0]
    from_left_ref[...] = landed[1]


def neighbour_swap(to_left, to_right, tag):
    shape = jax.ShapeDtypeStruct(to_left.shape, to_left.dtype)
    return pl.pallas_call(
        swap_kernel,
        out_shape=(shape, shape),
        in_specs=[pl.BlockSpec(memory_space=pltpu.VMEM)] * 2,
        out_specs=(pl.BlockSpec(memory_space=pltpu.VMEM),) * 2,
        scratch_shapes=[
            pltpu.VMEM((2,) + to_left.shape, to_left.dtype),
            pltpu.SemaphoreType.DMA((4,)),
        ],
        compiler_params=pltpu.CompilerParams(collective_id=tag, has_side_effects=True),
        cost_estimate=pl.CostEstimate(
            flops=0, bytes_accessed=4 * to_left.size, transcendentals=0
        ),
    )(to_left, to_right)


def halo_kernel(
    to_left_ref, own_ref, to_right_ref, beta_ref, coupled_ref, lower_half_ref,
    proj_ref, placed_ref,
    landed, outgoing, landed_spread, sems,
):
    count = lax.axis_size("fft")
    me = lax.axis_index("fft")
    band = lax.axis_index("band")
    left = (me + count - 1) % count
    right = (me + 1) % count
    barrier = pltpu.get_barrier_semaphore()
    for neighbour in (left, right):
        pl.semaphore_signal(barrier, inc=1, device_id=(band, neighbour), device_id_type=MESH)
    pl.semaphore_wait(barrier, 2)

    def swap(first, second, into, base):
        copies = [
            pltpu.make_async_remote_copy(
                src_ref=first,
                dst_ref=into.at[0],
                send_sem=sems.at[base],
                recv_sem=sems.at[base + 1],
                device_id=(band, left),
                device_id_type=MESH,
            ),
            pltpu.make_async_remote_copy(
                src_ref=second,
                dst_ref=into.at[1],
                send_sem=sems.at[base + 2],
                recv_sem=sems.at[base + 3],
                device_id=(band, right),
                device_id_type=MESH,
            ),
        ]
        for copy in copies:
            copy.start()
        for copy in copies:
            copy.wait()

    swap(to_left_ref, to_right_ref, landed, 0)
    atoms, nproj = beta_ref.shape[0], beta_ref.shape[1]
    lane = lax.broadcasted_iota(jnp.int32, (1, 128), 1)
    for c in range(2):
        for a in range(atoms):
            block = (
                own_ref[c, a].astype(jnp.float32)
                + landed[0, c, a].astype(jnp.float32)
                + landed[1, c, a].astype(jnp.float32)
            )
            sums = []
            row = jnp.zeros((1, 128), jnp.float32)
            for j in range(nproj):
                value = jnp.sum(beta_ref[a, j].astype(jnp.float32) * block, keepdims=True)
                sums.append(value)
                row = row + jnp.where(lane == j, value, 0.0)
            proj_ref[pl.ds(a * 2 + c, 1), :] = row
            spread = jnp.zeros(block.shape, jnp.float32)
            for i in range(nproj):
                energy = sums[0] * coupled_ref[i, 0]
                for j in range(1, nproj):
                    energy = energy + sums[j] * coupled_ref[i, j]
                spread = spread + beta_ref[a, i].astype(jnp.float32) * energy
            place(placed_ref, lower_half_ref, c, 1, a, spread)
            outgoing[c, a] = spread.astype(outgoing.dtype)
    swap(outgoing, outgoing, landed_spread, 4)
    for c in range(2):
        for a in range(atoms):
            place(placed_ref, lower_half_ref, c, 0, a, landed_spread[1, c, a].astype(jnp.float32))
            place(placed_ref, lower_half_ref, c, 2, a, landed_spread[0, c, a].astype(jnp.float32))


def place(placed_ref, lower_half_ref, c, side, a, value):
    width = value.shape[-1]
    keep = lower_half_ref[side, a]
    upper = value.astype(jnp.bfloat16)
    lower = (value - upper.astype(jnp.float32)).astype(jnp.bfloat16)
    for part, piece in ((0, upper), (1, lower)):
        piece = piece.astype(jnp.float32)
        placed_ref[2 * part + c, side, a, :, pl.ds(0, width)] = (piece * keep).astype(jnp.bfloat16)
        placed_ref[2 * part + c, side, a, :, pl.ds(width, width)] = (
            piece * (1.0 - keep)
        ).astype(jnp.bfloat16)


def halo_exchange(to_left, own, to_right, projectors, coupled, lower_half):
    atoms = projectors.shape[0]
    vmem = pl.BlockSpec(memory_space=pltpu.VMEM)
    return pl.pallas_call(
        halo_kernel,
        out_shape=(
            jax.ShapeDtypeStruct((2 * atoms, 128), jnp.float32),
            jax.ShapeDtypeStruct((4, 3) + own.shape[1:-1] + (2 * own.shape[-1],), jnp.bfloat16),
        ),
        in_specs=[vmem, vmem, vmem, vmem, pl.BlockSpec(memory_space=pltpu.SMEM), vmem],
        out_specs=(vmem, vmem),
        scratch_shapes=[
            pltpu.VMEM((2,) + own.shape, jnp.bfloat16),
            pltpu.VMEM(own.shape, jnp.bfloat16),
            pltpu.VMEM((2,) + own.shape, jnp.bfloat16),
            pltpu.SemaphoreType.DMA((8,)),
        ],
        compiler_params=pltpu.CompilerParams(collective_id=2, has_side_effects=True),
        cost_estimate=pl.CostEstimate(
            flops=8 * projectors.size, bytes_accessed=16 * own.size, transcendentals=0
        ),
    )(to_left, own, to_right, projectors, coupled, lower_half)


def extended_2(shard, sides, width):
    for axis, dim in sides:
        count, length = (lax.axis_size(axis), shard.shape[dim])
        up = [(i, (i + 1) % count) for i in range(count)]
        down = [(j, i) for i, j in up]
        last = lax.slice_in_dim(shard, length - width, length, axis=dim)
        first = lax.slice_in_dim(shard, 0, width, axis=dim)
        before = lax.ppermute(last, axis, up)
        after = lax.ppermute(first, axis, down)
        shard = jnp.concatenate([before, shard, after], axis=dim)
    return shard


def passed_along(block, axis, distance):
    devices = range(lax.axis_size(axis))
    route = [((i - distance) % len(devices), i) for i in devices]
    return lax.ppermute(block, axis, route)


def dft_table(length, sign_value):
    indices = jnp.arange(length, dtype=jnp.int32)
    phases = indices[:, None] * indices[None, :] % length
    angles = 2.0 * math.pi / length * phases.astype(jnp.float32)
    factor = 1.0 / math.sqrt(length)
    cosine = jnp.cos(angles) * factor
    sine_part = jnp.sin(angles) * (sign_value * factor)
    upper_rows = jnp.stack([cosine, -sine_part])
    bottom = jnp.stack([sine_part, cosine])
    return jnp.stack([upper_rows, bottom]).astype(jnp.bfloat16)


def dft_table_constant(length, sign_value):
    indices = np.arange(length, dtype=np.int64)
    phases = indices[:, None] * indices[None, :] % length
    angles = np.float32(2.0 * math.pi / length) * phases.astype(np.float32)
    factor = np.float32(1.0 / math.sqrt(length))
    cosine = np.cos(angles).astype(np.float32) * factor
    sine_part = np.sin(angles).astype(np.float32) * np.float32(sign_value) * factor
    table = np.stack([np.stack([cosine, -sine_part]), np.stack([sine_part, cosine])])
    return table.astype(ml_dtypes.bfloat16)


def wave_squares(indices, length):
    frequency = (
        jnp.where(2 * indices < length, indices, indices - length).astype(jnp.float32) / length
    )
    return frequency * frequency


def per_device(wave_coeffs, occupation, potential, projectors, coupling, sphere_blocks):
    pieces = lax.axis_size("fft")
    slab_index = lax.axis_index("fft")
    coeffs = wave_coeffs[0]
    size_x = coeffs.shape[1]
    columns = coeffs.shape[2]
    size_z = coeffs.shape[3]
    slab_planes = potential.shape[0]
    size_y = potential.shape[1]
    atom_dev = projectors.shape[0]
    nproj_count = projectors.shape[1]
    block_cells = projectors.shape[3]
    zblocks = size_z // block_cells
    plane_blocks = size_y * zblocks
    table_x = (
        dft_table_constant(size_x, 1.0)
        .reshape(2, 2, pieces, slab_planes, size_x)
        .transpose(2, 0, 3, 1, 4)
        .reshape(2 * size_x, 2 * size_x)
    )
    inverse_y = dft_table(size_y, 1.0)
    inverse_z = dft_table(size_z, 1.0)
    table_x = jnp.asarray(table_x).reshape(2 * size_x, 2, size_x)
    along_x = jnp.einsum(
        "ypcx,cxyz->ypz",
        jnp.broadcast_to(table_x[None], (columns,) + table_x.shape),
        coeffs,
        preferred_element_type=jnp.float32,
    ).astype(jnp.bfloat16)
    along_x = along_x.reshape(columns, pieces, 2, slab_planes, size_z).transpose(1, 2, 3, 0, 4)
    arrived = lax.all_to_all(along_x, "fft", split_axis=0, concat_axis=0, tiled=True)
    along_y = jnp.einsum(
        "abysu,sbxuz->axyz",
        inverse_y.reshape(2, 2, size_y, pieces, columns),
        arrived,
        preferred_element_type=jnp.float32,
    ).astype(jnp.bfloat16)
    wave_field = jnp.einsum(
        "abzk,bxyk->axyz", inverse_z, along_y, preferred_element_type=jnp.float32
    ).astype(jnp.bfloat16)
    weights = occupation[0]
    real_part = wave_field[0].astype(jnp.float32)
    imag_part = wave_field[1].astype(jnp.float32)
    partial_density = weights[0] * real_part * real_part + weights[1] * imag_part * imag_part
    density = band_sum(partial_density.astype(jnp.bfloat16))
    strength = 3.0 * math.sqrt(block_cells * projectors.shape[2]) / nproj_count
    coupled = (coupling + coupling.T) * (0.5 * strength)
    slab_blocks = slab_planes * plane_blocks
    slab_rows = slab_planes * size_y
    around = [(slab_index + shift) % pieces for shift in (-1, 0, 1)]
    atom_rows = jnp.stack(
        [lax.dynamic_slice_in_dim(sphere_blocks, d * atom_dev, atom_dev, 0) for d in around]
    ).reshape(-1)
    local_index = atom_rows - slab_index * slab_blocks
    is_mine = (atom_rows // slab_blocks) == slab_index
    row_of = local_index // zblocks
    half_of = (local_index % zblocks)[None, :, None]
    selector = (
        (row_of[:, None] == jnp.arange(slab_rows, dtype=jnp.int32)[None, :]) & is_mine[:, None]
    ).astype(jnp.bfloat16)
    selector = lax.optimization_barrier(selector)
    field_rows = wave_field.reshape(2, slab_rows, size_z)
    picked_rows = jnp.einsum(
        "er,crz->cez", selector, field_rows, preferred_element_type=jnp.float32
    ).reshape(2, -1, zblocks, block_cells)
    picked = jnp.zeros_like(picked_rows[:, :, 0])
    for q in range(zblocks):
        picked = jnp.where(half_of == q, picked_rows[:, :, q], picked)
    picked = picked.astype(jnp.bfloat16).reshape(2, 3, atom_dev, -1, block_cells)
    lower_half = (half_of == 0).astype(jnp.float32).reshape(3, atom_dev, -1, 1)
    proj_rows, placed = halo_exchange(
        picked[:, 0], picked[:, 1], picked[:, 2], projectors, coupled, lower_half
    )
    projections_own = proj_rows[:, :nproj_count].reshape(atom_dev, 2, nproj_count)
    nonlocal_parts = jnp.einsum(
        "er,cez->crz",
        selector,
        placed.reshape(4, -1, size_z),
        preferred_element_type=jnp.float32,
    )
    nonlocal_term = (nonlocal_parts[:2] + nonlocal_parts[2:]).reshape(
        2, slab_planes, size_y, size_z
    )
    total_field = (
        potential.astype(jnp.float32)[None] * wave_field.astype(jnp.float32) + nonlocal_term
    ).astype(jnp.bfloat16)
    forward_z = dft_table(size_z, -1.0)
    forward_y = dft_table(size_y, -1.0)
    forward_x = dft_table(size_x, -1.0)
    back_z = jnp.einsum(
        "abzk,bxyk->axyz", forward_z, total_field, preferred_element_type=jnp.float32
    ).astype(jnp.bfloat16)
    back_y = jnp.einsum(
        "abyk,bxkz->axyz", forward_y, back_z, preferred_element_type=jnp.float32
    ).astype(jnp.bfloat16)
    transformed = jnp.einsum(
        "abxk,bkyz->axyz",
        forward_x,
        lax.all_to_all(back_y, "fft", split_axis=2, concat_axis=1, tiled=True),
        preferred_element_type=jnp.float32,
    )
    index_x = jnp.arange(size_x, dtype=jnp.int32)
    index_y = slab_index * columns + jnp.arange(columns, dtype=jnp.int32)
    index_z = jnp.arange(size_z, dtype=jnp.int32)
    kinetic = (
        wave_squares(index_x, size_x)[:, None, None]
        + wave_squares(index_y, size_y)[None, :, None]
        + wave_squares(index_z, size_z)[None, None, :]
    )
    applied = (transformed + kinetic[None] * coeffs.astype(jnp.float32)).astype(jnp.bfloat16)
    return (applied[None], density, projections_own[None])


def solution(mesh):
    placed = (
        P("band", None, None, "fft", None),
        P("band", None),
        P("fft", None, None),
        P("fft", None, None, None),
        P(),
        P(),
    )
    return jax.shard_map(
        per_device,
        mesh=mesh,
        in_specs=placed,
        out_specs=(
            P("band", None, None, "fft", None),
            P("fft", None, None),
            P("band", "fft", None, None),
        ),
        check_vma=False,
    )
```

```python
import math

import jax
import ml_dtypes
import numpy as np
import jax.numpy as jnp
from jax import lax
from jax.experimental import pallas as pl
from jax.experimental.pallas import tpu as pltpu
from jax.sharding import PartitionSpec as P

HALO = 6


MESH = pl.DeviceIdType.MESH


def band_sum_kernel(part_ref, out_ref, received, reduced, sems):
    count = part_ref.shape[0]
    me = lax.axis_index("band")
    column = lax.axis_index("fft")
    barrier = pltpu.get_barrier_semaphore()
    for k in range(1, count):
        pl.semaphore_signal(
            barrier, inc=1, device_id=((me + k) % count, column), device_id_type=MESH
        )
    pl.semaphore_wait(barrier, count - 1)
    scatter = []
    for k in range(1, count):
        target = (me + k) % count
        scatter.append(
            pltpu.make_async_remote_copy(
                src_ref=part_ref.at[target],
                dst_ref=received.at[me],
                send_sem=sems.at[0, k],
                recv_sem=sems.at[1, k],
                device_id=(target, column),
                device_id_type=MESH,
            )
        )
    for copy in scatter:
        copy.start()
    for copy in scatter:
        copy.wait()
    total = part_ref[me].astype(jnp.float32)
    for k in range(1, count):
        total = total + received[(me + count - k) % count].astype(jnp.float32)
    reduced[me] = total.astype(reduced.dtype)
    spread_out = []
    for k in range(1, count):
        target = (me + k) % count
        spread_out.append(
            pltpu.make_async_remote_copy(
                src_ref=reduced.at[me],
                dst_ref=reduced.at[me],
                send_sem=sems.at[2, k],
                recv_sem=sems.at[3, k],
                device_id=(target, column),
                device_id_type=MESH,
            )
        )
    for copy in spread_out:
        copy.start()
    for copy in spread_out:
        copy.wait()
    out_ref[...] = reduced[...]


def band_sum(values):
    count = lax.axis_size("band")
    shape = values.shape
    rows = values.size // (count * 128)
    chunks = values.reshape(count, rows, 128)
    summed = pl.pallas_call(
        band_sum_kernel,
        out_shape=jax.ShapeDtypeStruct(chunks.shape, chunks.dtype),
        in_specs=[pl.BlockSpec(memory_space=pltpu.VMEM)],
        out_specs=pl.BlockSpec(memory_space=pltpu.VMEM),
        scratch_shapes=[
            pltpu.VMEM(chunks.shape, chunks.dtype),
            pltpu.VMEM(chunks.shape, chunks.dtype),
            pltpu.SemaphoreType.DMA((4, count)),
        ],
        compiler_params=pltpu.CompilerParams(collective_id=0, has_side_effects=True),
        cost_estimate=pl.CostEstimate(
            flops=values.size, bytes_accessed=6 * values.size, transcendentals=0
        ),
    )(chunks)
    return summed.reshape(shape)


def swap_kernel(to_left_ref, to_right_ref, from_right_ref, from_left_ref, landed, sems):
    count = lax.axis_size("fft")
    me = lax.axis_index("fft")
    band = lax.axis_index("band")
    left = (me + count - 1) % count
    right = (me + 1) % count
    barrier = pltpu.get_barrier_semaphore()
    for neighbour in (left, right):
        pl.semaphore_signal(barrier, inc=1, device_id=(band, neighbour), device_id_type=MESH)
    pl.semaphore_wait(barrier, 2)
    copies = [
        pltpu.make_async_remote_copy(
            src_ref=to_left_ref,
            dst_ref=landed.at[0],
            send_sem=sems.at[0],
            recv_sem=sems.at[1],
            device_id=(band, left),
            device_id_type=MESH,
        ),
        pltpu.make_async_remote_copy(
            src_ref=to_right_ref,
            dst_ref=landed.at[1],
            send_sem=sems.at[2],
            recv_sem=sems.at[3],
            device_id=(band, right),
            device_id_type=MESH,
        ),
    ]
    for copy in copies:
        copy.start()
    for copy in copies:
        copy.wait()
    from_right_ref[...] = landed[0]
    from_left_ref[...] = landed[1]


def neighbour_swap(to_left, to_right, tag):
    shape = jax.ShapeDtypeStruct(to_left.shape, to_left.dtype)
    return pl.pallas_call(
        swap_kernel,
        out_shape=(shape, shape),
        in_specs=[pl.BlockSpec(memory_space=pltpu.VMEM)] * 2,
        out_specs=(pl.BlockSpec(memory_space=pltpu.VMEM),) * 2,
        scratch_shapes=[
            pltpu.VMEM((2,) + to_left.shape, to_left.dtype),
            pltpu.SemaphoreType.DMA((4,)),
        ],
        compiler_params=pltpu.CompilerParams(collective_id=tag, has_side_effects=True),
        cost_estimate=pl.CostEstimate(
            flops=0, bytes_accessed=4 * to_left.size, transcendentals=0
        ),
    )(to_left, to_right)


def halo_kernel(
    to_left_ref, own_ref, to_right_ref, beta_ref, coupled_ref, lower_half_ref,
    proj_ref, placed_ref,
    landed, outgoing, landed_spread, sems,
):
    count = lax.axis_size("fft")
    me = lax.axis_index("fft")
    band = lax.axis_index("band")
    left = (me + count - 1) % count
    right = (me + 1) % count
    barrier = pltpu.get_barrier_semaphore()
    for neighbour in (left, right):
        pl.semaphore_signal(barrier, inc=1, device_id=(band, neighbour), device_id_type=MESH)
    pl.semaphore_wait(barrier, 2)

    def swap(first, second, into, base):
        copies = [
            pltpu.make_async_remote_copy(
                src_ref=first,
                dst_ref=into.at[0],
                send_sem=sems.at[base],
                recv_sem=sems.at[base + 1],
                device_id=(band, left),
                device_id_type=MESH,
            ),
            pltpu.make_async_remote_copy(
                src_ref=second,
                dst_ref=into.at[1],
                send_sem=sems.at[base + 2],
                recv_sem=sems.at[base + 3],
                device_id=(band, right),
                device_id_type=MESH,
            ),
        ]
        for copy in copies:
            copy.start()
        for copy in copies:
            copy.wait_recv()
        return copies

    first = swap(to_left_ref, to_right_ref, landed, 0)
    atoms, nproj = beta_ref.shape[0], beta_ref.shape[1]
    lane = lax.broadcasted_iota(jnp.int32, (1, 128), 1)
    for c in range(2):
        for a in range(atoms):
            block = (
                own_ref[c, a].astype(jnp.float32)
                + landed[0, c, a].astype(jnp.float32)
                + landed[1, c, a].astype(jnp.float32)
            )
            sums = []
            row = jnp.zeros((1, 128), jnp.float32)
            for j in range(nproj):
                value = jnp.sum(beta_ref[a, j].astype(jnp.float32) * block, keepdims=True)
                sums.append(value)
                row = row + jnp.where(lane == j, value, 0.0)
            proj_ref[pl.ds(a * 2 + c, 1), :] = row
            spread = jnp.zeros(block.shape, jnp.float32)
            for i in range(nproj):
                energy = sums[0] * coupled_ref[i, 0]
                for j in range(1, nproj):
                    energy = energy + sums[j] * coupled_ref[i, j]
                spread = spread + beta_ref[a, i].astype(jnp.float32) * energy
            place(placed_ref, lower_half_ref, c, 1, a, spread)
            outgoing[c, a] = spread.astype(outgoing.dtype)
    second = swap(outgoing, outgoing, landed_spread, 4)
    for c in range(2):
        for a in range(atoms):
            place(placed_ref, lower_half_ref, c, 0, a, landed_spread[1, c, a].astype(jnp.float32))
            place(placed_ref, lower_half_ref, c, 2, a, landed_spread[0, c, a].astype(jnp.float32))
    for copy in first + second:
        copy.wait_send()


def place(placed_ref, lower_half_ref, c, side, a, value):
    width = value.shape[-1]
    keep = lower_half_ref[side, a]
    upper = value.astype(jnp.bfloat16)
    lower = (value - upper.astype(jnp.float32)).astype(jnp.bfloat16)
    for part, piece in ((0, upper), (1, lower)):
        piece = piece.astype(jnp.float32)
        placed_ref[2 * part + c, side, a, :, pl.ds(0, width)] = (piece * keep).astype(jnp.bfloat16)
        placed_ref[2 * part + c, side, a, :, pl.ds(width, width)] = (
            piece * (1.0 - keep)
        ).astype(jnp.bfloat16)


def halo_exchange(to_left, own, to_right, projectors, coupled, lower_half):
    atoms = projectors.shape[0]
    vmem = pl.BlockSpec(memory_space=pltpu.VMEM)
    return pl.pallas_call(
        halo_kernel,
        out_shape=(
            jax.ShapeDtypeStruct((2 * atoms, 128), jnp.float32),
            jax.ShapeDtypeStruct((4, 3) + own.shape[1:-1] + (2 * own.shape[-1],), jnp.bfloat16),
        ),
        in_specs=[vmem, vmem, vmem, vmem, pl.BlockSpec(memory_space=pltpu.SMEM), vmem],
        out_specs=(vmem, vmem),
        scratch_shapes=[
            pltpu.VMEM((2,) + own.shape, jnp.bfloat16),
            pltpu.VMEM(own.shape, jnp.bfloat16),
            pltpu.VMEM((2,) + own.shape, jnp.bfloat16),
            pltpu.SemaphoreType.DMA((8,)),
        ],
        compiler_params=pltpu.CompilerParams(collective_id=2, has_side_effects=True),
        cost_estimate=pl.CostEstimate(
            flops=8 * projectors.size, bytes_accessed=16 * own.size, transcendentals=0
        ),
    )(to_left, own, to_right, projectors, coupled, lower_half)


def extended_2(shard, sides, width):
    for axis, dim in sides:
        count, length = (lax.axis_size(axis), shard.shape[dim])
        up = [(i, (i + 1) % count) for i in range(count)]
        down = [(j, i) for i, j in up]
        last = lax.slice_in_dim(shard, length - width, length, axis=dim)
        first = lax.slice_in_dim(shard, 0, width, axis=dim)
        before = lax.ppermute(last, axis, up)
        after = lax.ppermute(first, axis, down)
        shard = jnp.concatenate([before, shard, after], axis=dim)
    return shard


def passed_along(block, axis, distance):
    devices = range(lax.axis_size(axis))
    route = [((i - distance) % len(devices), i) for i in devices]
    return lax.ppermute(block, axis, route)


def dft_table(length, sign_value):
    indices = jnp.arange(length, dtype=jnp.int32)
    phases = indices[:, None] * indices[None, :] % length
    angles = 2.0 * math.pi / length * phases.astype(jnp.float32)
    factor = 1.0 / math.sqrt(length)
    cosine = jnp.cos(angles) * factor
    sine_part = jnp.sin(angles) * (sign_value * factor)
    upper_rows = jnp.stack([cosine, -sine_part])
    bottom = jnp.stack([sine_part, cosine])
    return jnp.stack([upper_rows, bottom]).astype(jnp.bfloat16)


def dft_table_constant(length, sign_value):
    indices = np.arange(length, dtype=np.int64)
    phases = indices[:, None] * indices[None, :] % length
    angles = np.float32(2.0 * math.pi / length) * phases.astype(np.float32)
    factor = np.float32(1.0 / math.sqrt(length))
    cosine = np.cos(angles).astype(np.float32) * factor
    sine_part = np.sin(angles).astype(np.float32) * np.float32(sign_value) * factor
    table = np.stack([np.stack([cosine, -sine_part]), np.stack([sine_part, cosine])])
    return table.astype(ml_dtypes.bfloat16)


def wave_squares(indices, length):
    frequency = (
        jnp.where(2 * indices < length, indices, indices - length).astype(jnp.float32) / length
    )
    return frequency * frequency


def per_device(wave_coeffs, occupation, potential, projectors, coupling, sphere_blocks):
    pieces = lax.axis_size("fft")
    slab_index = lax.axis_index("fft")
    coeffs = wave_coeffs[0]
    size_x = coeffs.shape[1]
    columns = coeffs.shape[2]
    size_z = coeffs.shape[3]
    slab_planes = potential.shape[0]
    size_y = potential.shape[1]
    atom_dev = projectors.shape[0]
    nproj_count = projectors.shape[1]
    block_cells = projectors.shape[3]
    zblocks = size_z // block_cells
    plane_blocks = size_y * zblocks
    table_x = (
        dft_table_constant(size_x, 1.0)
        .reshape(2, 2, pieces, slab_planes, size_x)
        .transpose(2, 0, 3, 1, 4)
        .reshape(2 * size_x, 2 * size_x)
    )
    inverse_y = dft_table(size_y, 1.0)
    inverse_z = dft_table(size_z, 1.0)
    table_x = jnp.asarray(table_x).reshape(2 * size_x, 2, size_x)
    along_x = jnp.einsum(
        "ypcx,cxyz->ypz",
        jnp.broadcast_to(table_x[None], (columns,) + table_x.shape),
        coeffs,
        preferred_element_type=jnp.float32,
    ).astype(jnp.bfloat16)
    along_x = along_x.reshape(columns, pieces, 2, slab_planes, size_z).transpose(1, 2, 3, 0, 4)
    arrived = lax.all_to_all(along_x, "fft", split_axis=0, concat_axis=0, tiled=True)
    along_y = jnp.einsum(
        "abysu,sbxuz->axyz",
        inverse_y.reshape(2, 2, size_y, pieces, columns),
        arrived,
        preferred_element_type=jnp.float32,
    ).astype(jnp.bfloat16)
    wave_field = jnp.einsum(
        "abzk,bxyk->axyz", inverse_z, along_y, preferred_element_type=jnp.float32
    ).astype(jnp.bfloat16)
    weights = occupation[0]
    real_part = wave_field[0].astype(jnp.float32)
    imag_part = wave_field[1].astype(jnp.float32)
    partial_density = weights[0] * real_part * real_part + weights[1] * imag_part * imag_part
    density = band_sum(partial_density.astype(jnp.bfloat16))
    strength = 3.0 * math.sqrt(block_cells * projectors.shape[2]) / nproj_count
    coupled = (coupling + coupling.T) * (0.5 * strength)
    slab_blocks = slab_planes * plane_blocks
    slab_rows = slab_planes * size_y
    around = [(slab_index + shift) % pieces for shift in (-1, 0, 1)]
    atom_rows = jnp.stack(
        [lax.dynamic_slice_in_dim(sphere_blocks, d * atom_dev, atom_dev, 0) for d in around]
    ).reshape(-1)
    local_index = atom_rows - slab_index * slab_blocks
    is_mine = (atom_rows // slab_blocks) == slab_index
    row_of = local_index // zblocks
    half_of = (local_index % zblocks)[None, :, None]
    selector = (
        (row_of[:, None] == jnp.arange(slab_rows, dtype=jnp.int32)[None, :]) & is_mine[:, None]
    ).astype(jnp.bfloat16)
    field_rows = wave_field.reshape(2, slab_rows, size_z)
    picked_rows = jnp.einsum(
        "er,crz->cez", selector, field_rows, preferred_element_type=jnp.float32
    ).reshape(2, -1, zblocks, block_cells)
    picked = jnp.zeros_like(picked_rows[:, :, 0])
    for q in range(zblocks):
        picked = jnp.where(half_of == q, picked_rows[:, :, q], picked)
    picked = picked.astype(jnp.bfloat16).reshape(2, 3, atom_dev, -1, block_cells)
    lower_half = (half_of == 0).astype(jnp.float32).reshape(3, atom_dev, -1, 1)
    proj_rows, placed = halo_exchange(
        picked[:, 0], picked[:, 1], picked[:, 2], projectors, coupled, lower_half
    )
    projections_own = proj_rows[:, :nproj_count].reshape(atom_dev, 2, nproj_count)
    nonlocal_parts = jnp.einsum(
        "er,cez->crz",
        selector,
        placed.reshape(4, -1, size_z),
        preferred_element_type=jnp.float32,
    )
    nonlocal_term = (nonlocal_parts[:2] + nonlocal_parts[2:]).reshape(
        2, slab_planes, size_y, size_z
    )
    total_field = (
        potential.astype(jnp.float32)[None] * wave_field.astype(jnp.float32) + nonlocal_term
    ).astype(jnp.bfloat16)
    forward_z = dft_table(size_z, -1.0)
    forward_y = dft_table(size_y, -1.0)
    forward_x = dft_table(size_x, -1.0)
    back_z = jnp.einsum(
        "abzk,bxyk->axyz", forward_z, total_field, preferred_element_type=jnp.float32
    ).astype(jnp.bfloat16)
    back_y = jnp.einsum(
        "abyk,bxkz->axyz", forward_y, back_z, preferred_element_type=jnp.float32
    ).astype(jnp.bfloat16)
    transformed = jnp.einsum(
        "abxk,bkyz->axyz",
        forward_x,
        lax.all_to_all(back_y, "fft", split_axis=2, concat_axis=1, tiled=True),
        preferred_element_type=jnp.float32,
    )
    index_x = jnp.arange(size_x, dtype=jnp.int32)
    index_y = slab_index * columns + jnp.arange(columns, dtype=jnp.int32)
    index_z = jnp.arange(size_z, dtype=jnp.int32)
    kinetic = (
        wave_squares(index_x, size_x)[:, None, None]
        + wave_squares(index_y, size_y)[None, :, None]
        + wave_squares(index_z, size_z)[None, None, :]
    )
    applied = (transformed + kinetic[None] * coeffs.astype(jnp.float32)).astype(jnp.bfloat16)
    return (applied[None], density, projections_own[None])


def solution(mesh):
    placed = (
        P("band", None, None, "fft", None),
        P("band", None),
        P("fft", None, None),
        P("fft", None, None, None),
        P(),
        P(),
    )
    return jax.shard_map(
        per_device,
        mesh=mesh,
        in_specs=placed,
        out_specs=(
            P("band", None, None, "fft", None),
            P("fft", None, None),
            P("band", "fft", None, None),
        ),
        check_vma=False,
    )
```
